32 devices in a mesh: batch: 4 (over y, core), blk: 8 (over z, x).
Axes of the slice: x: 2, y: 2, z: 4, core: 2. Of those that a mesh axis runs over, the one named last changes fastest.
Arguments:
- inputs: bfloat16 [2, 4, 1024, 1024], P(None, 'batch', 'blk'), may hold values from -6 to 6
- segment_ids: int32 [2, 4, 1024], P(None, 'batch', 'blk'), may hold values from 0 to 3, never falling along the last dimension, each value on 1 to 640 neighbouring positions
- cotangent: bfloat16 [2, 4, 1024, 1024], P(None, 'batch', 'blk'), may hold values from -6 to 6
- qkv_weight: bfloat16 [1024, 3072], P(('batch', 'blk')), may hold values from -0.1875 to 0.1875
- out_weight: bfloat16 [1024, 1024], P(('batch', 'blk')), may hold values from -0.75 to 0.75
- up_weight: bfloat16 [1024, 4096], P(('batch', 'blk')), may hold values from -0.1875 to 0.1875
- down_weight: bfloat16 [4096, 1024], P(('batch', 'blk')), may hold values from -0.09375 to 0.09375
- first_gain: bfloat16 [1024], P(('batch', 'blk')), may hold values from 0.5 to 1.5
- first_bias: bfloat16 [1024], P(('batch', 'blk')), may hold values from -4 to 4
- second_gain: bfloat16 [1024], P(('batch', 'blk')), may hold values from 0.5 to 1.5
- second_bias: bfloat16 [1024], P(('batch', 'blk')), may hold values from -4 to 4
- out_bias: bfloat16 [1024], P(('batch', 'blk')), may hold values from -4 to 4
- up_bias: bfloat16 [4096], P(('batch', 'blk')), may hold values from -4 to 4
- down_bias: bfloat16 [1024], P(('batch', 'blk')), may hold values from -4 to 4
Outputs:
- result: float32 [2, 4, 1024, 1024], P(None, 'batch', 'blk')
- input_grad: float32 [2, 4, 1024, 1024], P(None, 'batch', 'blk')
- qkv_grad: float32 [1024, 3072], P(('batch', 'blk'))
- out_grad: float32 [1024, 1024], P(('batch', 'blk'))
- up_grad: float32 [1024, 4096], P(('batch', 'blk'))
- down_grad: float32 [4096, 1024], P(('batch', 'blk'))
- first_gain_grad: float32 [1024], P(('batch', 'blk'))
- first_bias_grad: float32 [1024], P(('batch', 'blk'))
- second_gain_grad: float32 [1024], P(('batch', 'blk'))
- second_bias_grad: float32 [1024], P(('batch', 'blk'))
- out_bias_grad: float32 [1024], P(('batch', 'blk'))
- up_bias_grad: float32 [4096], P(('batch', 'blk'))
- down_bias_grad: float32 [1024], P(('batch', 'blk'))
The draws below stay inside these ranges and needn't reach their ends.
Inputs may be any that keep to these rules, and one draw needn't show every extreme that they name: `segment_ids`: along each set the ids never fall; each image holds 1 to 640 latents, and one image of every set holds exactly 640.
All inputs are finite; a program needn't handle non-finite values.
Results may differ from the reference program's by a relative error of at most 0.025.
Values may be sent and summed in bfloat16 or wider, within the bound.
No kernel may reach another device: no remote copies, remote signals or barrier semaphores. Data moves between devices by JAX's collectives and lax.ppermute only.
A program may use at most 320 MiB of HBM per device.

```python
import math
import jax
import jax.numpy as jnp
import numpy as np
from jax import lax

D = 1024
H = 8
HD = 128
FF = 4096
MICRO = 2
IMAGES = 4
SETS = 4
SEQ = 1024
IMG_MOST = 640


def steps_of(key, dims, cuts, low, high):
    factor_of, own = 1.0, jax.random.fold_in(key, 6)
    for dim, parts in cuts:
        steps = jnp.exp(jax.random.uniform(jax.random.fold_in(own, dim), (parts,), jnp.float32, low / len(cuts), high / len(cuts)))
        factor_of = factor_of * jnp.repeat(steps, dims[dim] // parts).reshape([-1 if axis == dim else 1 for axis in range(len(dims))])
    return factor_of


def profile(count, total, bound, lean):
    weights = [(1 << 20) // math.isqrt(grade ** lean) + 1 for grade in range(2, count + 1)]
    surplus, counts = total - bound - (count - 1), [1] * (count - 1)
    while surplus > 0:
        movable = [i for i in range(count - 1) if counts[i] < bound]
        whole, remaining = sum([weights[i] for i in movable]), surplus
        for i in movable:
            extra = min(bound - counts[i], max(1, remaining * weights[i] // whole), surplus)
            counts[i] = counts[i] + extra
            surplus = surplus - extra
    return np.array([bound] + counts)


def uneven(rng, amount, total, limit, skew):
    if amount == 2:
        one = jax.random.randint(rng, (), max(1, total - limit), min(limit, total - 1) + 1)
        return jnp.stack([one, total - one])
    sizes = jnp.asarray(profile(amount, total, limit, skew), jnp.int32)
    couples = (amount - 1) // 2
    giver, receiver = sizes[1:1 + 2 * couples:2], sizes[2:2 + 2 * couples:2]
    slack = jnp.minimum(giver - 1, limit - receiver)
    passed = jax.random.randint(jax.random.fold_in(rng, 1), (couples,), 0, 1 << 20) % (slack + 1)
    sizes = sizes.at[1:1 + 2 * couples:2].set(giver - passed).at[2:2 + 2 * couples:2].set(receiver + passed)
    return sizes[jax.random.permutation(jax.random.fold_in(rng, 2), amount)]


def noise(stream_key, dims, deviation, reach, split=(), kind=jnp.bfloat16):
    array = deviation * jax.random.normal(stream_key, dims, jnp.float32)
    if split:
        array = array * steps_of(stream_key, dims, split, -0.22, 0.18)
    return jnp.clip(array, -reach, reach).astype(kind)


def setup_inputs(seed: int = 0) -> dict:
    key_of = jax.random.split(jax.random.key(seed), 15)
    inputs = noise(key_of[0], (MICRO, SETS, SEQ, D), 1.0, 6.0, ((1, 4), (2, 8)))
    segment_ids = jax.vmap(lambda own: jnp.searchsorted(jnp.cumsum(uneven(own, IMAGES, SEQ, IMG_MOST, 0)), jnp.arange(SEQ), side="right"))(jax.random.split(key_of[1], MICRO * SETS)).reshape((MICRO, SETS, SEQ)).astype(jnp.int32)
    cotangent = noise(key_of[2], (MICRO, SETS, SEQ, D), 1.0, 6.0, ((1, 4), (2, 8)))
    qkv_weight = noise(key_of[3], (D, 3 * D), D ** -0.5, 0.1875, ((0, 32),))
    out_weight = noise(key_of[4], (D, D), (D // 16) ** -0.5, 0.75, ((0, 32),))
    up_weight = noise(key_of[5], (D, FF), D ** -0.5, 0.1875, ((0, 32),))
    down_weight = noise(key_of[6], (FF, D), FF ** -0.5, 0.09375, ((0, 32),))
    first_gain = jnp.clip(1.0 + 0.1 * jax.random.normal(key_of[7], (D,), jnp.float32), 0.5, 1.5).astype(jnp.bfloat16)
    first_bias = noise(key_of[8], (D,), 0.3, 4.0, ((0, 32),))
    second_gain = jnp.clip(1.0 + 0.1 * jax.random.normal(key_of[9], (D,), jnp.float32), 0.5, 1.5).astype(jnp.bfloat16)
    second_bias = noise(key_of[10], (D,), 0.3, 4.0, ((0, 32),))
    out_bias = noise(key_of[11], (D,), 0.3, 4.0, ((0, 32),))
    up_bias = noise(key_of[12], (FF,), 0.3, 4.0, ((0, 32),))
    down_bias = noise(key_of[13], (D,), 0.3, 4.0, ((0, 32),))
    return {"inputs": inputs, "segment_ids": segment_ids, "cotangent": cotangent, "qkv_weight": qkv_weight, "out_weight": out_weight, "up_weight": up_weight, "down_weight": down_weight, "first_gain": first_gain, "first_bias": first_bias, "second_gain": second_gain, "second_bias": second_bias, "out_bias": out_bias, "up_bias": up_bias, "down_bias": down_bias}


@jax.custom_vjp
def low(v):
    return lax.optimization_barrier(v.astype(jnp.bfloat16)).astype(jnp.float32)

@jax.custom_vjp
def low_back(v):
    return v

def low_keep(v):
    return (low(v), None)

def low_pass(kept, grad):
    return (grad,)

def back_keep(v):
    return (v, None)

def back_low(kept, grad):
    return (low(grad),)
low.defvjp(low_keep, low_pass)
low_back.defvjp(back_keep, back_low)
highest = lax.Precision.HIGHEST

def matmul(former, latter):
    return jnp.dot(former, latter, precision=highest, preferred_element_type=jnp.float32)

def norm_rows(values, gains, shifts):
    average = lax.optimization_barrier(jnp.mean(values, axis=-1, keepdims=True))
    centred = values - average
    spread = lax.optimization_barrier(jnp.mean(centred * centred, axis=-1, keepdims=True))
    return centred * lax.rsqrt(spread + 1e-05) * gains + shifts

def attend_block(query_block, query_segs, key_vecs, value_vecs, set_segs):
    scores = jnp.einsum('qhd,khd->hqk', query_block, key_vecs, precision=highest) * HD ** (-0.5)
    scores = low_back(scores)
    allowed = query_segs[:, None] == set_segs[None, :]
    scores = jnp.where(allowed[None], scores, -1e+30)
    shares = jax.nn.softmax(scores, axis=-1)
    return jnp.einsum('hqk,khd->qhd', low(shares), value_vecs, precision=highest)

def layer_set(set_rows, set_segs, params):
    qkv_weight, out_weight, up_weight, down_weight, first_gain, first_bias, second_gain, second_bias, out_bias, up_bias, down_bias = params
    length = set_rows.shape[0]
    normed = low(norm_rows(set_rows, first_gain, first_bias))
    mixed = low(low_back(matmul(normed, qkv_weight)))
    queries = mixed[:, :D].reshape(length, H, HD)
    key_vecs = mixed[:, D:2 * D].reshape(length, H, HD)
    value_vecs = mixed[:, 2 * D:].reshape(length, H, HD)
    block_rows = min(512, length)
    blocks = length // block_rows

    def one_block(element):
        return attend_block(element[0], element[1], key_vecs, value_vecs, set_segs)
    attended = lax.map(jax.checkpoint(one_block), (queries.reshape(blocks, block_rows, H, HD), set_segs.reshape(blocks, block_rows)))
    attended = low(low_back(attended.reshape(length, D)))
    branch = low_back(matmul(attended, out_weight) + out_bias)
    middle = set_rows + branch
    normed_two = low(norm_rows(middle, second_gain, second_bias))
    upper = low_back(matmul(normed_two, up_weight) + up_bias)
    activ = low(jax.nn.gelu(upper, approximate=False))
    output = low_back(matmul(activ, down_weight) + down_bias)
    return middle + output

def reference(inputs, segment_ids, cotangent, qkv_weight, out_weight, up_weight, down_weight, first_gain, first_bias, second_gain, second_bias, out_bias, up_bias, down_bias):
    params = tuple((member.astype(jnp.float32) for member in (qkv_weight, out_weight, up_weight, down_weight, first_gain, first_bias, second_gain, second_bias, out_bias, up_bias, down_bias)))
    flat_rows = inputs.astype(jnp.float32).reshape(-1, SEQ, D)
    flat_segs = segment_ids.reshape(-1, SEQ)

    def forward(rows_all, params_all):

        def scan_step(running, element):
            return (running, layer_set(element[0], element[1], params_all))
        unused, outcome = lax.scan(scan_step, jnp.float32(0.0), (rows_all, flat_segs))
        return outcome
    outcome, pullback = jax.vjp(forward, flat_rows, params)
    input_grad, grads = pullback(cotangent.astype(jnp.float32).reshape(flat_rows.shape))
    return (outcome.reshape(inputs.shape), input_grad.reshape(inputs.shape), grads[0], grads[1], grads[2], grads[3], grads[4], grads[5], grads[6], grads[7], grads[8], grads[9], grads[10])
```

```python
from functools import partial

import jax
import jax.numpy as jnp
from jax import lax
from jax.experimental import pallas as pl
from jax.experimental.pallas import tpu as pltpu
from jax.sharding import PartitionSpec as P

H = 8


epsilon = 1e-05
masked_score = -1e30


def dense(former, latter):
    return jnp.dot(former, latter, preferred_element_type=jnp.float32)


def norm_rows(values, gains, shifts):
    average = jnp.mean(values, axis=-1, keepdims=True)
    centred = values - average
    inverse = lax.rsqrt(jnp.mean(centred * centred, axis=-1, keepdims=True) + epsilon)
    scaled = centred * inverse
    return (scaled * gains + shifts, scaled, inverse)


def norm_back(gradient, scaled, inverse, gains):
    upstream = gradient * gains
    return inverse * (
        upstream
        - jnp.mean(upstream, axis=-1, keepdims=True)
        - scaled * jnp.mean(upstream * scaled, axis=-1, keepdims=True)
    )


def block_scan(update, carried, pieces):
    amount = pieces[0].shape[1]
    stride = min(512, amount)

    def block_step(state_now, number):
        sliced = tuple(
            (lax.dynamic_slice_in_dim(member, number * stride, stride, 1) for member in pieces)
        )
        return (update(state_now, sliced), None)

    carried, unused = lax.scan(block_step, carried, jnp.arange(amount // stride))
    return carried


def split_heads(rows, head_count):
    return rows.reshape(rows.shape[0], rows.shape[1], head_count, rows.shape[2] // head_count)


def attend_piece(running, sliced, queries, query_segs):
    maximum, totals, accumulated = running
    key_part, value_part, seg_part = sliced
    head_count, head_size = (queries.shape[2], queries.shape[3])
    key_heads = split_heads(key_part, head_count)
    value_heads = split_heads(value_part, head_count)
    scores = jnp.einsum(
        "sqhd,skhd->shqk", queries, key_heads, preferred_element_type=jnp.float32
    ) * head_size ** (-0.5)
    allowed = query_segs[:, None, :, None] == seg_part[:, None, None, :]
    scores = jnp.where(allowed, scores, masked_score)
    highest = jnp.maximum(maximum, jnp.max(scores, axis=-1, keepdims=True))
    factor = jnp.exp(maximum - highest)
    shares = jnp.exp(scores - highest)
    totals = totals * factor + jnp.sum(shares, axis=-1, keepdims=True)
    accumulated = accumulated * factor + jnp.einsum(
        "shqk,skhd->shqd",
        shares.astype(jnp.bfloat16),
        value_heads,
        preferred_element_type=jnp.float32,
    )
    return (highest, totals, accumulated)


def fold_keys(running, pieces, queries, query_segs):
    return block_scan(
        partial(attend_piece, queries=queries, query_segs=query_segs), running, pieces
    )


def grad_block(queries, grad_heads, query_segs, log_total, delta, key_heads, value_heads, key_segs):
    head_size = queries.shape[3]
    scores = jnp.einsum(
        "sqhd,skhd->shqk", queries, key_heads, preferred_element_type=jnp.float32
    ) * head_size ** (-0.5)
    allowed = query_segs[:, None, :, None] == key_segs[:, None, None, :]
    shares = jnp.where(allowed, jnp.exp(scores - log_total), 0.0)
    grad_shares = jnp.einsum(
        "sqhd,skhd->shqk", grad_heads, value_heads, preferred_element_type=jnp.float32
    )
    grad_scores = (shares * (grad_shares - delta)).astype(jnp.bfloat16)
    return (shares.astype(jnp.bfloat16), grad_scores)


def micro_step(set_inputs, set_segs, set_cotangent, gathered):
    (
        weight_qkv,
        weight_out,
        weight_up,
        weight_down,
        gain_one,
        shift_one,
        gain_two,
        shift_two,
        bias_out,
        bias_up,
        bias_down,
    ) = gathered
    set_count, tok_count, features = set_inputs.shape
    head_count = H
    head_size = features // head_count
    scale = head_size ** (-0.5)
    rows = set_inputs.astype(jnp.float32).reshape(-1, features)
    normed, scaled_one, inverse_one = norm_rows(
        rows, gain_one.astype(jnp.float32), shift_one.astype(jnp.float32)
    )
    normed_low = normed.astype(jnp.bfloat16)
    mixed = dense(normed_low, weight_qkv).astype(jnp.bfloat16)
    queries = mixed[:, :features].reshape(set_count, tok_count, head_count, head_size)
    key_rows = mixed[:, features : 2 * features].reshape(set_count, tok_count, features)
    value_rows = mixed[:, 2 * features :].reshape(set_count, tok_count, features)
    running = (
        jnp.full((set_count, head_count, tok_count, 1), masked_score, jnp.float32),
        jnp.zeros((set_count, head_count, tok_count, 1), jnp.float32),
        jnp.zeros((set_count, head_count, tok_count, head_size), jnp.float32),
    )
    running = fold_keys(
        running,
        (
            lax.all_gather(key_rows, "blk", axis=1, tiled=True),
            lax.all_gather(value_rows, "blk", axis=1, tiled=True),
            lax.all_gather(set_segs, "blk", axis=1, tiled=True),
        ),
        queries=queries,
        query_segs=set_segs,
    )
    maximum, totals, accumulated = running
    attended = accumulated / totals
    log_total = maximum + jnp.log(totals)
    attended_low = jnp.transpose(attended, (0, 2, 1, 3)).reshape(-1, features).astype(jnp.bfloat16)
    middle = rows + dense(attended_low, weight_out) + bias_out.astype(jnp.float32)
    normed_two, scaled_two, inverse_two = norm_rows(
        middle, gain_two.astype(jnp.float32), shift_two.astype(jnp.float32)
    )
    normed_two_low = normed_two.astype(jnp.bfloat16)
    upper = dense(normed_two_low, weight_up) + bias_up.astype(jnp.float32)
    activ_value, gelu_back = jax.vjp(lambda v: jax.nn.gelu(v, approximate=False), upper)
    activ_low = activ_value.astype(jnp.bfloat16)
    final = middle + dense(activ_low, weight_down) + bias_down.astype(jnp.float32)
    grad_out = set_cotangent.astype(jnp.float32).reshape(-1, features)
    grad_low = grad_out.astype(jnp.bfloat16)
    grad_down_bias = jnp.sum(grad_low.astype(jnp.float32), axis=0)
    grad_down = jnp.einsum("rf,rd->fd", activ_low, grad_low, preferred_element_type=jnp.float32)
    grad_activ = jnp.einsum("rd,fd->rf", grad_low, weight_down, preferred_element_type=jnp.float32)
    grad_upper = gelu_back(grad_activ)[0].astype(jnp.bfloat16)
    grad_up_bias = jnp.sum(grad_upper.astype(jnp.float32), axis=0)
    grad_up = jnp.einsum(
        "rd,rf->df", normed_two_low, grad_upper, preferred_element_type=jnp.float32
    )
    grad_normed_two = jnp.einsum(
        "rf,df->rd", grad_upper, weight_up, preferred_element_type=jnp.float32
    )
    grad_gain_two = jnp.sum(grad_normed_two * scaled_two, axis=0)
    grad_shift_two = jnp.sum(grad_normed_two, axis=0)
    grad_middle = grad_out + norm_back(
        grad_normed_two, scaled_two, inverse_two, gain_two.astype(jnp.float32)
    )
    branch_low = grad_middle.astype(jnp.bfloat16)
    grad_out_bias = jnp.sum(branch_low.astype(jnp.float32), axis=0)
    grad_out_weight = jnp.einsum(
        "rd,re->de", attended_low, branch_low, preferred_element_type=jnp.float32
    )
    grad_attended = jnp.einsum(
        "re,de->rd", branch_low, weight_out, preferred_element_type=jnp.float32
    )
    grad_heads = grad_attended.astype(jnp.bfloat16).reshape(
        set_count, tok_count, head_count, head_size
    )
    delta = jnp.einsum("sqhd,shqd->shq", grad_heads.astype(jnp.float32), attended)[..., None]
    everything = (
        lax.all_gather(key_rows, "blk", axis=1, tiled=True),
        lax.all_gather(value_rows, "blk", axis=1, tiled=True),
        lax.all_gather(set_segs, "blk", axis=1, tiled=True),
    )
    length = everything[0].shape[1]
    stride = min(512, length)

    def key_block(grad_query, number):
        key_part = lax.dynamic_slice_in_dim(everything[0], number * stride, stride, 1)
        value_part = lax.dynamic_slice_in_dim(everything[1], number * stride, stride, 1)
        seg_part = lax.dynamic_slice_in_dim(everything[2], number * stride, stride, 1)
        key_heads = split_heads(key_part, head_count)
        share_low, score_low = grad_block(
            queries,
            grad_heads,
            set_segs,
            log_total,
            delta,
            key_heads,
            split_heads(value_part, head_count),
            seg_part,
        )
        grad_query = (
            grad_query
            + jnp.einsum(
                "shqk,skhd->sqhd", score_low, key_heads, preferred_element_type=jnp.float32
            )
            * scale
        )
        key_term = (
            jnp.einsum("shqk,sqhd->kshd", score_low, queries, preferred_element_type=jnp.float32)
            * scale
        )
        value_term = jnp.einsum(
            "shqk,sqhd->kshd", share_low, grad_heads, preferred_element_type=jnp.float32
        )
        return (
            grad_query,
            jnp.concatenate(
                (
                    key_term.reshape(stride, set_count, features),
                    value_term.reshape(stride, set_count, features),
                ),
                axis=-1,
            ),
        )

    grad_query, terms = lax.scan(
        key_block, jnp.zeros(queries.shape, jnp.float32), jnp.arange(length // stride)
    )
    summed = lax.psum_scatter(
        terms.reshape(length, set_count, 2 * features).astype(jnp.bfloat16),
        "blk",
        scatter_dimension=0,
        tiled=True,
    ).astype(jnp.float32)
    summed = jnp.transpose(summed, (1, 0, 2)).reshape(-1, 2 * features)
    grad_keys = summed[:, :features]
    grad_values = summed[:, features:]
    grad_mixed = jnp.concatenate(
        (grad_query.reshape(-1, features), grad_keys, grad_values), axis=-1
    ).astype(jnp.bfloat16)
    grad_qkv = jnp.einsum("rd,re->de", normed_low, grad_mixed, preferred_element_type=jnp.float32)
    grad_normed = jnp.einsum(
        "re,de->rd", grad_mixed, weight_qkv, preferred_element_type=jnp.float32
    )
    grad_gain_one = jnp.sum(grad_normed * scaled_one, axis=0)
    grad_shift_one = jnp.sum(grad_normed, axis=0)
    grad_input = grad_middle + norm_back(
        grad_normed, scaled_one, inverse_one, gain_one.astype(jnp.float32)
    )
    local_grads = (
        grad_qkv,
        grad_out_weight,
        grad_up,
        grad_down,
        grad_gain_one,
        grad_shift_one,
        grad_gain_two,
        grad_shift_two,
        grad_out_bias,
        grad_up_bias,
        grad_down_bias,
    )
    return (
        final.reshape(set_count, tok_count, features),
        grad_input.reshape(set_count, tok_count, features),
        local_grads,
    )


def body(
    inputs,
    segment_ids,
    cotangent,
    qkv_weight,
    out_weight,
    up_weight,
    down_weight,
    first_gain,
    first_bias,
    second_gain,
    second_bias,
    out_bias,
    up_bias,
    down_bias,
):
    shards = (
        qkv_weight,
        out_weight,
        up_weight,
        down_weight,
        first_gain,
        first_bias,
        second_gain,
        second_bias,
        out_bias,
        up_bias,
        down_bias,
    )
    shard_sums = tuple((jnp.zeros(member.shape, jnp.float32) for member in shards))
    outcomes = []
    input_grads = []
    for micro_index in range(inputs.shape[0]):
        gathered = (
            lax.all_gather(qkv_weight, ("batch", "blk"), axis=0, tiled=True),
            lax.all_gather(out_weight, ("batch", "blk"), axis=0, tiled=True),
            lax.all_gather(up_weight, ("batch", "blk"), axis=0, tiled=True),
            lax.all_gather(down_weight, ("batch", "blk"), axis=0, tiled=True),
            lax.all_gather(first_gain, ("batch", "blk"), axis=0, tiled=True),
            lax.all_gather(first_bias, ("batch", "blk"), axis=0, tiled=True),
            lax.all_gather(second_gain, ("batch", "blk"), axis=0, tiled=True),
            lax.all_gather(second_bias, ("batch", "blk"), axis=0, tiled=True),
            lax.all_gather(out_bias, ("batch", "blk"), axis=0, tiled=True),
            lax.all_gather(up_bias, ("batch", "blk"), axis=0, tiled=True),
            lax.all_gather(down_bias, ("batch", "blk"), axis=0, tiled=True),
        )
        final, grad_input, local_grads = micro_step(
            inputs[micro_index], segment_ids[micro_index], cotangent[micro_index], gathered
        )
        outcomes.append(final)
        input_grads.append(grad_input)
        summed = (
            lax.psum_scatter(local_grads[0], ("batch", "blk"), scatter_dimension=0, tiled=True),
            lax.psum_scatter(local_grads[1], ("batch", "blk"), scatter_dimension=0, tiled=True),
            lax.psum_scatter(local_grads[2], ("batch", "blk"), scatter_dimension=0, tiled=True),
            lax.psum_scatter(local_grads[3], ("batch", "blk"), scatter_dimension=0, tiled=True),
            lax.psum_scatter(local_grads[4], ("batch", "blk"), scatter_dimension=0, tiled=True),
            lax.psum_scatter(local_grads[5], ("batch", "blk"), scatter_dimension=0, tiled=True),
            lax.psum_scatter(local_grads[6], ("batch", "blk"), scatter_dimension=0, tiled=True),
            lax.psum_scatter(local_grads[7], ("batch", "blk"), scatter_dimension=0, tiled=True),
            lax.psum_scatter(local_grads[8], ("batch", "blk"), scatter_dimension=0, tiled=True),
            lax.psum_scatter(local_grads[9], ("batch", "blk"), scatter_dimension=0, tiled=True),
            lax.psum_scatter(local_grads[10], ("batch", "blk"), scatter_dimension=0, tiled=True),
        )
        shard_sums = tuple((former + latter for former, latter in zip(shard_sums, summed)))
    return (jnp.stack(outcomes), jnp.stack(input_grads)) + tuple(shard_sums)


AXES = ("batch", "blk")
Y, C, ZH, Z0, X = 16, 8, 4, 2, 1
TEAM = (0, Z0, C, C | Z0)


def swap(values, mask):
    return lax.ppermute(values, AXES, [(i, i ^ mask) for i in range(32)])


def regroup(values, flip):
    pairs = []
    for i in range(32):
        core, right = (i >> 3) & 1, i & 1
        pairs.append((i, (i & (Y | Z0)) | (right << 3) | ((i & ZH) ^ (flip << 2)) | core))
    return lax.ppermute(values, AXES, pairs)


def ordered(near, far, bit, axis):
    return jnp.stack((jnp.where(bit == 0, near, far), jnp.where(bit == 0, far, near)), axis)


def grow(values, axis, bit, mask):
    return ordered(values, swap(values, mask), bit, axis)


def pick(values, place, axis=0):
    return lax.dynamic_index_in_dim(values, place, axis, keepdims=False)


def shrink(values, axis, bit, mask):
    got = swap(pick(values, 1 - bit, axis), mask)
    return pick(values, bit, axis).astype(jnp.float32) + got.astype(jnp.float32)


def low(values):
    return values.astype(jnp.bfloat16)


def wide(values):
    return values.astype(jnp.float32)


def team_trade(parts, quarter, bit_c, bit_z):
    own = pick(parts, quarter)
    got = [swap(pick(parts, quarter ^ r), TEAM[r]) for r in (1, 2, 3)]
    return ordered(
        ordered(own, got[0], bit_z, 0), ordered(got[1], got[2], bit_z, 0), bit_c, 0
    )


def team_gather(rows):
    near = jnp.concatenate((rows, swap(rows, Z0)), 0)
    return jnp.concatenate((near, swap(near, C)), 0)


def team_scatter(near, far):
    half = near.shape[0] // 2
    near = wide(near) + wide(swap(low(far), C))
    return near[:half] + wide(swap(low(near[half:]), Z0))


def dot_t(former, latter):
    return lax.dot_general(
        former, latter, (((1,), (1,)), ((), ())), preferred_element_type=jnp.float32
    )


def dot_rows(former, latter):
    return lax.dot_general(
        former, latter, (((0,), (0,)), ((), ())), preferred_element_type=jnp.float32
    )


STEP = 256
HEAD = 128


def attend_kernel(seg_col, seg_row, mixed, out, logs):
    rows = mixed.shape[0]
    heads = out.shape[1] // HEAD
    scale = HEAD ** (-0.5)
    for head in range(heads):
        at_q, at_k, at_v = (HEAD * (part * heads + head) for part in range(3))

        def block(number, unused):
            spot = pl.ds(pl.multiple_of(number * STEP, STEP), STEP)
            scores = dot_t(mixed[:, at_k : at_k + HEAD], mixed[spot, at_q : at_q + HEAD]) * scale
            scores = jnp.where(seg_col[...] == seg_row[:, spot], scores, masked_score)
            highest = jnp.max(scores, axis=0, keepdims=True)
            shares = jnp.exp(scores - highest)
            total = jnp.sum(shares, axis=0, keepdims=True)
            mixture = dot_rows(mixed[:, at_v : at_v + HEAD], low(shares)) / total
            out[spot, at_q : at_q + HEAD] = low(mixture.T)
            logs[head : head + 1, spot] = highest + jnp.log(total)
            return unused

        lax.fori_loop(0, rows // STEP, block, 0)


def attend_back_kernel(seg_col, seg_row, mixed, grads, logs, out, key_sum, value_sum):
    rows = mixed.shape[0]
    heads = grads.shape[1] // HEAD
    scale = HEAD ** (-0.5)
    for head in range(heads):
        at_q, at_k, at_v = (HEAD * (part * heads + head) for part in range(3))
        key_sum[...] = jnp.zeros_like(key_sum)
        value_sum[...] = jnp.zeros_like(value_sum)

        def block(number, unused):
            spot = pl.ds(pl.multiple_of(number * STEP, STEP), STEP)
            queries = mixed[spot, at_q : at_q + HEAD]
            grad = grads[spot, at_q : at_q + HEAD]
            keys = mixed[:, at_k : at_k + HEAD]
            scores = dot_t(keys, queries) * scale
            shares = jnp.exp(scores - logs[head : head + 1, spot])
            shares = jnp.where(seg_col[...] == seg_row[:, spot], shares, 0.0)
            grad_shares = dot_t(mixed[:, at_v : at_v + HEAD], grad)
            delta = jnp.sum(shares * grad_shares, axis=0, keepdims=True)
            grad_scores = low(shares * (grad_shares - delta))
            value_sum[...] += jnp.dot(low(shares), grad, preferred_element_type=jnp.float32)
            key_sum[...] += jnp.dot(grad_scores, queries, preferred_element_type=jnp.float32)
            out[spot, at_q : at_q + HEAD] = low((dot_rows(keys, grad_scores) * scale).T)
            return unused

        lax.fori_loop(0, rows // STEP, block, 0)
        out[:, at_k : at_k + HEAD] = low(key_sum[...] * scale)
        out[:, at_v : at_v + HEAD] = low(value_sum[...])


def attend(seg_col, seg_row, mixed):
    rows, columns = mixed.shape
    heads = columns // (3 * HEAD)
    work = 2 * rows * rows * HEAD * heads
    return pl.pallas_call(
        attend_kernel,
        out_shape=(
            jax.ShapeDtypeStruct((rows, heads * HEAD), jnp.bfloat16),
            jax.ShapeDtypeStruct((heads, rows), jnp.float32),
        ),
        compiler_params=pltpu.CompilerParams(vmem_limit_bytes=24 << 20),
        cost_estimate=pl.CostEstimate(
            flops=2 * work, transcendentals=rows * rows * heads, bytes_accessed=4 << 20
        ),
        name="attend",
    )(seg_col, seg_row, mixed)


def attend_back(seg_col, seg_row, mixed, grads, logs):
    rows, columns = mixed.shape
    heads = columns // (3 * HEAD)
    work = 2 * rows * rows * HEAD * heads
    return pl.pallas_call(
        attend_back_kernel,
        out_shape=jax.ShapeDtypeStruct((rows, columns), jnp.bfloat16),
        scratch_shapes=[pltpu.VMEM((rows, HEAD), jnp.float32)] * 2,
        compiler_params=pltpu.CompilerParams(vmem_limit_bytes=32 << 20),
        cost_estimate=pl.CostEstimate(
            flops=5 * work, transcendentals=rows * rows * heads, bytes_accessed=6 << 20
        ),
        name="attend_back",
    )(seg_col, seg_row, mixed, grads, logs)


def team_body(
    inputs,
    segment_ids,
    cotangent,
    qkv_weight,
    out_weight,
    up_weight,
    down_weight,
    first_gain,
    first_bias,
    second_gain,
    second_bias,
    out_bias,
    up_bias,
    down_bias,
):
    batch_at, blk_at = lax.axis_index("batch"), lax.axis_index("blk")
    y, c = batch_at >> 1, batch_at & 1
    zh, z0, x = blk_at >> 2, (blk_at >> 1) & 1, blk_at & 1
    quarter = 2 * c + z0
    tokens, features = inputs.shape[2:]
    own_rows = 2 * tokens

    packed = jnp.concatenate(
        (
            first_gain,
            first_bias,
            second_gain,
            second_bias,
            out_bias,
            down_bias,
            up_bias,
            low(segment_ids.reshape(-1)),
        )
    )[None]
    for bit, mask in ((c, C), (x, X), (z0, Z0), (y, Y), (zh, ZH)):
        axis = {C: 0, X: 1, Z0: 1, Y: 0, ZH: 2}[mask]
        packed = grow(packed, axis, bit, mask)
    packed = packed.reshape(32, -1)
    vectors = wide(packed[:, :192]).reshape(32, 6, 32).transpose(1, 0, 2).reshape(6, features)
    gain_one, shift_one, gain_two, shift_two, bias_out, bias_down = vectors
    bias_up = wide(packed[:, 192:320]).reshape(2, 2, 2, 2, 2, 128)
    bias_up = pick(pick(bias_up, z0, 3), c, 1).reshape(-1)
    ids = wide(packed[:, 320:]).reshape(2, 2, 8, 2, tokens)
    ids = pick(pick(pick(ids, y), x), zh, 1)
    row = jnp.arange(8)
    chunk = 4 * ((row & 1) ^ zh) + 2 * (((row >> 1) & 1) ^ z0) + ((row >> 2) ^ c)
    same = chunk[:, None] == jnp.arange(8)[None, :]
    ids = jnp.sum(jnp.where(same[:, :, None], ids[None], 0.0), axis=1)
    seg_row = ids.reshape(1, -1)
    seg_col = ids.reshape(-1, 1)

    qkv_parts = qkv_weight.reshape(32, 6, 4, 128).transpose(2, 0, 1, 3).reshape(4, 32, 768)
    up_parts = up_weight.reshape(32, 2, 2, 2, 2, 2, 128).transpose(2, 4, 0, 1, 3, 5, 6)
    up_parts = up_parts.reshape(4, 32, 1024)
    parts = team_trade(jnp.concatenate((qkv_parts, up_parts), 2), quarter, c, z0)
    w_qkv = parts[..., :768]
    w_qkv = grow(grow(grow(w_qkv, 1, zh, ZH), 3, x, X), 0, y, Y).reshape(features, -1)
    w_out = grow(out_weight, 0, z0, Z0)
    w_out = jnp.where(zh == z0, w_out, swap(w_out, ZH))
    w_out = grow(grow(w_out, 1, x, X), 0, y, Y).reshape(-1, features)
    w_up = grow(grow(grow(parts[..., 768:], 1, zh, ZH), 0, y, Y), 4, x, X).reshape(features, -1)
    w_down = grow(grow(grow(down_weight, 0, zh, ZH), 1, x, X), 0, y, Y).reshape(-1, features)

    def take_rows(values):
        return jnp.concatenate(
            [regroup(pick(values[:, 0], zh ^ flip), flip) for flip in (0, 1)], 0
        )

    def give_rows(values):
        near = regroup(low(values[:tokens]), 0)
        far = regroup(low(values[tokens:]), 1)
        return wide(ordered(near, far, zh, 0))[:, None]

    rows = wide(take_rows(inputs))
    normed, scaled_one, inverse_one = norm_rows(rows, gain_one, shift_one)
    normed = team_gather(low(normed))
    mixed = low(dense(normed, w_qkv))
    attended, logs = attend(seg_col, seg_row, mixed)
    half = attended.shape[0] // 2

    def split_dense(former, product):
        return team_scatter(product(former[:half]), product(former[half:]))

    middle = rows + split_dense(attended, lambda v: dense(v, w_out)) + bias_out
    normed_two, scaled_two, inverse_two = norm_rows(middle, gain_two, shift_two)
    normed_two = team_gather(low(normed_two))
    upper = dense(normed_two, w_up) + bias_up
    activ, gelu_back = jax.vjp(lambda v: jax.nn.gelu(v, approximate=False), upper)
    activ = low(activ)
    grad_own = take_rows(cotangent)
    grad_out = team_gather(grad_own)
    grad_own = wide(grad_own)
    grad_upper = low(gelu_back(dot_t(grad_out, w_down))[0])
    grad_two = split_dense(grad_upper, lambda v: dot_t(v, w_up))
    final = give_rows(middle + split_dense(activ, lambda v: dense(v, w_down)) + bias_down)

    grad_down = low(dot_rows(activ, grad_out)).reshape(2, 2, 2, 128, features)
    grad_down = shrink(low(shrink(low(shrink(grad_down, 0, y, Y)), 1, x, X)), 0, zh, ZH)
    grad_up = low(dot_rows(normed_two, grad_upper)).reshape(2, 2, 2, 2, 2, 32, -1)
    grad_up = shrink(low(shrink(low(shrink(grad_up, 4, x, X)), 0, y, Y)), 1, zh, ZH)
    grad_up = team_trade(low(grad_up).reshape(4, 32, -1), quarter, c, z0)
    grad_up = grad_up.reshape(2, 2, 32, 2, 2, 2, 128).transpose(2, 3, 0, 4, 1, 5, 6)
    grad_up = wide(grad_up.reshape(32, -1))

    grad_middle = grad_own + norm_back(grad_two, scaled_two, inverse_two, gain_two)
    branch_own = low(grad_middle)
    branch = team_gather(branch_own)
    grad_attended = low(dot_t(branch, w_out))
    grad_w_out = low(dot_rows(attended, branch)).reshape(2, 2, 2, 32, features)
    grad_w_out = low(shrink(low(shrink(grad_w_out, 0, y, Y)), 1, x, X))
    grad_w_out = wide(grad_w_out) + wide(swap(grad_w_out, ZH))
    handed = swap(low(pick(grad_w_out, 1 - z0)), Z0)
    grad_w_out = jnp.where(zh == z0, pick(grad_w_out, z0), wide(handed))

    grad_mixed = attend_back(seg_col, seg_row, mixed, grad_attended, logs)
    grad_one = split_dense(grad_mixed, lambda v: dot_t(v, w_qkv))
    grad_qkv = low(dot_rows(normed, grad_mixed)).reshape(2, 2, 2, 2, 2, 32, -1)
    grad_qkv = shrink(low(shrink(low(shrink(grad_qkv, 0, y, Y)), 3, x, X)), 1, zh, ZH)
    grad_qkv = team_trade(low(grad_qkv).reshape(4, 32, -1), quarter, c, z0)
    grad_qkv = wide(grad_qkv.reshape(4, 32, 6, 128).transpose(1, 2, 0, 3).reshape(32, -1))
    input_grad = give_rows(
        grad_middle + norm_back(grad_one, scaled_one, inverse_one, gain_one)
    )

    sums = jnp.stack(
        (
            jnp.sum(grad_one * scaled_one, 0),
            jnp.sum(grad_one, 0),
            jnp.sum(grad_two * scaled_two, 0),
            jnp.sum(grad_two, 0),
            jnp.sum(wide(branch_own), 0),
            jnp.sum(grad_own, 0),
        )
    )
    up_sums = jnp.sum(wide(grad_upper), 0)
    spread = jnp.where(jnp.arange(4)[:, None] == quarter, up_sums[None], 0.0)
    sums = jnp.concatenate((sums, spread), 0)
    for mask in (C, X, Z0, Y, ZH):
        sums = sums + swap(sums, mask)
    flat = batch_at * 8 + blk_at
    small = lax.dynamic_slice_in_dim(sums[:6], flat * 32, 32, 1)
    grad_up_bias = pick(sums[6:], quarter)
    grad_up_bias = lax.dynamic_slice_in_dim(grad_up_bias, (4 * y + 2 * zh + x) * 128, 128)
    return (
        final,
        input_grad,
        grad_qkv,
        grad_w_out,
        grad_up,
        grad_down,
        small[0],
        small[1],
        small[2],
        small[3],
        small[4],
        grad_up_bias,
        small[5],
    )


def chosen_body(mesh, *arrays):
    shape = arrays[0].shape
    sizes = (mesh.shape["batch"], mesh.shape["blk"])
    if sizes == (4, 8) and shape == (2, 1, 128, 1024) and arrays[5].shape == (32, 4096):
        return team_body(*arrays)
    return body(*arrays)


def solution(mesh):
    return jax.shard_map(
        partial(chosen_body, mesh),
        mesh=mesh,
        in_specs=(
            P(None, "batch", "blk", None),
            P(None, "batch", "blk"),
            P(None, "batch", "blk", None),
            P(("batch", "blk"), None),
            P(("batch", "blk"), None),
            P(("batch", "blk"), None),
            P(("batch", "blk"), None),
            P(("batch", "blk")),
            P(("batch", "blk")),
            P(("batch", "blk")),
            P(("batch", "blk")),
            P(("batch", "blk")),
            P(("batch", "blk")),
            P(("batch", "blk")),
        ),
        out_specs=(
            P(None, "batch", "blk", None),
            P(None, "batch", "blk", None),
            P(("batch", "blk"), None),
            P(("batch", "blk"), None),
            P(("batch", "blk"), None),
            P(("batch", "blk"), None),
            P(("batch", "blk")),
            P(("batch", "blk")),
            P(("batch", "blk")),
            P(("batch", "blk")),
            P(("batch", "blk")),
            P(("batch", "blk")),
            P(("batch", "blk")),
        ),
        check_vma=False,
    )
```

```python
from functools import partial

import jax
import jax.numpy as jnp
from jax import lax
from jax.experimental import pallas as pl
from jax.experimental.pallas import tpu as pltpu
from jax.sharding import PartitionSpec as P

H = 8


epsilon = 1e-05
masked_score = -1e30


def dense(former, latter):
    return jnp.dot(former, latter, preferred_element_type=jnp.float32)


def norm_rows(values, gains, shifts):
    average = jnp.mean(values, axis=-1, keepdims=True)
    centred = values - average
    inverse = lax.rsqrt(jnp.mean(centred * centred, axis=-1, keepdims=True) + epsilon)
    scaled = centred * inverse
    return (scaled * gains + shifts, scaled, inverse)


def norm_back(gradient, scaled, inverse, gains):
    upstream = gradient * gains
    return inverse * (
        upstream
        - jnp.mean(upstream, axis=-1, keepdims=True)
        - scaled * jnp.mean(upstream * scaled, axis=-1, keepdims=True)
    )


def block_scan(update, carried, pieces):
    amount = pieces[0].shape[1]
    stride = min(512, amount)

    def block_step(state_now, number):
        sliced = tuple(
            (lax.dynamic_slice_in_dim(member, number * stride, stride, 1) for member in pieces)
        )
        return (update(state_now, sliced), None)

    carried, unused = lax.scan(block_step, carried, jnp.arange(amount // stride))
    return carried


def split_heads(rows, head_count):
    return rows.reshape(rows.shape[0], rows.shape[1], head_count, rows.shape[2] // head_count)


def attend_piece(running, sliced, queries, query_segs):
    maximum, totals, accumulated = running
    key_part, value_part, seg_part = sliced
    head_count, head_size = (queries.shape[2], queries.shape[3])
    key_heads = split_heads(key_part, head_count)
    value_heads = split_heads(value_part, head_count)
    scores = jnp.einsum(
        "sqhd,skhd->shqk", queries, key_heads, preferred_element_type=jnp.float32
    ) * head_size ** (-0.5)
    allowed = query_segs[:, None, :, None] == seg_part[:, None, None, :]
    scores = jnp.where(allowed, scores, masked_score)
    highest = jnp.maximum(maximum, jnp.max(scores, axis=-1, keepdims=True))
    factor = jnp.exp(maximum - highest)
    shares = jnp.exp(scores - highest)
    totals = totals * factor + jnp.sum(shares, axis=-1, keepdims=True)
    accumulated = accumulated * factor + jnp.einsum(
        "shqk,skhd->shqd",
        shares.astype(jnp.bfloat16),
        value_heads,
        preferred_element_type=jnp.float32,
    )
    return (highest, totals, accumulated)


def fold_keys(running, pieces, queries, query_segs):
    return block_scan(
        partial(attend_piece, queries=queries, query_segs=query_segs), running, pieces
    )


def grad_block(queries, grad_heads, query_segs, log_total, delta, key_heads, value_heads, key_segs):
    head_size = queries.shape[3]
    scores = jnp.einsum(
        "sqhd,skhd->shqk", queries, key_heads, preferred_element_type=jnp.float32
    ) * head_size ** (-0.5)
    allowed = query_segs[:, None, :, None] == key_segs[:, None, None, :]
    shares = jnp.where(allowed, jnp.exp(scores - log_total), 0.0)
    grad_shares = jnp.einsum(
        "sqhd,skhd->shqk", grad_heads, value_heads, preferred_element_type=jnp.float32
    )
    grad_scores = (shares * (grad_shares - delta)).astype(jnp.bfloat16)
    return (shares.astype(jnp.bfloat16), grad_scores)


def micro_step(set_inputs, set_segs, set_cotangent, gathered):
    (
        weight_qkv,
        weight_out,
        weight_up,
        weight_down,
        gain_one,
        shift_one,
        gain_two,
        shift_two,
        bias_out,
        bias_up,
        bias_down,
    ) = gathered
    set_count, tok_count, features = set_inputs.shape
    head_count = H
    head_size = features // head_count
    scale = head_size ** (-0.5)
    rows = set_inputs.astype(jnp.float32).reshape(-1, features)
    normed, scaled_one, inverse_one = norm_rows(
        rows, gain_one.astype(jnp.float32), shift_one.astype(jnp.float32)
    )
    normed_low = normed.astype(jnp.bfloat16)
    mixed = dense(normed_low, weight_qkv).astype(jnp.bfloat16)
    queries = mixed[:, :features].reshape(set_count, tok_count, head_count, head_size)
    key_rows = mixed[:, features : 2 * features].reshape(set_count, tok_count, features)
    value_rows = mixed[:, 2 * features :].reshape(set_count, tok_count, features)
    running = (
        jnp.full((set_count, head_count, tok_count, 1), masked_score, jnp.float32),
        jnp.zeros((set_count, head_count, tok_count, 1), jnp.float32),
        jnp.zeros((set_count, head_count, tok_count, head_size), jnp.float32),
    )
    running = fold_keys(
        running,
        (
            lax.all_gather(key_rows, "blk", axis=1, tiled=True),
            lax.all_gather(value_rows, "blk", axis=1, tiled=True),
            lax.all_gather(set_segs, "blk", axis=1, tiled=True),
        ),
        queries=queries,
        query_segs=set_segs,
    )
    maximum, totals, accumulated = running
    attended = accumulated / totals
    log_total = maximum + jnp.log(totals)
    attended_low = jnp.transpose(attended, (0, 2, 1, 3)).reshape(-1, features).astype(jnp.bfloat16)
    middle = rows + dense(attended_low, weight_out) + bias_out.astype(jnp.float32)
    normed_two, scaled_two, inverse_two = norm_rows(
        middle, gain_two.astype(jnp.float32), shift_two.astype(jnp.float32)
    )
    normed_two_low = normed_two.astype(jnp.bfloat16)
    upper = dense(normed_two_low, weight_up) + bias_up.astype(jnp.float32)
    activ_value, gelu_back = jax.vjp(lambda v: jax.nn.gelu(v, approximate=False), upper)
    activ_low = activ_value.astype(jnp.bfloat16)
    final = middle + dense(activ_low, weight_down) + bias_down.astype(jnp.float32)
    grad_out = set_cotangent.astype(jnp.float32).reshape(-1, features)
    grad_low = grad_out.astype(jnp.bfloat16)
    grad_down_bias = jnp.sum(grad_low.astype(jnp.float32), axis=0)
    grad_down = jnp.einsum("rf,rd->fd", activ_low, grad_low, preferred_element_type=jnp.float32)
    grad_activ = jnp.einsum("rd,fd->rf", grad_low, weight_down, preferred_element_type=jnp.float32)
    grad_upper = gelu_back(grad_activ)[0].astype(jnp.bfloat16)
    grad_up_bias = jnp.sum(grad_upper.astype(jnp.float32), axis=0)
    grad_up = jnp.einsum(
        "rd,rf->df", normed_two_low, grad_upper, preferred_element_type=jnp.float32
    )
    grad_normed_two = jnp.einsum(
        "rf,df->rd", grad_upper, weight_up, preferred_element_type=jnp.float32
    )
    grad_gain_two = jnp.sum(grad_normed_two * scaled_two, axis=0)
    grad_shift_two = jnp.sum(grad_normed_two, axis=0)
    grad_middle = grad_out + norm_back(
        grad_normed_two, scaled_two, inverse_two, gain_two.astype(jnp.float32)
    )
    branch_low = grad_middle.astype(jnp.bfloat16)
    grad_out_bias = jnp.sum(branch_low.astype(jnp.float32), axis=0)
    grad_out_weight = jnp.einsum(
        "rd,re->de", attended_low, branch_low, preferred_element_type=jnp.float32
    )
    grad_attended = jnp.einsum(
        "re,de->rd", branch_low, weight_out, preferred_element_type=jnp.float32
    )
    grad_heads = grad_attended.astype(jnp.bfloat16).reshape(
        set_count, tok_count, head_count, head_size
    )
    delta = jnp.einsum("sqhd,shqd->shq", grad_heads.astype(jnp.float32), attended)[..., None]
    everything = (
        lax.all_gather(key_rows, "blk", axis=1, tiled=True),
        lax.all_gather(value_rows, "blk", axis=1, tiled=True),
        lax.all_gather(set_segs, "blk", axis=1, tiled=True),
    )
    length = everything[0].shape[1]
    stride = min(512, length)

    def key_block(grad_query, number):
        key_part = lax.dynamic_slice_in_dim(everything[0], number * stride, stride, 1)
        value_part = lax.dynamic_slice_in_dim(everything[1], number * stride, stride, 1)
        seg_part = lax.dynamic_slice_in_dim(everything[2], number * stride, stride, 1)
        key_heads = split_heads(key_part, head_count)
        share_low, score_low = grad_block(
            queries,
            grad_heads,
            set_segs,
            log_total,
            delta,
            key_heads,
            split_heads(value_part, head_count),
            seg_part,
        )
        grad_query = (
            grad_query
            + jnp.einsum(
                "shqk,skhd->sqhd", score_low, key_heads, preferred_element_type=jnp.float32
            )
            * scale
        )
        key_term = (
            jnp.einsum("shqk,sqhd->kshd", score_low, queries, preferred_element_type=jnp.float32)
            * scale
        )
        value_term = jnp.einsum(
            "shqk,sqhd->kshd", share_low, grad_heads, preferred_element_type=jnp.float32
        )
        return (
            grad_query,
            jnp.concatenate(
                (
                    key_term.reshape(stride, set_count, features),
                    value_term.reshape(stride, set_count, features),
                ),
                axis=-1,
            ),
        )

    grad_query, terms = lax.scan(
        key_block, jnp.zeros(queries.shape, jnp.float32), jnp.arange(length // stride)
    )
    summed = lax.psum_scatter(
        terms.reshape(length, set_count, 2 * features).astype(jnp.bfloat16),
        "blk",
        scatter_dimension=0,
        tiled=True,
    ).astype(jnp.float32)
    summed = jnp.transpose(summed, (1, 0, 2)).reshape(-1, 2 * features)
    grad_keys = summed[:, :features]
    grad_values = summed[:, features:]
    grad_mixed = jnp.concatenate(
        (grad_query.reshape(-1, features), grad_keys, grad_values), axis=-1
    ).astype(jnp.bfloat16)
    grad_qkv = jnp.einsum("rd,re->de", normed_low, grad_mixed, preferred_element_type=jnp.float32)
    grad_normed = jnp.einsum(
        "re,de->rd", grad_mixed, weight_qkv, preferred_element_type=jnp.float32
    )
    grad_gain_one = jnp.sum(grad_normed * scaled_one, axis=0)
    grad_shift_one = jnp.sum(grad_normed, axis=0)
    grad_input = grad_middle + norm_back(
        grad_normed, scaled_one, inverse_one, gain_one.astype(jnp.float32)
    )
    local_grads = (
        grad_qkv,
        grad_out_weight,
        grad_up,
        grad_down,
        grad_gain_one,
        grad_shift_one,
        grad_gain_two,
        grad_shift_two,
        grad_out_bias,
        grad_up_bias,
        grad_down_bias,
    )
    return (
        final.reshape(set_count, tok_count, features),
        grad_input.reshape(set_count, tok_count, features),
        local_grads,
    )


def body(
    inputs,
    segment_ids,
    cotangent,
    qkv_weight,
    out_weight,
    up_weight,
    down_weight,
    first_gain,
    first_bias,
    second_gain,
    second_bias,
    out_bias,
    up_bias,
    down_bias,
):
    shards = (
        qkv_weight,
        out_weight,
        up_weight,
        down_weight,
        first_gain,
        first_bias,
        second_gain,
        second_bias,
        out_bias,
        up_bias,
        down_bias,
    )
    shard_sums = tuple((jnp.zeros(member.shape, jnp.float32) for member in shards))
    outcomes = []
    input_grads = []
    for micro_index in range(inputs.shape[0]):
        gathered = (
            lax.all_gather(qkv_weight, ("batch", "blk"), axis=0, tiled=True),
            lax.all_gather(out_weight, ("batch", "blk"), axis=0, tiled=True),
            lax.all_gather(up_weight, ("batch", "blk"), axis=0, tiled=True),
            lax.all_gather(down_weight, ("batch", "blk"), axis=0, tiled=True),
            lax.all_gather(first_gain, ("batch", "blk"), axis=0, tiled=True),
            lax.all_gather(first_bias, ("batch", "blk"), axis=0, tiled=True),
            lax.all_gather(second_gain, ("batch", "blk"), axis=0, tiled=True),
            lax.all_gather(second_bias, ("batch", "blk"), axis=0, tiled=True),
            lax.all_gather(out_bias, ("batch", "blk"), axis=0, tiled=True),
            lax.all_gather(up_bias, ("batch", "blk"), axis=0, tiled=True),
            lax.all_gather(down_bias, ("batch", "blk"), axis=0, tiled=True),
        )
        final, grad_input, local_grads = micro_step(
            inputs[micro_index], segment_ids[micro_index], cotangent[micro_index], gathered
        )
        outcomes.append(final)
        input_grads.append(grad_input)
        summed = (
            lax.psum_scatter(local_grads[0], ("batch", "blk"), scatter_dimension=0, tiled=True),
            lax.psum_scatter(local_grads[1], ("batch", "blk"), scatter_dimension=0, tiled=True),
            lax.psum_scatter(local_grads[2], ("batch", "blk"), scatter_dimension=0, tiled=True),
            lax.psum_scatter(local_grads[3], ("batch", "blk"), scatter_dimension=0, tiled=True),
            lax.psum_scatter(local_grads[4], ("batch", "blk"), scatter_dimension=0, tiled=True),
            lax.psum_scatter(local_grads[5], ("batch", "blk"), scatter_dimension=0, tiled=True),
            lax.psum_scatter(local_grads[6], ("batch", "blk"), scatter_dimension=0, tiled=True),
            lax.psum_scatter(local_grads[7], ("batch", "blk"), scatter_dimension=0, tiled=True),
            lax.psum_scatter(local_grads[8], ("batch", "blk"), scatter_dimension=0, tiled=True),
            lax.psum_scatter(local_grads[9], ("batch", "blk"), scatter_dimension=0, tiled=True),
            lax.psum_scatter(local_grads[10], ("batch", "blk"), scatter_dimension=0, tiled=True),
        )
        shard_sums = tuple((former + latter for former, latter in zip(shard_sums, summed)))
    return (jnp.stack(outcomes), jnp.stack(input_grads)) + tuple(shard_sums)


AXES = ("batch", "blk")
Y, C, ZH, Z0, X = 16, 8, 4, 2, 1
TEAM = (0, Z0, C, C | Z0)


def swap(values, mask):
    return lax.ppermute(values, AXES, [(i, i ^ mask) for i in range(32)])


def regroup(values, flip):
    pairs = []
    for i in range(32):
        core, right = (i >> 3) & 1, i & 1
        pairs.append((i, (i & (Y | Z0)) | (right << 3) | ((i & ZH) ^ (flip << 2)) | core))
    return lax.ppermute(values, AXES, pairs)


def ordered(near, far, bit, axis):
    return jnp.stack((jnp.where(bit == 0, near, far), jnp.where(bit == 0, far, near)), axis)


def grow(values, axis, bit, mask):
    return ordered(values, swap(values, mask), bit, axis)


def pick(values, place, axis=0):
    return lax.dynamic_index_in_dim(values, place, axis, keepdims=False)


def shrink(values, axis, bit, mask):
    got = swap(pick(values, 1 - bit, axis), mask)
    return pick(values, bit, axis).astype(jnp.float32) + got.astype(jnp.float32)


def tie(*values):
    return lax.optimization_barrier(values)


def low(values):
    return values.astype(jnp.bfloat16)


def wide(values):
    return values.astype(jnp.float32)


def team_trade(parts, quarter, bit_c, bit_z):
    own = pick(parts, quarter)
    got = [swap(pick(parts, quarter ^ r), TEAM[r]) for r in (1, 2, 3)]
    return ordered(
        ordered(own, got[0], bit_z, 0), ordered(got[1], got[2], bit_z, 0), bit_c, 0
    )


def team_gather(rows):
    near = jnp.concatenate((rows, swap(rows, Z0)), 0)
    return jnp.concatenate((near, swap(near, C)), 0)


def team_scatter(near, far):
    half = near.shape[0] // 2
    near = wide(near) + wide(swap(low(far), C))
    return near[:half] + wide(swap(low(near[half:]), Z0))


def dot_t(former, latter):
    return lax.dot_general(
        former, latter, (((1,), (1,)), ((), ())), preferred_element_type=jnp.float32
    )


def dot_rows(former, latter):
    return lax.dot_general(
        former, latter, (((0,), (0,)), ((), ())), preferred_element_type=jnp.float32
    )


STEP = 256
HEAD = 128


def image_of(ends, flips, shape, axis, base=0):
    row = lax.broadcasted_iota(jnp.int32, shape, axis) + base
    block = row >> 7
    chunk = 4 * ((block & 1) ^ flips[0]) + 2 * (((block >> 1) & 1) ^ flips[1])
    chunk = chunk + ((block >> 2) ^ flips[2])
    spot = (chunk * 128 + (row & 127)).astype(jnp.float32)
    return sum(jnp.where(spot >= ends[i], 1.0, 0.0) for i in range(3))


def attend_kernel(ends, flips, mixed, near, far, logs, images):
    rows = mixed.shape[0]
    heads = near.shape[1] // HEAD
    scale = HEAD ** (-0.5)
    images[...] = image_of(ends, flips, images.shape, 0)
    for head in range(heads):
        at_q, at_k, at_v = (HEAD * (part * heads + head) for part in range(3))
        for place, out in enumerate((near, far)):

            def block(number, unused):
                start = pl.multiple_of((2 * number + place) * STEP, STEP)
                spot = pl.ds(start, STEP)
                scores = dot_t(mixed[:, at_k : at_k + HEAD], mixed[spot, at_q : at_q + HEAD])
                image = image_of(ends, flips, (1, STEP), 1, start)
                column = images[...]
                column = jnp.concatenate([column] * (STEP // HEAD), 1)
                scores = jnp.where(column == image, scores * scale, masked_score)
                highest = jnp.max(scores, axis=0, keepdims=True)
                shares = jnp.exp(scores - highest)
                total = jnp.sum(shares, axis=0, keepdims=True)
                mixture = dot_rows(mixed[:, at_v : at_v + HEAD], low(shares)) / total
                target = pl.ds(pl.multiple_of(number * STEP, STEP), STEP)
                out[target, at_q : at_q + HEAD] = low(mixture.T)
                logs[head : head + 1, spot] = highest + jnp.log(total)
                return unused

            lax.fori_loop(0, rows // STEP // 2, block, 0)


def attend_back_kernel(
    ends, flips, mixed, near, far, logs, out, key_sum, value_sum, images
):
    rows = mixed.shape[0]
    heads = near.shape[1] // HEAD
    scale = HEAD ** (-0.5)
    images[...] = image_of(ends, flips, images.shape, 0)
    for head in range(heads):
        at_q, at_k, at_v = (HEAD * (part * heads + head) for part in range(3))
        key_sum[...] = jnp.zeros_like(key_sum)
        value_sum[...] = jnp.zeros_like(value_sum)
        for place, grads in enumerate((near, far)):

            def block(number, unused):
                start = pl.multiple_of((2 * number + place) * STEP, STEP)
                spot = pl.ds(start, STEP)
                source = pl.ds(pl.multiple_of(number * STEP, STEP), STEP)
                queries = mixed[spot, at_q : at_q + HEAD]
                grad = grads[source, at_q : at_q + HEAD]
                keys = mixed[:, at_k : at_k + HEAD]
                image = image_of(ends, flips, (1, STEP), 1, start)
                column = images[...]
                column = jnp.concatenate([column] * (STEP // HEAD), 1)
                scores = dot_t(keys, queries) * scale
                shares = jnp.exp(scores - logs[head : head + 1, spot])
                shares = jnp.where(column == image, shares, 0.0)
                grad_shares = dot_t(mixed[:, at_v : at_v + HEAD], grad)
                delta = jnp.sum(shares * grad_shares, axis=0, keepdims=True)
                grad_scores = low(shares * (grad_shares - delta))
                value_sum[...] += jnp.dot(low(shares), grad, preferred_element_type=jnp.float32)
                key_sum[...] += jnp.dot(grad_scores, queries, preferred_element_type=jnp.float32)
                out[spot, at_q : at_q + HEAD] = low((dot_rows(keys, grad_scores) * scale).T)
                return unused

            lax.fori_loop(0, rows // STEP // 2, block, 0)
        out[:, at_k : at_k + HEAD] = low(key_sum[...] * scale)
        out[:, at_v : at_v + HEAD] = low(value_sum[...])


def in_smem():
    return pl.BlockSpec(memory_space=pltpu.SMEM)


def in_vmem():
    return pl.BlockSpec(memory_space=pltpu.VMEM)


def attend(ends, flips, mixed):
    rows, columns = mixed.shape
    heads = columns // (3 * HEAD)
    work = 2 * rows * rows * HEAD * heads
    half = jax.ShapeDtypeStruct((rows // 2, heads * HEAD), jnp.bfloat16)
    return pl.pallas_call(
        attend_kernel,
        in_specs=[in_smem(), in_smem(), in_vmem()],
        out_shape=(half, half, jax.ShapeDtypeStruct((heads, rows), jnp.float32)),
        scratch_shapes=[pltpu.VMEM((rows, HEAD), jnp.float32)],
        compiler_params=pltpu.CompilerParams(vmem_limit_bytes=24 << 20),
        cost_estimate=pl.CostEstimate(
            flops=2 * work, transcendentals=rows * rows * heads, bytes_accessed=4 << 20
        ),
        name="attend",
    )(ends, flips, mixed)


def attend_back(ends, flips, mixed, near, far, logs):
    rows, columns = mixed.shape
    heads = columns // (3 * HEAD)
    work = 2 * rows * rows * HEAD * heads
    return pl.pallas_call(
        attend_back_kernel,
        in_specs=[in_smem(), in_smem()] + [in_vmem()] * 4,
        out_shape=jax.ShapeDtypeStruct((rows, columns), jnp.bfloat16),
        scratch_shapes=[pltpu.VMEM((rows, HEAD), jnp.float32)] * 3,
        compiler_params=pltpu.CompilerParams(vmem_limit_bytes=32 << 20),
        cost_estimate=pl.CostEstimate(
            flops=5 * work, transcendentals=rows * rows * heads, bytes_accessed=6 << 20
        ),
        name="attend_back",
    )(ends, flips, mixed, near, far, logs)


def split_kernel(quarter, qkv, up, ids, up_vector, *refs):
    singles, outs, board = refs[:6], refs[6:10], refs[10]
    board[...] = jnp.zeros_like(board)
    for i, single in enumerate(singles):
        board[i : i + 1, :32] = wide(single[...])
    for i in range(4):
        board[6 + i : 7 + i, :32] = wide(up_vector[:, 32 * i : 32 * i + 32])
    for m in range(2):
        for i in range(3):
            below = jnp.where(ids[m : m + 1] <= i, 1.0, 0.0)
            below = jnp.sum(below, axis=1, keepdims=True)
            board[10 + 3 * m + i : 11 + 3 * m + i, :] = jnp.broadcast_to(below, (1, 128))
    extra = low(board[...].T[:32])
    for r, out in enumerate(outs):
        member = quarter[0] ^ r
        for part in range(6):
            spot = pl.ds(pl.multiple_of((4 * part + member) * HEAD, HEAD), HEAD)
            out[:, part * HEAD : (part + 1) * HEAD] = qkv[:, spot]
        out[:, 6 * HEAD : 7 * HEAD] = extra
        for part in range(8):
            block = 16 * (part >> 2) + 8 * (member >> 1) + 4 * ((part >> 1) & 1)
            block = block + 2 * (member & 1) + (part & 1)
            spot = pl.ds(pl.multiple_of(block * HEAD, HEAD), HEAD)
            out[:, (7 + part) * HEAD : (8 + part) * HEAD] = up[:, spot]


def split(quarter, qkv, up, ids, up_vector, singles):
    rows = qkv.shape[0]
    return pl.pallas_call(
        split_kernel,
        in_specs=[in_smem()] + [in_vmem()] * 10,
        out_shape=[jax.ShapeDtypeStruct((rows, 15 * HEAD), jnp.bfloat16)] * 4,
        out_specs=[in_vmem()] * 4,
        scratch_shapes=[pltpu.VMEM((128, 128), jnp.float32)],
        cost_estimate=pl.CostEstimate(flops=0, transcendentals=0, bytes_accessed=1 << 20),
        name="split",
    )(
        quarter.reshape(1),
        qkv,
        up,
        ids.reshape(2, -1),
        up_vector.reshape(1, -1),
        *(single.reshape(1, -1) for single in singles),
    )


def feed_kernel(rows, grads, w_up, w_down, bias, activ, grad_up, back, forth, sums):
    total = jnp.zeros((1, w_up.shape[1]), jnp.float32)
    for number in range(rows.shape[0] // STEP):
        spot = slice(number * STEP, (number + 1) * STEP)
        upper = dense(rows[spot], w_up[...]) + bias[...]
        share = 0.5 + 0.5 * lax.erf(upper * (0.5**0.5))
        act = low(upper * share)
        slope = share + upper * jnp.exp(-0.5 * upper * upper) * 0.3989422804014327
        grad = low(dot_t(grads[spot], w_down[...]) * slope)
        activ[spot] = act
        grad_up[spot] = grad
        total += jnp.sum(wide(grad), axis=0, keepdims=True)
        back[spot] = low(dot_t(grad, w_up[...]))
        forth[spot] = low(dense(act, w_down[...]))
    sums[...] = total


def feed(rows, grads, w_up, w_down, bias):
    count, features = rows.shape
    hidden = w_up.shape[1]
    kind = jnp.bfloat16
    return pl.pallas_call(
        feed_kernel,
        out_shape=(
            jax.ShapeDtypeStruct((count, hidden), kind),
            jax.ShapeDtypeStruct((count, hidden), kind),
            jax.ShapeDtypeStruct((count, features), kind),
            jax.ShapeDtypeStruct((count, features), kind),
            jax.ShapeDtypeStruct((1, hidden), jnp.float32),
        ),
        compiler_params=pltpu.CompilerParams(vmem_limit_bytes=40 << 20),
        cost_estimate=pl.CostEstimate(
            flops=8 * count * features * hidden,
            transcendentals=2 * count * hidden,
            bytes_accessed=8 << 20,
        ),
        name="feed",
    )(rows, grads, w_up, w_down, bias)


def team_body(
    inputs,
    segment_ids,
    cotangent,
    qkv_weight,
    out_weight,
    up_weight,
    down_weight,
    first_gain,
    first_bias,
    second_gain,
    second_bias,
    out_bias,
    up_bias,
    down_bias,
):
    batch_at, blk_at = lax.axis_index("batch"), lax.axis_index("blk")
    y, c = batch_at >> 1, batch_at & 1
    zh, z0, x = blk_at >> 2, (blk_at >> 1) & 1, blk_at & 1
    quarter = 2 * c + z0
    tokens, features = inputs.shape[2:]

    def send_rows(values):
        return [regroup(pick(values[:, 0], zh ^ flip), flip) for flip in (0, 1)]

    rows_near, rows_far = send_rows(inputs)
    singles = (first_gain, first_bias, second_gain, second_bias, out_bias, down_bias)
    own, *others = split(quarter, qkv_weight, up_weight, segment_ids, up_bias, singles)
    got = [swap(other, mask) for other, mask in zip(others, TEAM[1:])]
    w_out = grow(out_weight, 0, zh, ZH)
    rows_near, rows_far, own, *got, w_out, down_weight = tie(
        rows_near, rows_far, own, *got, w_out, down_weight
    )

    parts = ordered(ordered(own, got[0], z0, 0), ordered(got[1], got[2], z0, 0), c, 0)
    w_qkv = grow(parts[..., :896], 1, zh, ZH)
    w_up = parts[..., 896:]
    rows = wide(jnp.concatenate((rows_near, rows_far), 0))
    average = jnp.mean(rows, axis=-1, keepdims=True)
    centred = rows - average
    inverse_one = lax.rsqrt(jnp.mean(centred * centred, axis=-1, keepdims=True) + epsilon)
    scaled_one = centred * inverse_one
    sent = low(scaled_one)
    side = jnp.concatenate((sent, swap(sent, Z0)), 0)
    across = swap(side, C)
    w_qkv, down_weight = tie(w_qkv, down_weight)
    w_near = grow(w_qkv[0], 2, x, X)
    w_far = grow(w_qkv[1], 0, y, Y)
    w_near = grow(w_near, 0, y, Y)
    w_far = grow(w_far, 3, x, X)
    w_down = grow(down_weight, 0, zh, ZH)
    w_out = grow(grow(w_out, 1, z0, Z0), 0, y, Y)
    side, across, w_near, w_far, w_out, w_up, w_down, cotangent = tie(
        side, across, w_near, w_far, w_out, w_up, w_down, cotangent
    )

    w_qkv = jnp.stack((w_near, w_far), 1).reshape(features, -1)
    extra = wide(w_qkv[:, 768:]).T
    w_qkv = w_qkv[:, :768]
    gain_one, shift_one, gain_two, shift_two, bias_out, bias_down = (
        extra[i : i + 1] for i in range(6)
    )
    bias_up = extra[6:10].reshape(4, 2, 2, 2, 2, 2, 32)
    bias_up = pick(pick(bias_up, z0, 4), c, 2).transpose(1, 2, 3, 0, 4).reshape(1, -1)
    place = jnp.arange(features)
    ours = ((place >> 9) == y) & (((place >> 8) & 1) == x)
    ends = jnp.where(ours[None], lax.dynamic_slice_in_dim(extra, 10 + 3 * zh, 3, 0), 0.0)
    ends = jnp.sum(ends, 1) * (1.0 / 32.0)
    flips = jnp.stack((zh, z0, c))
    normed = low(wide(jnp.concatenate((side, across), 0)) * gain_one + shift_one)
    grad_near, grad_far = send_rows(cotangent)
    w_out = grow(w_out, 3, x, X)
    w_down = grow(w_down, 0, y, Y)
    mixed = low(dense(normed, w_qkv))
    attended, away, logs = attend(ends, flips, mixed)
    attended, away, w_out, w_up, w_down, grad_near, grad_far = tie(
        attended, away, w_out, w_up, w_down, grad_near, grad_far
    )

    tokens_two = 2 * tokens
    came = swap(away, Z0)
    out_own = pick(w_out, z0, 1).reshape(-1, features)
    out_came = pick(w_out, 1 - z0, 1).reshape(-1, features)
    grad_own = jnp.concatenate((grad_near, grad_far), 0)
    w_up = grow(w_up, 1, zh, ZH)
    w_down = grow(w_down, 2, x, X)
    came, out_own, out_came, grad_own = tie(came, out_own, out_came, grad_own)

    grad_side = jnp.concatenate((grad_own, swap(grad_own, Z0)), 0)
    far = dense(attended[tokens_two:], out_own) + dense(came[tokens_two:], out_came)
    near = dense(attended[:tokens_two], out_own) + dense(came[:tokens_two], out_came)
    middle = rows + near + wide(swap(low(far), C)) + bias_out
    middle, w_up = tie(middle, w_up)
    normed_two, scaled_two, inverse_two = norm_rows(middle, gain_two, shift_two)
    normed_two = low(normed_two)
    near = jnp.concatenate((normed_two, swap(normed_two, Z0)), 0)
    w_near = grow(w_up[0], 2, x, X)
    w_far = grow(w_up[1], 0, y, Y)
    near, grad_side, w_near, w_far = tie(near, grad_side, w_near, w_far)
    far = swap(near, C)
    grad_across = swap(grad_side, C)
    w_near = grow(w_near, 0, y, Y)
    w_far = grow(w_far, 3, x, X)
    w_up = jnp.stack((w_near, w_far), 1).reshape(features, -1)
    w_down = w_down.reshape(-1, features)
    near, far, w_down, w_up, grad_side, grad_across = tie(
        near, far, w_down, w_up, grad_side, grad_across
    )

    activ_far, upper_far, back_far, forth_far, sums_far = feed(
        far, grad_across, w_up, w_down, bias_up
    )
    activ, upper, back, forth, sums_near = feed(near, grad_side, w_up, w_down, bias_up)
    back, forth, back_far, forth_far, activ, upper = tie(
        back, forth, swap(back_far, C), swap(forth_far, C), activ, upper
    )

    count = back.shape[0] // 2
    back = wide(back) + wide(back_far)
    forth = wide(forth) + wide(forth_far)
    grad_two = back[:count] + wide(swap(low(back[count:]), Z0))
    grad_out = jnp.concatenate((grad_side, grad_across), 0)
    normed_two = jnp.concatenate((near, far), 0)
    activ = jnp.concatenate((activ, activ_far), 0)
    grad_upper = jnp.concatenate((upper, upper_far), 0)
    grad_down = low(dot_rows(activ, grad_out)).reshape(2, 2, 2, 128, features)
    grad_up = low(dot_rows(normed_two, grad_upper)).reshape(2, 2, 2, 2, 2, 32, -1)
    grad_two, grad_down, grad_up, forth = tie(grad_two, grad_down, grad_up, forth)
    grad_down = low(shrink(grad_down, 0, y, Y))
    grad_up = low(shrink(grad_up, 4, x, X))

    grad_middle = wide(grad_own) + norm_back(grad_two, scaled_two, inverse_two, gain_two)
    branch_own = low(grad_middle)
    branch_own, branch, forth = tie(branch_own, swap(branch_own, C), forth)
    branch = jnp.concatenate((branch_own, branch), 0)
    grad_came = swap(low(dot_t(branch, out_came)), Z0)
    grad_attended = low(dot_t(branch, out_own))
    grad_w_out = ordered(
        low(dot_rows(attended, branch)).reshape(2, 2, 2, 32, features),
        low(dot_rows(came, branch)).reshape(2, 2, 2, 32, features),
        z0,
        1,
    )
    grad_came, grad_down, grad_up, grad_w_out, forth = tie(
        grad_came, grad_down, grad_up, grad_w_out, forth
    )

    def give_rows(values):
        got = (regroup(values[:tokens], 0), regroup(values[tokens:], 1))
        return wide(ordered(*got, zh, 0))[:, None]

    grad_down = low(shrink(grad_down, 1, x, X))
    grad_up = low(shrink(grad_up, 0, y, Y))
    grad_mixed = attend_back(ends, flips, mixed, grad_attended, grad_came, logs)
    final = low(middle + forth[:count] + wide(swap(low(forth[count:]), Z0)) + bias_down)
    grad_mixed, grad_w_out, grad_up, grad_down, final = tie(
        grad_mixed, grad_w_out, grad_up, grad_down, final
    )

    half = 2 * tokens_two
    far = swap(low(dot_t(grad_mixed[half:], w_qkv)), C)
    back = dot_t(grad_mixed[:half], w_qkv)
    grad_qkv = low(dot_rows(normed, grad_mixed)).reshape(2, 2, 2, 2, 2, 32, -1)
    far, back, grad_qkv, grad_w_out, grad_up, grad_down, final = tie(
        far, back, grad_qkv, grad_w_out, grad_up, grad_down, final
    )
    back = back + wide(far)
    grad_one = back[:count] + wide(swap(low(back[count:]), Z0))
    qkv_near = low(shrink(low(shrink(grad_qkv[:, 0], 3, x, X)), 0, y, Y))
    qkv_far = low(shrink(low(shrink(grad_qkv[:, 1], 0, y, Y)), 2, x, X))
    grads = jnp.stack((grad_down, grad_up.transpose(1, 0, 2, 3, 4).reshape(2, 128, -1)), 1)
    grads = shrink(grads, 0, zh, ZH)
    grad_down = grads[0]
    grad_up = low(grads[1]).reshape(4, 32, -1)
    grad_w_out = low(shrink(grad_w_out, 0, y, Y))
    grad_qkv = jnp.stack((qkv_near, qkv_far), 0)
    given = low(grad_middle + norm_back(grad_one, scaled_one, inverse_one, gain_one))
    given, grad_qkv, grad_w_out, grad_up, grad_down, grad_one, final = tie(
        given, grad_qkv, grad_w_out, grad_up, grad_down, grad_one, final
    )

    input_grad = give_rows(given)
    final = give_rows(final)
    grad_qkv = low(shrink(grad_qkv, 1, zh, ZH)).reshape(4, 32, -1)
    grads = team_trade(jnp.concatenate((grad_qkv, grad_up), 2), quarter, c, z0)
    grad_qkv = grads[..., :768].reshape(4, 32, 6, 128).transpose(1, 2, 0, 3)
    grad_qkv = wide(grad_qkv.reshape(32, -1))
    grad_up = grads[..., 768:].reshape(2, 2, 32, 2, 2, 2, 128).transpose(2, 3, 0, 4, 1, 5, 6)
    grad_up = wide(grad_up.reshape(32, -1))
    grad_w_out = low(shrink(grad_w_out, 2, x, X))
    grad_w_out = shrink(low(shrink(grad_w_out, 0, zh, ZH)), 0, z0, Z0)
    sums = jnp.stack(
        (
            jnp.sum(grad_one * scaled_one, 0),
            jnp.sum(grad_one, 0),
            jnp.sum(grad_two * scaled_two, 0),
            jnp.sum(grad_two, 0),
            jnp.sum(wide(branch_own), 0),
            jnp.sum(wide(grad_own), 0),
        )
    )
    spread = jnp.where(jnp.arange(4)[:, None] == quarter, sums_near + sums_far, 0.0)
    sums = jnp.concatenate((sums, spread), 0)
    for mask in (ZH, C, X, Z0, Y):
        sums = sums + swap(sums, mask)
    flat = batch_at * 8 + blk_at
    small = lax.dynamic_slice_in_dim(sums[:6], flat * 32, 32, 1)
    grad_up_bias = pick(sums[6:], quarter)
    grad_up_bias = lax.dynamic_slice_in_dim(grad_up_bias, (4 * y + 2 * zh + x) * 128, 128)
    return (
        final,
        input_grad,
        grad_qkv,
        grad_w_out,
        grad_up,
        grad_down,
        small[0],
        small[1],
        small[2],
        small[3],
        small[4],
        grad_up_bias,
        small[5],
    )


def chosen_body(mesh, *arrays):
    shape = arrays[0].shape
    sizes = (mesh.shape["batch"], mesh.shape["blk"])
    if sizes == (4, 8) and shape == (2, 1, 128, 1024) and arrays[5].shape == (32, 4096):
        return team_body(*arrays)
    return body(*arrays)


def solution(mesh):
    return jax.shard_map(
        partial(chosen_body, mesh),
        mesh=mesh,
        in_specs=(
            P(None, "batch", "blk", None),
            P(None, "batch", "blk"),
            P(None, "batch", "blk", None),
            P(("batch", "blk"), None),
            P(("batch", "blk"), None),
            P(("batch", "blk"), None),
            P(("batch", "blk"), None),
            P(("batch", "blk")),
            P(("batch", "blk")),
            P(("batch", "blk")),
            P(("batch", "blk")),
            P(("batch", "blk")),
            P(("batch", "blk")),
            P(("batch", "blk")),
        ),
        out_specs=(
            P(None, "batch", "blk", None),
            P(None, "batch", "blk", None),
            P(("batch", "blk"), None),
            P(("batch", "blk"), None),
            P(("batch", "blk"), None),
            P(("batch", "blk"), None),
            P(("batch", "blk")),
            P(("batch", "blk")),
            P(("batch", "blk")),
            P(("batch", "blk")),
            P(("batch", "blk")),
            P(("batch", "blk")),
            P(("batch", "blk")),
        ),
        check_vma=False,
    )
```

```python
from functools import partial

import jax
import jax.numpy as jnp
from jax import lax
from jax.experimental import pallas as pl
from jax.experimental.pallas import tpu as pltpu
from jax.sharding import PartitionSpec as P

H = 8


epsilon = 1e-05
masked_score = -1e30


def dense(former, latter):
    return jnp.dot(former, latter, preferred_element_type=jnp.float32)


def norm_rows(values, gains, shifts):
    average = jnp.mean(values, axis=-1, keepdims=True)
    centred = values - average
    inverse = lax.rsqrt(jnp.mean(centred * centred, axis=-1, keepdims=True) + epsilon)
    scaled = centred * inverse
    return (scaled * gains + shifts, scaled, inverse)


def norm_back(gradient, scaled, inverse, gains):
    upstream = gradient * gains
    return inverse * (
        upstream
        - jnp.mean(upstream, axis=-1, keepdims=True)
        - scaled * jnp.mean(upstream * scaled, axis=-1, keepdims=True)
    )


def block_scan(update, carried, pieces):
    amount = pieces[0].shape[1]
    stride = min(512, amount)

    def block_step(state_now, number):
        sliced = tuple(
            (lax.dynamic_slice_in_dim(member, number * stride, stride, 1) for member in pieces)
        )
        return (update(state_now, sliced), None)

    carried, unused = lax.scan(block_step, carried, jnp.arange(amount // stride))
    return carried


def split_heads(rows, head_count):
    return rows.reshape(rows.shape[0], rows.shape[1], head_count, rows.shape[2] // head_count)


def attend_piece(running, sliced, queries, query_segs):
    maximum, totals, accumulated = running
    key_part, value_part, seg_part = sliced
    head_count, head_size = (queries.shape[2], queries.shape[3])
    key_heads = split_heads(key_part, head_count)
    value_heads = split_heads(value_part, head_count)
    scores = jnp.einsum(
        "sqhd,skhd->shqk", queries, key_heads, preferred_element_type=jnp.float32
    ) * head_size ** (-0.5)
    allowed = query_segs[:, None, :, None] == seg_part[:, None, None, :]
    scores = jnp.where(allowed, scores, masked_score)
    highest = jnp.maximum(maximum, jnp.max(scores, axis=-1, keepdims=True))
    factor = jnp.exp(maximum - highest)
    shares = jnp.exp(scores - highest)
    totals = totals * factor + jnp.sum(shares, axis=-1, keepdims=True)
    accumulated = accumulated * factor + jnp.einsum(
        "shqk,skhd->shqd",
        shares.astype(jnp.bfloat16),
        value_heads,
        preferred_element_type=jnp.float32,
    )
    return (highest, totals, accumulated)


def fold_keys(running, pieces, queries, query_segs):
    return block_scan(
        partial(attend_piece, queries=queries, query_segs=query_segs), running, pieces
    )


def grad_block(queries, grad_heads, query_segs, log_total, delta, key_heads, value_heads, key_segs):
    head_size = queries.shape[3]
    scores = jnp.einsum(
        "sqhd,skhd->shqk", queries, key_heads, preferred_element_type=jnp.float32
    ) * head_size ** (-0.5)
    allowed = query_segs[:, None, :, None] == key_segs[:, None, None, :]
    shares = jnp.where(allowed, jnp.exp(scores - log_total), 0.0)
    grad_shares = jnp.einsum(
        "sqhd,skhd->shqk", grad_heads, value_heads, preferred_element_type=jnp.float32
    )
    grad_scores = (shares * (grad_shares - delta)).astype(jnp.bfloat16)
    return (shares.astype(jnp.bfloat16), grad_scores)


def micro_step(set_inputs, set_segs, set_cotangent, gathered):
    (
        weight_qkv,
        weight_out,
        weight_up,
        weight_down,
        gain_one,
        shift_one,
        gain_two,
        shift_two,
        bias_out,
        bias_up,
        bias_down,
    ) = gathered
    set_count, tok_count, features = set_inputs.shape
    head_count = H
    head_size = features // head_count
    scale = head_size ** (-0.5)
    rows = set_inputs.astype(jnp.float32).reshape(-1, features)
    normed, scaled_one, inverse_one = norm_rows(
        rows, gain_one.astype(jnp.float32), shift_one.astype(jnp.float32)
    )
    normed_low = normed.astype(jnp.bfloat16)
    mixed = dense(normed_low, weight_qkv).astype(jnp.bfloat16)
    queries = mixed[:, :features].reshape(set_count, tok_count, head_count, head_size)
    key_rows = mixed[:, features : 2 * features].reshape(set_count, tok_count, features)
    value_rows = mixed[:, 2 * features :].reshape(set_count, tok_count, features)
    running = (
        jnp.full((set_count, head_count, tok_count, 1), masked_score, jnp.float32),
        jnp.zeros((set_count, head_count, tok_count, 1), jnp.float32),
        jnp.zeros((set_count, head_count, tok_count, head_size), jnp.float32),
    )
    running = fold_keys(
        running,
        (
            lax.all_gather(key_rows, "blk", axis=1, tiled=True),
            lax.all_gather(value_rows, "blk", axis=1, tiled=True),
            lax.all_gather(set_segs, "blk", axis=1, tiled=True),
        ),
        queries=queries,
        query_segs=set_segs,
    )
    maximum, totals, accumulated = running
    attended = accumulated / totals
    log_total = maximum + jnp.log(totals)
    attended_low = jnp.transpose(attended, (0, 2, 1, 3)).reshape(-1, features).astype(jnp.bfloat16)
    middle = rows + dense(attended_low, weight_out) + bias_out.astype(jnp.float32)
    normed_two, scaled_two, inverse_two = norm_rows(
        middle, gain_two.astype(jnp.float32), shift_two.astype(jnp.float32)
    )
    normed_two_low = normed_two.astype(jnp.bfloat16)
    upper = dense(normed_two_low, weight_up) + bias_up.astype(jnp.float32)
    activ_value, gelu_back = jax.vjp(lambda v: jax.nn.gelu(v, approximate=False), upper)
    activ_low = activ_value.astype(jnp.bfloat16)
    final = middle + dense(activ_low, weight_down) + bias_down.astype(jnp.float32)
    grad_out = set_cotangent.astype(jnp.float32).reshape(-1, features)
    grad_low = grad_out.astype(jnp.bfloat16)
    grad_down_bias = jnp.sum(grad_low.astype(jnp.float32), axis=0)
    grad_down = jnp.einsum("rf,rd->fd", activ_low, grad_low, preferred_element_type=jnp.float32)
    grad_activ = jnp.einsum("rd,fd->rf", grad_low, weight_down, preferred_element_type=jnp.float32)
    grad_upper = gelu_back(grad_activ)[0].astype(jnp.bfloat16)
    grad_up_bias = jnp.sum(grad_upper.astype(jnp.float32), axis=0)
    grad_up = jnp.einsum(
        "rd,rf->df", normed_two_low, grad_upper, preferred_element_type=jnp.float32
    )
    grad_normed_two = jnp.einsum(
        "rf,df->rd", grad_upper, weight_up, preferred_element_type=jnp.float32
    )
    grad_gain_two = jnp.sum(grad_normed_two * scaled_two, axis=0)
    grad_shift_two = jnp.sum(grad_normed_two, axis=0)
    grad_middle = grad_out + norm_back(
        grad_normed_two, scaled_two, inverse_two, gain_two.astype(jnp.float32)
    )
    branch_low = grad_middle.astype(jnp.bfloat16)
    grad_out_bias = jnp.sum(branch_low.astype(jnp.float32), axis=0)
    grad_out_weight = jnp.einsum(
        "rd,re->de", attended_low, branch_low, preferred_element_type=jnp.float32
    )
    grad_attended = jnp.einsum(
        "re,de->rd", branch_low, weight_out, preferred_element_type=jnp.float32
    )
    grad_heads = grad_attended.astype(jnp.bfloat16).reshape(
        set_count, tok_count, head_count, head_size
    )
    delta = jnp.einsum("sqhd,shqd->shq", grad_heads.astype(jnp.float32), attended)[..., None]
    everything = (
        lax.all_gather(key_rows, "blk", axis=1, tiled=True),
        lax.all_gather(value_rows, "blk", axis=1, tiled=True),
        lax.all_gather(set_segs, "blk", axis=1, tiled=True),
    )
    length = everything[0].shape[1]
    stride = min(512, length)

    def key_block(grad_query, number):
        key_part = lax.dynamic_slice_in_dim(everything[0], number * stride, stride, 1)
        value_part = lax.dynamic_slice_in_dim(everything[1], number * stride, stride, 1)
        seg_part = lax.dynamic_slice_in_dim(everything[2], number * stride, stride, 1)
        key_heads = split_heads(key_part, head_count)
        share_low, score_low = grad_block(
            queries,
            grad_heads,
            set_segs,
            log_total,
            delta,
            key_heads,
            split_heads(value_part, head_count),
            seg_part,
        )
        grad_query = (
            grad_query
            + jnp.einsum(
                "shqk,skhd->sqhd", score_low, key_heads, preferred_element_type=jnp.float32
            )
            * scale
        )
        key_term = (
            jnp.einsum("shqk,sqhd->kshd", score_low, queries, preferred_element_type=jnp.float32)
            * scale
        )
        value_term = jnp.einsum(
            "shqk,sqhd->kshd", share_low, grad_heads, preferred_element_type=jnp.float32
        )
        return (
            grad_query,
            jnp.concatenate(
                (
                    key_term.reshape(stride, set_count, features),
                    value_term.reshape(stride, set_count, features),
                ),
                axis=-1,
            ),
        )

    grad_query, terms = lax.scan(
        key_block, jnp.zeros(queries.shape, jnp.float32), jnp.arange(length // stride)
    )
    summed = lax.psum_scatter(
        terms.reshape(length, set_count, 2 * features).astype(jnp.bfloat16),
        "blk",
        scatter_dimension=0,
        tiled=True,
    ).astype(jnp.float32)
    summed = jnp.transpose(summed, (1, 0, 2)).reshape(-1, 2 * features)
    grad_keys = summed[:, :features]
    grad_values = summed[:, features:]
    grad_mixed = jnp.concatenate(
        (grad_query.reshape(-1, features), grad_keys, grad_values), axis=-1
    ).astype(jnp.bfloat16)
    grad_qkv = jnp.einsum("rd,re->de", normed_low, grad_mixed, preferred_element_type=jnp.float32)
    grad_normed = jnp.einsum(
        "re,de->rd", grad_mixed, weight_qkv, preferred_element_type=jnp.float32
    )
    grad_gain_one = jnp.sum(grad_normed * scaled_one, axis=0)
    grad_shift_one = jnp.sum(grad_normed, axis=0)
    grad_input = grad_middle + norm_back(
        grad_normed, scaled_one, inverse_one, gain_one.astype(jnp.float32)
    )
    local_grads = (
        grad_qkv,
        grad_out_weight,
        grad_up,
        grad_down,
        grad_gain_one,
        grad_shift_one,
        grad_gain_two,
        grad_shift_two,
        grad_out_bias,
        grad_up_bias,
        grad_down_bias,
    )
    return (
        final.reshape(set_count, tok_count, features),
        grad_input.reshape(set_count, tok_count, features),
        local_grads,
    )


def body(
    inputs,
    segment_ids,
    cotangent,
    qkv_weight,
    out_weight,
    up_weight,
    down_weight,
    first_gain,
    first_bias,
    second_gain,
    second_bias,
    out_bias,
    up_bias,
    down_bias,
):
    shards = (
        qkv_weight,
        out_weight,
        up_weight,
        down_weight,
        first_gain,
        first_bias,
        second_gain,
        second_bias,
        out_bias,
        up_bias,
        down_bias,
    )
    shard_sums = tuple((jnp.zeros(member.shape, jnp.float32) for member in shards))
    outcomes = []
    input_grads = []
    for micro_index in range(inputs.shape[0]):
        gathered = (
            lax.all_gather(qkv_weight, ("batch", "blk"), axis=0, tiled=True),
            lax.all_gather(out_weight, ("batch", "blk"), axis=0, tiled=True),
            lax.all_gather(up_weight, ("batch", "blk"), axis=0, tiled=True),
            lax.all_gather(down_weight, ("batch", "blk"), axis=0, tiled=True),
            lax.all_gather(first_gain, ("batch", "blk"), axis=0, tiled=True),
            lax.all_gather(first_bias, ("batch", "blk"), axis=0, tiled=True),
            lax.all_gather(second_gain, ("batch", "blk"), axis=0, tiled=True),
            lax.all_gather(second_bias, ("batch", "blk"), axis=0, tiled=True),
            lax.all_gather(out_bias, ("batch", "blk"), axis=0, tiled=True),
            lax.all_gather(up_bias, ("batch", "blk"), axis=0, tiled=True),
            lax.all_gather(down_bias, ("batch", "blk"), axis=0, tiled=True),
        )
        final, grad_input, local_grads = micro_step(
            inputs[micro_index], segment_ids[micro_index], cotangent[micro_index], gathered
        )
        outcomes.append(final)
        input_grads.append(grad_input)
        summed = (
            lax.psum_scatter(local_grads[0], ("batch", "blk"), scatter_dimension=0, tiled=True),
            lax.psum_scatter(local_grads[1], ("batch", "blk"), scatter_dimension=0, tiled=True),
            lax.psum_scatter(local_grads[2], ("batch", "blk"), scatter_dimension=0, tiled=True),
            lax.psum_scatter(local_grads[3], ("batch", "blk"), scatter_dimension=0, tiled=True),
            lax.psum_scatter(local_grads[4], ("batch", "blk"), scatter_dimension=0, tiled=True),
            lax.psum_scatter(local_grads[5], ("batch", "blk"), scatter_dimension=0, tiled=True),
            lax.psum_scatter(local_grads[6], ("batch", "blk"), scatter_dimension=0, tiled=True),
            lax.psum_scatter(local_grads[7], ("batch", "blk"), scatter_dimension=0, tiled=True),
            lax.psum_scatter(local_grads[8], ("batch", "blk"), scatter_dimension=0, tiled=True),
            lax.psum_scatter(local_grads[9], ("batch", "blk"), scatter_dimension=0, tiled=True),
            lax.psum_scatter(local_grads[10], ("batch", "blk"), scatter_dimension=0, tiled=True),
        )
        shard_sums = tuple((former + latter for former, latter in zip(shard_sums, summed)))
    return (jnp.stack(outcomes), jnp.stack(input_grads)) + tuple(shard_sums)


AXES = ("batch", "blk")
Y, C, ZH, Z0, X = 16, 8, 4, 2, 1
TEAM = (0, Z0, C, C | Z0)


def swap(values, mask):
    return lax.ppermute(values, AXES, [(i, i ^ mask) for i in range(32)])


def regroup(values, flip):
    pairs = []
    for i in range(32):
        core, right = (i >> 3) & 1, i & 1
        pairs.append((i, (i & (Y | Z0)) | (right << 3) | ((i & ZH) ^ (flip << 2)) | core))
    return lax.ppermute(values, AXES, pairs)


def ordered(near, far, bit, axis):
    return jnp.stack((jnp.where(bit == 0, near, far), jnp.where(bit == 0, far, near)), axis)


def grow(values, axis, bit, mask):
    return ordered(values, swap(values, mask), bit, axis)


def pick(values, place, axis=0):
    return lax.dynamic_index_in_dim(values, place, axis, keepdims=False)


def shrink(values, axis, bit, mask):
    got = swap(pick(values, 1 - bit, axis), mask)
    return pick(values, bit, axis).astype(jnp.float32) + got.astype(jnp.float32)


def tie(*values):
    return lax.optimization_barrier(values)


def low(values):
    return values.astype(jnp.bfloat16)


def wide(values):
    return values.astype(jnp.float32)


def team_trade(parts, quarter, bit_c, bit_z):
    own = pick(parts, quarter)
    got = [swap(pick(parts, quarter ^ r), TEAM[r]) for r in (1, 2, 3)]
    return ordered(
        ordered(own, got[0], bit_z, 0), ordered(got[1], got[2], bit_z, 0), bit_c, 0
    )


def team_gather(rows):
    near = jnp.concatenate((rows, swap(rows, Z0)), 0)
    return jnp.concatenate((near, swap(near, C)), 0)


def team_scatter(near, far):
    half = near.shape[0] // 2
    near = wide(near) + wide(swap(low(far), C))
    return near[:half] + wide(swap(low(near[half:]), Z0))


def dot_t(former, latter):
    return lax.dot_general(
        former, latter, (((1,), (1,)), ((), ())), preferred_element_type=jnp.float32
    )


def dot_rows(former, latter):
    return lax.dot_general(
        former, latter, (((0,), (0,)), ((), ())), preferred_element_type=jnp.float32
    )


STEP = 256
HEAD = 128


def image_of(ends, flips, shape, axis, base=0):
    row = lax.broadcasted_iota(jnp.int32, shape, axis) + base
    block = row >> 7
    chunk = 4 * ((block & 1) ^ flips[0]) + 2 * (((block >> 1) & 1) ^ flips[1])
    chunk = chunk + ((block >> 2) ^ flips[2])
    spot = (chunk * 128 + (row & 127)).astype(jnp.float32)
    return sum(jnp.where(spot >= ends[i], 1.0, 0.0) for i in range(3))


def attend_kernel(ends, flips, mixed, near, far, logs, images):
    rows = mixed.shape[0]
    heads = near.shape[1] // HEAD
    scale = HEAD ** (-0.5)
    images[...] = image_of(ends, flips, images.shape, 0)
    for head in range(heads):
        at_q, at_k, at_v = (HEAD * (part * heads + head) for part in range(3))
        for place, out in enumerate((near, far)):

            def block(number, unused):
                start = pl.multiple_of((2 * number + place) * STEP, STEP)
                spot = pl.ds(start, STEP)
                scores = dot_t(mixed[:, at_k : at_k + HEAD], mixed[spot, at_q : at_q + HEAD])
                image = image_of(ends, flips, (1, STEP), 1, start)
                column = images[...]
                column = jnp.concatenate([column] * (STEP // HEAD), 1)
                scores = jnp.where(column == image, scores * scale, masked_score)
                highest = jnp.max(scores, axis=0, keepdims=True)
                shares = jnp.exp(scores - highest)
                total = jnp.sum(shares, axis=0, keepdims=True)
                mixture = dot_rows(mixed[:, at_v : at_v + HEAD], low(shares)) / total
                target = pl.ds(pl.multiple_of(number * STEP, STEP), STEP)
                out[target, at_q : at_q + HEAD] = low(mixture.T)
                logs[head : head + 1, spot] = highest + jnp.log(total)
                return unused

            lax.fori_loop(0, rows // STEP // 2, block, 0)


def attend_back_kernel(
    ends, flips, mixed, near, far, logs, out, key_sum, value_sum, images
):
    rows = mixed.shape[0]
    heads = near.shape[1] // HEAD
    scale = HEAD ** (-0.5)
    images[...] = image_of(ends, flips, images.shape, 0)
    for head in range(heads):
        at_q, at_k, at_v = (HEAD * (part * heads + head) for part in range(3))
        key_sum[...] = jnp.zeros_like(key_sum)
        value_sum[...] = jnp.zeros_like(value_sum)
        for place, grads in enumerate((near, far)):

            def block(number, unused):
                start = pl.multiple_of((2 * number + place) * STEP, STEP)
                spot = pl.ds(start, STEP)
                source = pl.ds(pl.multiple_of(number * STEP, STEP), STEP)
                queries = mixed[spot, at_q : at_q + HEAD]
                grad = grads[source, at_q : at_q + HEAD]
                keys = mixed[:, at_k : at_k + HEAD]
                image = image_of(ends, flips, (1, STEP), 1, start)
                column = images[...]
                column = jnp.concatenate([column] * (STEP // HEAD), 1)
                scores = dot_t(keys, queries) * scale
                shares = jnp.exp(scores - logs[head : head + 1, spot])
                shares = jnp.where(column == image, shares, 0.0)
                grad_shares = dot_t(mixed[:, at_v : at_v + HEAD], grad)
                delta = jnp.sum(shares * grad_shares, axis=0, keepdims=True)
                grad_scores = low(shares * (grad_shares - delta))
                value_sum[...] += jnp.dot(low(shares), grad, preferred_element_type=jnp.float32)
                key_sum[...] += jnp.dot(grad_scores, queries, preferred_element_type=jnp.float32)
                out[spot, at_q : at_q + HEAD] = low((dot_rows(keys, grad_scores) * scale).T)
                return unused

            lax.fori_loop(0, rows // STEP // 2, block, 0)
        out[:, at_k : at_k + HEAD] = low(key_sum[...] * scale)
        out[:, at_v : at_v + HEAD] = low(value_sum[...])


def in_smem():
    return pl.BlockSpec(memory_space=pltpu.SMEM)


def in_vmem():
    return pl.BlockSpec(memory_space=pltpu.VMEM)


def attend(ends, flips, mixed):
    rows, columns = mixed.shape
    heads = columns // (3 * HEAD)
    work = 2 * rows * rows * HEAD * heads
    half = jax.ShapeDtypeStruct((rows // 2, heads * HEAD), jnp.bfloat16)
    return pl.pallas_call(
        attend_kernel,
        in_specs=[in_smem(), in_smem(), in_vmem()],
        out_shape=(half, half, jax.ShapeDtypeStruct((heads, rows), jnp.float32)),
        scratch_shapes=[pltpu.VMEM((rows, HEAD), jnp.float32)],
        compiler_params=pltpu.CompilerParams(vmem_limit_bytes=24 << 20),
        cost_estimate=pl.CostEstimate(
            flops=2 * work, transcendentals=rows * rows * heads, bytes_accessed=4 << 20
        ),
        name="attend",
    )(ends, flips, mixed)


def attend_back(ends, flips, mixed, near, far, logs):
    rows, columns = mixed.shape
    heads = columns // (3 * HEAD)
    work = 2 * rows * rows * HEAD * heads
    return pl.pallas_call(
        attend_back_kernel,
        in_specs=[in_smem(), in_smem()] + [in_vmem()] * 4,
        out_shape=jax.ShapeDtypeStruct((rows, columns), jnp.bfloat16),
        scratch_shapes=[pltpu.VMEM((rows, HEAD), jnp.float32)] * 3,
        compiler_params=pltpu.CompilerParams(vmem_limit_bytes=32 << 20),
        cost_estimate=pl.CostEstimate(
            flops=5 * work, transcendentals=rows * rows * heads, bytes_accessed=6 << 20
        ),
        name="attend_back",
    )(ends, flips, mixed, near, far, logs)


def split_kernel(quarter, qkv, up, ids, up_vector, *refs):
    singles, outs, board = refs[:6], refs[6:10], refs[10]
    board[...] = jnp.zeros_like(board)
    for i, single in enumerate(singles):
        board[i : i + 1, :32] = wide(single[...])
    for i in range(4):
        board[6 + i : 7 + i, :32] = wide(up_vector[:, 32 * i : 32 * i + 32])
    for m in range(2):
        for i in range(3):
            below = jnp.where(ids[m : m + 1] <= i, 1.0, 0.0)
            below = jnp.sum(below, axis=1, keepdims=True)
            board[10 + 3 * m + i : 11 + 3 * m + i, :] = jnp.broadcast_to(below, (1, 128))
    extra = low(board[...].T[:32])
    for r, out in enumerate(outs):
        member = quarter[0] ^ r
        for part in range(6):
            spot = pl.ds(pl.multiple_of((4 * part + member) * HEAD, HEAD), HEAD)
            out[:, part * HEAD : (part + 1) * HEAD] = qkv[:, spot]
        out[:, 6 * HEAD : 7 * HEAD] = extra
        for part in range(8):
            block = 16 * (part >> 2) + 8 * (member >> 1) + 4 * ((part >> 1) & 1)
            block = block + 2 * (member & 1) + (part & 1)
            spot = pl.ds(pl.multiple_of(block * HEAD, HEAD), HEAD)
            out[:, (7 + part) * HEAD : (8 + part) * HEAD] = up[:, spot]


def split(quarter, qkv, up, ids, up_vector, singles):
    rows = qkv.shape[0]
    return pl.pallas_call(
        split_kernel,
        in_specs=[in_smem()] + [in_vmem()] * 10,
        out_shape=[jax.ShapeDtypeStruct((rows, 15 * HEAD), jnp.bfloat16)] * 4,
        out_specs=[in_vmem()] * 4,
        scratch_shapes=[pltpu.VMEM((128, 128), jnp.float32)],
        cost_estimate=pl.CostEstimate(flops=0, transcendentals=0, bytes_accessed=1 << 20),
        name="split",
    )(
        quarter.reshape(1),
        qkv,
        up,
        ids.reshape(2, -1),
        up_vector.reshape(1, -1),
        *(single.reshape(1, -1) for single in singles),
    )


def feed_kernel(rows, grads, w_up, w_down, bias, activ, grad_up, back, forth, sums):
    total = jnp.zeros((1, w_up.shape[1]), jnp.float32)
    for number in range(rows.shape[0] // STEP):
        spot = slice(number * STEP, (number + 1) * STEP)
        upper = dense(rows[spot], w_up[...]) + bias[...]
        share = 0.5 + 0.5 * lax.erf(upper * (0.5**0.5))
        act = low(upper * share)
        slope = share + upper * jnp.exp(-0.5 * upper * upper) * 0.3989422804014327
        grad = low(dot_t(grads[spot], w_down[...]) * slope)
        activ[spot] = act
        grad_up[spot] = grad
        total += jnp.sum(wide(grad), axis=0, keepdims=True)
        back[spot] = low(dot_t(grad, w_up[...]))
        forth[spot] = low(dense(act, w_down[...]))
    sums[...] = total


def feed(rows, grads, w_up, w_down, bias):
    count, features = rows.shape
    hidden = w_up.shape[1]
    kind = jnp.bfloat16
    return pl.pallas_call(
        feed_kernel,
        out_shape=(
            jax.ShapeDtypeStruct((count, hidden), kind),
            jax.ShapeDtypeStruct((count, hidden), kind),
            jax.ShapeDtypeStruct((count, features), kind),
            jax.ShapeDtypeStruct((count, features), kind),
            jax.ShapeDtypeStruct((1, hidden), jnp.float32),
        ),
        compiler_params=pltpu.CompilerParams(vmem_limit_bytes=40 << 20),
        cost_estimate=pl.CostEstimate(
            flops=8 * count * features * hidden,
            transcendentals=2 * count * hidden,
            bytes_accessed=8 << 20,
        ),
        name="feed",
    )(rows, grads, w_up, w_down, bias)


def team_body(
    inputs,
    segment_ids,
    cotangent,
    qkv_weight,
    out_weight,
    up_weight,
    down_weight,
    first_gain,
    first_bias,
    second_gain,
    second_bias,
    out_bias,
    up_bias,
    down_bias,
):
    batch_at, blk_at = lax.axis_index("batch"), lax.axis_index("blk")
    y, c = batch_at >> 1, batch_at & 1
    zh, z0, x = blk_at >> 2, (blk_at >> 1) & 1, blk_at & 1
    quarter = 2 * c + z0
    tokens, features = inputs.shape[2:]

    def send_rows(values):
        return [regroup(pick(values[:, 0], zh ^ flip), flip) for flip in (0, 1)]

    rows_near, rows_far = send_rows(inputs)
    singles = (first_gain, first_bias, second_gain, second_bias, out_bias, down_bias)
    own, *others = split(quarter, qkv_weight, up_weight, segment_ids, up_bias, singles)
    got = [swap(other, mask) for other, mask in zip(others, TEAM[1:])]
    w_out = grow(out_weight, 0, zh, ZH)
    rows_near, rows_far, own, *got, w_out, down_weight = tie(
        rows_near, rows_far, own, *got, w_out, down_weight
    )

    parts = ordered(ordered(own, got[0], z0, 0), ordered(got[1], got[2], z0, 0), c, 0)
    w_qkv = grow(parts[..., :896], 1, zh, ZH)
    w_up = parts[..., 896:]
    rows = wide(jnp.concatenate((rows_near, rows_far), 0))
    average = jnp.mean(rows, axis=-1, keepdims=True)
    centred = rows - average
    inverse_one = lax.rsqrt(jnp.mean(centred * centred, axis=-1, keepdims=True) + epsilon)
    scaled_one = centred * inverse_one
    sent = low(scaled_one)
    side = jnp.concatenate((sent, swap(sent, Z0)), 0)
    across = swap(side, C)
    w_qkv, down_weight = tie(w_qkv, down_weight)
    w_near = grow(w_qkv[0], 2, x, X)
    w_far = grow(w_qkv[1], 0, y, Y)
    w_near = grow(w_near, 0, y, Y)
    w_far = grow(w_far, 3, x, X)
    w_down = grow(down_weight, 0, zh, ZH)
    w_out = grow(grow(w_out, 1, z0, Z0), 0, y, Y)
    side, across, w_near, w_far, w_out, w_up, w_down, cotangent = tie(
        side, across, w_near, w_far, w_out, w_up, w_down, cotangent
    )

    w_qkv = jnp.stack((w_near, w_far), 1).reshape(features, -1)
    extra = wide(w_qkv[:, 768:]).T
    w_qkv = w_qkv[:, :768]
    gain_one, shift_one, gain_two, shift_two, bias_out, bias_down = (
        extra[i : i + 1] for i in range(6)
    )
    bias_up = extra[6:10].reshape(4, 2, 2, 2, 2, 2, 32)
    bias_up = pick(pick(bias_up, z0, 4), c, 2).transpose(1, 2, 3, 0, 4).reshape(1, -1)
    place = jnp.arange(features)
    ours = ((place >> 9) == y) & (((place >> 8) & 1) == x)
    ends = jnp.where(ours[None], lax.dynamic_slice_in_dim(extra, 10 + 3 * zh, 3, 0), 0.0)
    ends = jnp.sum(ends, 1) * (1.0 / 32.0)
    flips = jnp.stack((zh, z0, c))
    normed = low(wide(jnp.concatenate((side, across), 0)) * gain_one + shift_one)
    grad_near, grad_far = send_rows(cotangent)
    w_out = grow(w_out, 3, x, X)
    w_down = grow(w_down, 0, y, Y)
    mixed = low(dense(normed, w_qkv))
    attended, away, logs = attend(ends, flips, mixed)
    attended, away, w_out, w_up, w_down, grad_near, grad_far = tie(
        attended, away, w_out, w_up, w_down, grad_near, grad_far
    )

    tokens_two = 2 * tokens
    came = swap(away, Z0)
    out_own = pick(w_out, z0, 1).reshape(-1, features)
    out_came = pick(w_out, 1 - z0, 1).reshape(-1, features)
    grad_own = jnp.concatenate((grad_near, grad_far), 0)
    w_up = grow(w_up, 1, zh, ZH)
    w_down = grow(w_down, 2, x, X)
    came, out_own, out_came, grad_own = tie(came, out_own, out_came, grad_own)

    grad_side = jnp.concatenate((grad_own, swap(grad_own, Z0)), 0)
    far = dense(attended[tokens_two:], out_own) + dense(came[tokens_two:], out_came)
    near = dense(attended[:tokens_two], out_own) + dense(came[:tokens_two], out_came)
    middle = rows + near + wide(swap(low(far), C)) + bias_out
    middle, w_up = tie(middle, w_up)
    normed_two, scaled_two, inverse_two = norm_rows(middle, gain_two, shift_two)
    normed_two = low(normed_two)
    near = jnp.concatenate((normed_two, swap(normed_two, Z0)), 0)
    w_near = grow(w_up[0], 2, x, X)
    w_far = grow(w_up[1], 0, y, Y)
    near, grad_side = tie(near, grad_side)
    far = swap(near, C)
    grad_across = swap(grad_side, C)
    w_near = grow(w_near, 0, y, Y)
    w_far = grow(w_far, 3, x, X)
    w_up = jnp.stack((w_near, w_far), 1).reshape(features, -1)
    w_down = w_down.reshape(-1, features)
    near, far, w_down, w_up, grad_side, grad_across = tie(
        near, far, w_down, w_up, grad_side, grad_across
    )

    activ_far, upper_far, back_far, forth_far, sums_far = feed(
        far, grad_across, w_up, w_down, bias_up
    )
    activ, upper, back, forth, sums_near = feed(near, grad_side, w_up, w_down, bias_up)
    back, forth, back_far, forth_far, activ, upper = tie(
        back, forth, swap(back_far, C), swap(forth_far, C), activ, upper
    )

    count = back.shape[0] // 2
    back = wide(back) + wide(back_far)
    forth = wide(forth) + wide(forth_far)
    grad_two = back[:count] + wide(swap(low(back[count:]), Z0))
    grad_out = jnp.concatenate((grad_side, grad_across), 0)
    normed_two = jnp.concatenate((near, far), 0)
    activ = jnp.concatenate((activ, activ_far), 0)
    grad_upper = jnp.concatenate((upper, upper_far), 0)
    grad_down = low(dot_rows(activ, grad_out)).reshape(2, 2, 2, 128, features)
    grad_up = low(dot_rows(normed_two, grad_upper)).reshape(2, 2, 2, 2, 2, 32, -1)
    grad_two, grad_down, grad_up, forth = tie(grad_two, grad_down, grad_up, forth)
    grad_down = low(shrink(grad_down, 0, y, Y))
    grad_up = low(shrink(grad_up, 4, x, X))

    grad_middle = wide(grad_own) + norm_back(grad_two, scaled_two, inverse_two, gain_two)
    branch_own = low(grad_middle)
    branch_own, branch, forth = tie(branch_own, swap(branch_own, C), forth)
    branch = jnp.concatenate((branch_own, branch), 0)
    grad_came = swap(low(dot_t(branch, out_came)), Z0)
    grad_attended = low(dot_t(branch, out_own))
    grad_w_out = ordered(
        low(dot_rows(attended, branch)).reshape(2, 2, 2, 32, features),
        low(dot_rows(came, branch)).reshape(2, 2, 2, 32, features),
        z0,
        1,
    )
    grad_came, grad_down, grad_up, grad_w_out, forth = tie(
        grad_came, grad_down, grad_up, grad_w_out, forth
    )

    def give_rows(values):
        got = (regroup(values[:tokens], 0), regroup(values[tokens:], 1))
        return wide(ordered(*got, zh, 0))[:, None]

    grad_down = low(shrink(grad_down, 1, x, X))
    grad_up = low(shrink(grad_up, 0, y, Y))
    grad_mixed = attend_back(ends, flips, mixed, grad_attended, grad_came, logs)
    final = low(middle + forth[:count] + wide(swap(low(forth[count:]), Z0)) + bias_down)
    grad_mixed, grad_w_out, grad_up, grad_down, final = tie(
        grad_mixed, grad_w_out, grad_up, grad_down, final
    )

    half = 2 * tokens_two
    far = swap(low(dot_t(grad_mixed[half:], w_qkv)), C)
    back = dot_t(grad_mixed[:half], w_qkv)
    grad_qkv = low(dot_rows(normed, grad_mixed)).reshape(2, 2, 2, 2, 2, 32, -1)
    far, back, grad_qkv, grad_w_out, grad_up, grad_down, final = tie(
        far, back, grad_qkv, grad_w_out, grad_up, grad_down, final
    )
    back = back + wide(far)
    grad_one = back[:count] + wide(swap(low(back[count:]), Z0))
    qkv_near = low(shrink(low(shrink(grad_qkv[:, 0], 3, x, X)), 0, y, Y))
    qkv_far = low(shrink(low(shrink(grad_qkv[:, 1], 0, y, Y)), 2, x, X))
    grads = jnp.stack((grad_down, grad_up.transpose(1, 0, 2, 3, 4).reshape(2, 128, -1)), 1)
    grads = shrink(grads, 0, zh, ZH)
    grad_down = grads[0]
    grad_up = low(grads[1]).reshape(4, 32, -1)
    grad_w_out = low(shrink(grad_w_out, 0, y, Y))
    grad_qkv = jnp.stack((qkv_near, qkv_far), 0)
    given = low(grad_middle + norm_back(grad_one, scaled_one, inverse_one, gain_one))
    given, grad_qkv, grad_w_out, grad_up, grad_down, grad_one, final = tie(
        given, grad_qkv, grad_w_out, grad_up, grad_down, grad_one, final
    )

    input_grad = give_rows(given)
    final = give_rows(final)
    grad_qkv = low(shrink(grad_qkv, 1, zh, ZH)).reshape(4, 32, -1)
    grads = team_trade(jnp.concatenate((grad_qkv, grad_up), 2), quarter, c, z0)
    grad_qkv = grads[..., :768].reshape(4, 32, 6, 128).transpose(1, 2, 0, 3)
    grad_qkv = wide(grad_qkv.reshape(32, -1))
    grad_up = grads[..., 768:].reshape(2, 2, 32, 2, 2, 2, 128).transpose(2, 3, 0, 4, 1, 5, 6)
    grad_up = wide(grad_up.reshape(32, -1))
    grad_w_out = low(shrink(grad_w_out, 2, x, X))
    grad_w_out = shrink(low(shrink(grad_w_out, 0, zh, ZH)), 0, z0, Z0)
    sums = jnp.stack(
        (
            jnp.sum(grad_one * scaled_one, 0),
            jnp.sum(grad_one, 0),
            jnp.sum(grad_two * scaled_two, 0),
            jnp.sum(grad_two, 0),
            jnp.sum(wide(branch_own), 0),
            jnp.sum(wide(grad_own), 0),
        )
    )
    sums = sums.reshape(6, 32, 32).transpose(1, 0, 2).reshape(32, 192)
    up_sums = (sums_near + sums_far).reshape(8, 1, 128)
    up_sums = jnp.where(jnp.arange(4)[None, :, None] == quarter, up_sums, 0.0)
    up_sums = up_sums.reshape(2, 2, 2, 2, 2, 128).transpose(0, 3, 1, 4, 2, 5).reshape(32, 128)
    sums = jnp.concatenate((up_sums, sums), 1)
    sums = jnp.sum(lax.all_to_all(sums, AXES, 0, 0, tiled=True), 0)
    grad_up_bias = sums[:128]
    small = [sums[128 + 32 * i : 160 + 32 * i] for i in range(6)]
    return (
        final,
        input_grad,
        grad_qkv,
        grad_w_out,
        grad_up,
        grad_down,
        small[0],
        small[1],
        small[2],
        small[3],
        small[4],
        grad_up_bias,
        small[5],
    )


def chosen_body(mesh, *arrays):
    shape = arrays[0].shape
    sizes = (mesh.shape["batch"], mesh.shape["blk"])
    if sizes == (4, 8) and shape == (2, 1, 128, 1024) and arrays[5].shape == (32, 4096):
        return team_body(*arrays)
    return body(*arrays)


def solution(mesh):
    return jax.shard_map(
        partial(chosen_body, mesh),
        mesh=mesh,
        in_specs=(
            P(None, "batch", "blk", None),
            P(None, "batch", "blk"),
            P(None, "batch", "blk", None),
            P(("batch", "blk"), None),
            P(("batch", "blk"), None),
            P(("batch", "blk"), None),
            P(("batch", "blk"), None),
            P(("batch", "blk")),
            P(("batch", "blk")),
            P(("batch", "blk")),
            P(("batch", "blk")),
            P(("batch", "blk")),
            P(("batch", "blk")),
            P(("batch", "blk")),
        ),
        out_specs=(
            P(None, "batch", "blk", None),
            P(None, "batch", "blk", None),
            P(("batch", "blk"), None),
            P(("batch", "blk"), None),
            P(("batch", "blk"), None),
            P(("batch", "blk"), None),
            P(("batch", "blk")),
            P(("batch", "blk")),
            P(("batch", "blk")),
            P(("batch", "blk")),
            P(("batch", "blk")),
            P(("batch", "blk")),
            P(("batch", "blk")),
        ),
        check_vma=False,
    )
```

```python
from functools import partial

import jax
import jax.numpy as jnp
from jax import lax
from jax.experimental import pallas as pl
from jax.experimental.pallas import tpu as pltpu
from jax.sharding import PartitionSpec as P

H = 8


epsilon = 1e-05
masked_score = -1e30


def dense(former, latter):
    return jnp.dot(former, latter, preferred_element_type=jnp.float32)


def norm_rows(values, gains, shifts):
    average = jnp.mean(values, axis=-1, keepdims=True)
    centred = values - average
    inverse = lax.rsqrt(jnp.mean(centred * centred, axis=-1, keepdims=True) + epsilon)
    scaled = centred * inverse
    return (scaled * gains + shifts, scaled, inverse)


def norm_back(gradient, scaled, inverse, gains):
    upstream = gradient * gains
    return inverse * (
        upstream
        - jnp.mean(upstream, axis=-1, keepdims=True)
        - scaled * jnp.mean(upstream * scaled, axis=-1, keepdims=True)
    )


def block_scan(update, carried, pieces):
    amount = pieces[0].shape[1]
    stride = min(512, amount)

    def block_step(state_now, number):
        sliced = tuple(
            (lax.dynamic_slice_in_dim(member, number * stride, stride, 1) for member in pieces)
        )
        return (update(state_now, sliced), None)

    carried, unused = lax.scan(block_step, carried, jnp.arange(amount // stride))
    return carried


def split_heads(rows, head_count):
    return rows.reshape(rows.shape[0], rows.shape[1], head_count, rows.shape[2] // head_count)


def attend_piece(running, sliced, queries, query_segs):
    maximum, totals, accumulated = running
    key_part, value_part, seg_part = sliced
    head_count, head_size = (queries.shape[2], queries.shape[3])
    key_heads = split_heads(key_part, head_count)
    value_heads = split_heads(value_part, head_count)
    scores = jnp.einsum(
        "sqhd,skhd->shqk", queries, key_heads, preferred_element_type=jnp.float32
    ) * head_size ** (-0.5)
    allowed = query_segs[:, None, :, None] == seg_part[:, None, None, :]
    scores = jnp.where(allowed, scores, masked_score)
    highest = jnp.maximum(maximum, jnp.max(scores, axis=-1, keepdims=True))
    factor = jnp.exp(maximum - highest)
    shares = jnp.exp(scores - highest)
    totals = totals * factor + jnp.sum(shares, axis=-1, keepdims=True)
    accumulated = accumulated * factor + jnp.einsum(
        "shqk,skhd->shqd",
        shares.astype(jnp.bfloat16),
        value_heads,
        preferred_element_type=jnp.float32,
    )
    return (highest, totals, accumulated)


def fold_keys(running, pieces, queries, query_segs):
    return block_scan(
        partial(attend_piece, queries=queries, query_segs=query_segs), running, pieces
    )


def grad_block(queries, grad_heads, query_segs, log_total, delta, key_heads, value_heads, key_segs):
    head_size = queries.shape[3]
    scores = jnp.einsum(
        "sqhd,skhd->shqk", queries, key_heads, preferred_element_type=jnp.float32
    ) * head_size ** (-0.5)
    allowed = query_segs[:, None, :, None] == key_segs[:, None, None, :]
    shares = jnp.where(allowed, jnp.exp(scores - log_total), 0.0)
    grad_shares = jnp.einsum(
        "sqhd,skhd->shqk", grad_heads, value_heads, preferred_element_type=jnp.float32
    )
    grad_scores = (shares * (grad_shares - delta)).astype(jnp.bfloat16)
    return (shares.astype(jnp.bfloat16), grad_scores)


def micro_step(set_inputs, set_segs, set_cotangent, gathered):
    (
        weight_qkv,
        weight_out,
        weight_up,
        weight_down,
        gain_one,
        shift_one,
        gain_two,
        shift_two,
        bias_out,
        bias_up,
        bias_down,
    ) = gathered
    set_count, tok_count, features = set_inputs.shape
    head_count = H
    head_size = features // head_count
    scale = head_size ** (-0.5)
    rows = set_inputs.astype(jnp.float32).reshape(-1, features)
    normed, scaled_one, inverse_one = norm_rows(
        rows, gain_one.astype(jnp.float32), shift_one.astype(jnp.float32)
    )
    normed_low = normed.astype(jnp.bfloat16)
    mixed = dense(normed_low, weight_qkv).astype(jnp.bfloat16)
    queries = mixed[:, :features].reshape(set_count, tok_count, head_count, head_size)
    key_rows = mixed[:, features : 2 * features].reshape(set_count, tok_count, features)
    value_rows = mixed[:, 2 * features :].reshape(set_count, tok_count, features)
    running = (
        jnp.full((set_count, head_count, tok_count, 1), masked_score, jnp.float32),
        jnp.zeros((set_count, head_count, tok_count, 1), jnp.float32),
        jnp.zeros((set_count, head_count, tok_count, head_size), jnp.float32),
    )
    running = fold_keys(
        running,
        (
            lax.all_gather(key_rows, "blk", axis=1, tiled=True),
            lax.all_gather(value_rows, "blk", axis=1, tiled=True),
            lax.all_gather(set_segs, "blk", axis=1, tiled=True),
        ),
        queries=queries,
        query_segs=set_segs,
    )
    maximum, totals, accumulated = running
    attended = accumulated / totals
    log_total = maximum + jnp.log(totals)
    attended_low = jnp.transpose(attended, (0, 2, 1, 3)).reshape(-1, features).astype(jnp.bfloat16)
    middle = rows + dense(attended_low, weight_out) + bias_out.astype(jnp.float32)
    normed_two, scaled_two, inverse_two = norm_rows(
        middle, gain_two.astype(jnp.float32), shift_two.astype(jnp.float32)
    )
    normed_two_low = normed_two.astype(jnp.bfloat16)
    upper = dense(normed_two_low, weight_up) + bias_up.astype(jnp.float32)
    activ_value, gelu_back = jax.vjp(lambda v: jax.nn.gelu(v, approximate=False), upper)
    activ_low = activ_value.astype(jnp.bfloat16)
    final = middle + dense(activ_low, weight_down) + bias_down.astype(jnp.float32)
    grad_out = set_cotangent.astype(jnp.float32).reshape(-1, features)
    grad_low = grad_out.astype(jnp.bfloat16)
    grad_down_bias = jnp.sum(grad_low.astype(jnp.float32), axis=0)
    grad_down = jnp.einsum("rf,rd->fd", activ_low, grad_low, preferred_element_type=jnp.float32)
    grad_activ = jnp.einsum("rd,fd->rf", grad_low, weight_down, preferred_element_type=jnp.float32)
    grad_upper = gelu_back(grad_activ)[0].astype(jnp.bfloat16)
    grad_up_bias = jnp.sum(grad_upper.astype(jnp.float32), axis=0)
    grad_up = jnp.einsum(
        "rd,rf->df", normed_two_low, grad_upper, preferred_element_type=jnp.float32
    )
    grad_normed_two = jnp.einsum(
        "rf,df->rd", grad_upper, weight_up, preferred_element_type=jnp.float32
    )
    grad_gain_two = jnp.sum(grad_normed_two * scaled_two, axis=0)
    grad_shift_two = jnp.sum(grad_normed_two, axis=0)
    grad_middle = grad_out + norm_back(
        grad_normed_two, scaled_two, inverse_two, gain_two.astype(jnp.float32)
    )
    branch_low = grad_middle.astype(jnp.bfloat16)
    grad_out_bias = jnp.sum(branch_low.astype(jnp.float32), axis=0)
    grad_out_weight = jnp.einsum(
        "rd,re->de", attended_low, branch_low, preferred_element_type=jnp.float32
    )
    grad_attended = jnp.einsum(
        "re,de->rd", branch_low, weight_out, preferred_element_type=jnp.float32
    )
    grad_heads = grad_attended.astype(jnp.bfloat16).reshape(
        set_count, tok_count, head_count, head_size
    )
    delta = jnp.einsum("sqhd,shqd->shq", grad_heads.astype(jnp.float32), attended)[..., None]
    everything = (
        lax.all_gather(key_rows, "blk", axis=1, tiled=True),
        lax.all_gather(value_rows, "blk", axis=1, tiled=True),
        lax.all_gather(set_segs, "blk", axis=1, tiled=True),
    )
    length = everything[0].shape[1]
    stride = min(512, length)

    def key_block(grad_query, number):
        key_part = lax.dynamic_slice_in_dim(everything[0], number * stride, stride, 1)
        value_part = lax.dynamic_slice_in_dim(everything[1], number * stride, stride, 1)
        seg_part = lax.dynamic_slice_in_dim(everything[2], number * stride, stride, 1)
        key_heads = split_heads(key_part, head_count)
        share_low, score_low = grad_block(
            queries,
            grad_heads,
            set_segs,
            log_total,
            delta,
            key_heads,
            split_heads(value_part, head_count),
            seg_part,
        )
        grad_query = (
            grad_query
            + jnp.einsum(
                "shqk,skhd->sqhd", score_low, key_heads, preferred_element_type=jnp.float32
            )
            * scale
        )
        key_term = (
            jnp.einsum("shqk,sqhd->kshd", score_low, queries, preferred_element_type=jnp.float32)
            * scale
        )
        value_term = jnp.einsum(
            "shqk,sqhd->kshd", share_low, grad_heads, preferred_element_type=jnp.float32
        )
        return (
            grad_query,
            jnp.concatenate(
                (
                    key_term.reshape(stride, set_count, features),
                    value_term.reshape(stride, set_count, features),
                ),
                axis=-1,
            ),
        )

    grad_query, terms = lax.scan(
        key_block, jnp.zeros(queries.shape, jnp.float32), jnp.arange(length // stride)
    )
    summed = lax.psum_scatter(
        terms.reshape(length, set_count, 2 * features).astype(jnp.bfloat16),
        "blk",
        scatter_dimension=0,
        tiled=True,
    ).astype(jnp.float32)
    summed = jnp.transpose(summed, (1, 0, 2)).reshape(-1, 2 * features)
    grad_keys = summed[:, :features]
    grad_values = summed[:, features:]
    grad_mixed = jnp.concatenate(
        (grad_query.reshape(-1, features), grad_keys, grad_values), axis=-1
    ).astype(jnp.bfloat16)
    grad_qkv = jnp.einsum("rd,re->de", normed_low, grad_mixed, preferred_element_type=jnp.float32)
    grad_normed = jnp.einsum(
        "re,de->rd", grad_mixed, weight_qkv, preferred_element_type=jnp.float32
    )
    grad_gain_one = jnp.sum(grad_normed * scaled_one, axis=0)
    grad_shift_one = jnp.sum(grad_normed, axis=0)
    grad_input = grad_middle + norm_back(
        grad_normed, scaled_one, inverse_one, gain_one.astype(jnp.float32)
    )
    local_grads = (
        grad_qkv,
        grad_out_weight,
        grad_up,
        grad_down,
        grad_gain_one,
        grad_shift_one,
        grad_gain_two,
        grad_shift_two,
        grad_out_bias,
        grad_up_bias,
        grad_down_bias,
    )
    return (
        final.reshape(set_count, tok_count, features),
        grad_input.reshape(set_count, tok_count, features),
        local_grads,
    )


def body(
    inputs,
    segment_ids,
    cotangent,
    qkv_weight,
    out_weight,
    up_weight,
    down_weight,
    first_gain,
    first_bias,
    second_gain,
    second_bias,
    out_bias,
    up_bias,
    down_bias,
):
    shards = (
        qkv_weight,
        out_weight,
        up_weight,
        down_weight,
        first_gain,
        first_bias,
        second_gain,
        second_bias,
        out_bias,
        up_bias,
        down_bias,
    )
    shard_sums = tuple((jnp.zeros(member.shape, jnp.float32) for member in shards))
    outcomes = []
    input_grads = []
    for micro_index in range(inputs.shape[0]):
        gathered = (
            lax.all_gather(qkv_weight, ("batch", "blk"), axis=0, tiled=True),
            lax.all_gather(out_weight, ("batch", "blk"), axis=0, tiled=True),
            lax.all_gather(up_weight, ("batch", "blk"), axis=0, tiled=True),
            lax.all_gather(down_weight, ("batch", "blk"), axis=0, tiled=True),
            lax.all_gather(first_gain, ("batch", "blk"), axis=0, tiled=True),
            lax.all_gather(first_bias, ("batch", "blk"), axis=0, tiled=True),
            lax.all_gather(second_gain, ("batch", "blk"), axis=0, tiled=True),
            lax.all_gather(second_bias, ("batch", "blk"), axis=0, tiled=True),
            lax.all_gather(out_bias, ("batch", "blk"), axis=0, tiled=True),
            lax.all_gather(up_bias, ("batch", "blk"), axis=0, tiled=True),
            lax.all_gather(down_bias, ("batch", "blk"), axis=0, tiled=True),
        )
        final, grad_input, local_grads = micro_step(
            inputs[micro_index], segment_ids[micro_index], cotangent[micro_index], gathered
        )
        outcomes.append(final)
        input_grads.append(grad_input)
        summed = (
            lax.psum_scatter(local_grads[0], ("batch", "blk"), scatter_dimension=0, tiled=True),
            lax.psum_scatter(local_grads[1], ("batch", "blk"), scatter_dimension=0, tiled=True),
            lax.psum_scatter(local_grads[2], ("batch", "blk"), scatter_dimension=0, tiled=True),
            lax.psum_scatter(local_grads[3], ("batch", "blk"), scatter_dimension=0, tiled=True),
            lax.psum_scatter(local_grads[4], ("batch", "blk"), scatter_dimension=0, tiled=True),
            lax.psum_scatter(local_grads[5], ("batch", "blk"), scatter_dimension=0, tiled=True),
            lax.psum_scatter(local_grads[6], ("batch", "blk"), scatter_dimension=0, tiled=True),
            lax.psum_scatter(local_grads[7], ("batch", "blk"), scatter_dimension=0, tiled=True),
            lax.psum_scatter(local_grads[8], ("batch", "blk"), scatter_dimension=0, tiled=True),
            lax.psum_scatter(local_grads[9], ("batch", "blk"), scatter_dimension=0, tiled=True),
            lax.psum_scatter(local_grads[10], ("batch", "blk"), scatter_dimension=0, tiled=True),
        )
        shard_sums = tuple((former + latter for former, latter in zip(shard_sums, summed)))
    return (jnp.stack(outcomes), jnp.stack(input_grads)) + tuple(shard_sums)


AXES = ("batch", "blk")
Y, C, ZH, Z0, X = 16, 8, 4, 2, 1
TEAM = (0, Z0, C, C | Z0)


def swap(values, mask):
    return lax.ppermute(values, AXES, [(i, i ^ mask) for i in range(32)])


def regroup(values, flip):
    pairs = []
    for i in range(32):
        core, right = (i >> 3) & 1, i & 1
        pairs.append((i, (i & (Y | Z0)) | (right << 3) | ((i & ZH) ^ (flip << 2)) | core))
    return lax.ppermute(values, AXES, pairs)


def ordered(near, far, bit, axis):
    return jnp.stack((jnp.where(bit == 0, near, far), jnp.where(bit == 0, far, near)), axis)


def grow(values, axis, bit, mask):
    return ordered(values, swap(values, mask), bit, axis)


def pick(values, place, axis=0):
    return lax.dynamic_index_in_dim(values, place, axis, keepdims=False)


def shrink(values, axis, bit, mask):
    got = swap(pick(values, 1 - bit, axis), mask)
    return pick(values, bit, axis).astype(jnp.float32) + got.astype(jnp.float32)


def tie(*values):
    return lax.optimization_barrier(values)


def low(values):
    return values.astype(jnp.bfloat16)


def wide(values):
    return values.astype(jnp.float32)


def team_trade(parts, quarter, bit_c, bit_z):
    own = pick(parts, quarter)
    got = [swap(pick(parts, quarter ^ r), TEAM[r]) for r in (1, 2, 3)]
    return ordered(
        ordered(own, got[0], bit_z, 0), ordered(got[1], got[2], bit_z, 0), bit_c, 0
    )


def team_gather(rows):
    near = jnp.concatenate((rows, swap(rows, Z0)), 0)
    return jnp.concatenate((near, swap(near, C)), 0)


def team_scatter(near, far):
    half = near.shape[0] // 2
    near = wide(near) + wide(swap(low(far), C))
    return near[:half] + wide(swap(low(near[half:]), Z0))


def dot_t(former, latter):
    return lax.dot_general(
        former, latter, (((1,), (1,)), ((), ())), preferred_element_type=jnp.float32
    )


def dot_rows(former, latter):
    return lax.dot_general(
        former, latter, (((0,), (0,)), ((), ())), preferred_element_type=jnp.float32
    )


STEP = 256
HEAD = 128


def image_of(ends, flips, shape, axis, base=0):
    row = lax.broadcasted_iota(jnp.int32, shape, axis) + base
    block = row >> 7
    chunk = 4 * ((block & 1) ^ flips[0]) + 2 * (((block >> 1) & 1) ^ flips[1])
    chunk = chunk + ((block >> 2) ^ flips[2])
    spot = (chunk * 128 + (row & 127)).astype(jnp.float32)
    return sum(jnp.where(spot >= ends[i], 1.0, 0.0) for i in range(3))


LOG2E = 1.4426950408889634


def attend_kernel(ends, flips, mixed, near, far, logs, images):
    rows = mixed.shape[0]
    heads = near.shape[1] // HEAD
    scale = HEAD ** (-0.5) * LOG2E
    images[...] = image_of(ends, flips, images.shape, 0)

    def block(number, unused):
        start = pl.multiple_of(number * STEP, STEP)
        spot = pl.ds(start, STEP)
        target = pl.ds(pl.multiple_of((number >> 1) * STEP, STEP), STEP)
        image = image_of(ends, flips, (1, STEP), 1, start)
        column = images[...]
        same = jnp.concatenate([column] * (STEP // HEAD), 1) == image

        def one_head(head, unused):
            at_q, at_k, at_v = (
                pl.ds(pl.multiple_of((part * heads + head) * HEAD, HEAD), HEAD) for part in range(3)
            )
            scores = dot_t(mixed[:, at_k], mixed[spot, at_q])
            scores = jnp.where(same, scores * scale, masked_score)
            highest = jnp.max(scores, axis=0, keepdims=True)
            shares = jnp.exp2(scores - highest)
            total = jnp.sum(shares, axis=0, keepdims=True)
            mixture = dot_rows(mixed[:, at_v], low(shares)) / total
            mixture = low(mixture.T)
            logs[pl.ds(head, 1), spot] = highest + jnp.log2(total)

            @pl.when(number % 2 == 0)
            def _():
                near[target, at_q] = mixture

            @pl.when(number % 2 == 1)
            def _():
                far[target, at_q] = mixture

            return unused

        return lax.fori_loop(0, heads, one_head, unused)

    lax.fori_loop(0, rows // STEP, block, 0)


def attend_back_kernel(
    ends, flips, mixed, near, far, logs, out, key_sum, value_sum, images, both
):
    rows = mixed.shape[0]
    heads = near.shape[1] // HEAD
    scale = HEAD ** (-0.5)
    images[...] = image_of(ends, flips, images.shape, 0)
    key_sum[...] = jnp.zeros_like(key_sum)
    value_sum[...] = jnp.zeros_like(value_sum)
    for number in range(rows // STEP):
        source = (near, far)[number % 2]
        spot = (number // 2) * STEP
        both[number * STEP : (number + 1) * STEP] = source[spot : spot + STEP]

    def block(number, unused):
        start = pl.multiple_of(number * STEP, STEP)
        spot = pl.ds(start, STEP)
        image = image_of(ends, flips, (1, STEP), 1, start)
        column = images[...]
        same = jnp.concatenate([column] * (STEP // HEAD), 1) == image

        def one_head(head, unused):
            at_q, at_k, at_v = (
                pl.ds(pl.multiple_of((part * heads + head) * HEAD, HEAD), HEAD) for part in range(3)
            )
            queries = mixed[spot, at_q]
            grad = both[spot, at_q]
            keys = mixed[:, at_k]
            scores = dot_t(keys, queries) * (scale * LOG2E) - logs[pl.ds(head, 1), spot]
            shares = jnp.exp2(jnp.where(same, scores, masked_score))
            grad_shares = dot_t(mixed[:, at_v], grad)
            delta = jnp.sum(shares * grad_shares, axis=0, keepdims=True)
            grad_scores = low(shares * (grad_shares - delta))
            value_sum[:, at_q] += jnp.dot(low(shares), grad, preferred_element_type=jnp.float32)
            key_sum[:, at_q] += jnp.dot(grad_scores, queries, preferred_element_type=jnp.float32)
            out[spot, at_q] = low((dot_rows(keys, grad_scores) * scale).T)
            return unused

        return lax.fori_loop(0, heads, one_head, unused)

    lax.fori_loop(0, rows // STEP, block, 0)
    width = heads * HEAD
    out[:, width : 2 * width] = low(key_sum[...] * scale)
    out[:, 2 * width :] = low(value_sum[...])


def in_smem():
    return pl.BlockSpec(memory_space=pltpu.SMEM)


def in_vmem():
    return pl.BlockSpec(memory_space=pltpu.VMEM)


def attend(ends, flips, mixed):
    rows, columns = mixed.shape
    heads = columns // (3 * HEAD)
    work = 2 * rows * rows * HEAD * heads
    half = jax.ShapeDtypeStruct((rows // 2, heads * HEAD), jnp.bfloat16)
    return pl.pallas_call(
        attend_kernel,
        in_specs=[in_smem(), in_smem(), in_vmem()],
        out_shape=(half, half, jax.ShapeDtypeStruct((heads, rows), jnp.float32)),
        scratch_shapes=[pltpu.VMEM((rows, HEAD), jnp.float32)],
        compiler_params=pltpu.CompilerParams(vmem_limit_bytes=16 << 20),
        cost_estimate=pl.CostEstimate(
            flops=18 * work, transcendentals=rows * rows * heads, bytes_accessed=4 << 20
        ),
        name="attend",
    )(ends, flips, mixed)


def attend_back(ends, flips, mixed, near, far, logs):
    rows, columns = mixed.shape
    heads = columns // (3 * HEAD)
    work = 2 * rows * rows * HEAD * heads
    return pl.pallas_call(
        attend_back_kernel,
        in_specs=[in_smem(), in_smem()] + [in_vmem()] * 4,
        out_shape=jax.ShapeDtypeStruct((rows, columns), jnp.bfloat16),
        scratch_shapes=[
            pltpu.VMEM((rows, heads * HEAD), jnp.float32),
            pltpu.VMEM((rows, heads * HEAD), jnp.float32),
            pltpu.VMEM((rows, HEAD), jnp.float32),
            pltpu.VMEM((rows, heads * HEAD), jnp.bfloat16),
        ],
        compiler_params=pltpu.CompilerParams(vmem_limit_bytes=20 << 20),
        cost_estimate=pl.CostEstimate(
            flops=22 * work, transcendentals=rows * rows * heads, bytes_accessed=6 << 20
        ),
        name="attend_back",
    )(ends, flips, mixed, near, far, logs)


def split_kernel(quarter, qkv, up, ids, up_vector, *refs):
    singles, outs, board = refs[:6], refs[6:10], refs[10]
    board[...] = jnp.zeros_like(board)
    for i, single in enumerate(singles):
        board[i : i + 1, :32] = wide(single[...])
    for i in range(4):
        board[6 + i : 7 + i, :32] = wide(up_vector[:, 32 * i : 32 * i + 32])
    for m in range(2):
        for i in range(3):
            below = jnp.where(ids[m : m + 1] <= i, 1.0, 0.0)
            below = jnp.sum(below, axis=1, keepdims=True)
            board[10 + 3 * m + i : 11 + 3 * m + i, :] = jnp.broadcast_to(below, (1, 128))
    extra = low(board[...].T[:32])
    for r, out in enumerate(outs):
        member = quarter[0] ^ r
        for part in range(6):
            spot = pl.ds(pl.multiple_of((4 * part + member) * HEAD, HEAD), HEAD)
            out[:, part * HEAD : (part + 1) * HEAD] = qkv[:, spot]
        out[:, 6 * HEAD : 7 * HEAD] = extra
        for part in range(8):
            block = 16 * (part >> 2) + 8 * (member >> 1) + 4 * ((part >> 1) & 1)
            block = block + 2 * (member & 1) + (part & 1)
            spot = pl.ds(pl.multiple_of(block * HEAD, HEAD), HEAD)
            out[:, (7 + part) * HEAD : (8 + part) * HEAD] = up[:, spot]


def split(quarter, qkv, up, ids, up_vector, singles):
    rows = qkv.shape[0]
    return pl.pallas_call(
        split_kernel,
        in_specs=[in_smem()] + [in_vmem()] * 10,
        out_shape=[jax.ShapeDtypeStruct((rows, 15 * HEAD), jnp.bfloat16)] * 4,
        out_specs=[in_vmem()] * 4,
        scratch_shapes=[pltpu.VMEM((128, 128), jnp.float32)],
        cost_estimate=pl.CostEstimate(flops=0, transcendentals=0, bytes_accessed=1 << 20),
        name="split",
    )(
        quarter.reshape(1),
        qkv,
        up,
        ids.reshape(2, -1),
        up_vector.reshape(1, -1),
        *(single.reshape(1, -1) for single in singles),
    )


def join_kernel(quarter, own, got_z, got_c, got_both, qkv, up):
    for r, part_of in enumerate((own, got_z, got_c, got_both)):
        member = quarter[0] ^ r
        for part in range(6):
            spot = pl.ds(pl.multiple_of((4 * part + member) * HEAD, HEAD), HEAD)
            qkv[:, spot] = wide(part_of[:, part * HEAD : (part + 1) * HEAD])
        for part in range(8):
            block = 16 * (part >> 2) + 8 * (member >> 1) + 4 * ((part >> 1) & 1)
            block = block + 2 * (member & 1) + (part & 1)
            spot = pl.ds(pl.multiple_of(block * HEAD, HEAD), HEAD)
            up[:, spot] = wide(part_of[:, (6 + part) * HEAD : (7 + part) * HEAD])


def join(quarter, parts):
    rows = parts[0].shape[0]
    return pl.pallas_call(
        join_kernel,
        in_specs=[in_smem()] + [in_vmem()] * 4,
        out_shape=[jax.ShapeDtypeStruct((rows, n * HEAD), jnp.float32) for n in (24, 32)],
        out_specs=[in_vmem()] * 2,
        cost_estimate=pl.CostEstimate(flops=0, transcendentals=0, bytes_accessed=8 << 20),
        name="join",
    )(quarter.reshape(1), *parts)


def outer_kernel(former_near, former_far, latter_near, latter_far, out):
    def block(number, unused):
        spot = pl.ds(pl.multiple_of(number * STEP, STEP), STEP)
        total = dot_rows(former_near[:, spot], latter_near[...])
        out[spot] = low(total + dot_rows(former_far[:, spot], latter_far[...]))
        return unused

    lax.fori_loop(0, out.shape[0] // STEP, block, 0)


def outer(former_near, former_far, latter_near, latter_far):
    count, rows = former_near.shape
    columns = latter_near.shape[1]
    return pl.pallas_call(
        outer_kernel,
        out_shape=jax.ShapeDtypeStruct((rows, columns), jnp.bfloat16),
        compiler_params=pltpu.CompilerParams(vmem_limit_bytes=20 << 20),
        cost_estimate=pl.CostEstimate(
            flops=6 * count * rows * columns, transcendentals=0, bytes_accessed=6 << 20
        ),
        name="outer",
    )(former_near, former_far, latter_near, latter_far)


def feed_kernel(rows, grads, w_up, w_down, bias, activ, grad_up, back, forth, sums):
    step = rows.shape[0]
    pieces = w_up.shape[1] // STEP
    sums[...] = jnp.zeros_like(sums)

    def places(number):
        spot = pl.ds(pl.multiple_of((number // pieces) * step, step), step)
        return spot, pl.ds(pl.multiple_of((number % pieces) * STEP, STEP), STEP)

    def inner(number, unused):
        spot, unit = places(number)
        upper = dense(rows[spot], w_up[:, unit]) + bias[:, unit]
        share = 0.5 + 0.5 * lax.erf(upper * (0.5**0.5))
        activ[spot, unit] = low(upper * share)
        slope = share + upper * jnp.exp(-0.5 * upper * upper) * 0.3989422804014327
        grad = low(dot_t(grads[spot], w_down[unit]) * slope)
        grad_up[spot, unit] = grad
        sums[:, unit] += jnp.sum(wide(grad), axis=0, keepdims=True)
        return unused

    def outwards(number, unused):
        spot, unit = places(number)
        back[spot, unit] = low(dot_t(grad_up[spot], w_up[unit]))
        forth[spot, unit] = low(dense(activ[spot], w_down[:, unit]))
        return unused

    count = (rows.shape[0] // step) * pieces
    lax.fori_loop(0, count, inner, 0)
    lax.fori_loop(0, count, outwards, 0)


def feed(rows, grads, w_up, w_down, bias):
    count, features = rows.shape
    hidden = w_up.shape[1]
    kind = jnp.bfloat16
    return pl.pallas_call(
        feed_kernel,
        out_shape=(
            jax.ShapeDtypeStruct((count, hidden), kind),
            jax.ShapeDtypeStruct((count, hidden), kind),
            jax.ShapeDtypeStruct((count, features), kind),
            jax.ShapeDtypeStruct((count, features), kind),
            jax.ShapeDtypeStruct((1, hidden), jnp.float32),
        ),
        compiler_params=pltpu.CompilerParams(vmem_limit_bytes=28 << 20),
        cost_estimate=pl.CostEstimate(
            flops=11 * count * features * hidden,
            transcendentals=2 * count * hidden,
            bytes_accessed=8 << 20,
        ),
        name="feed",
    )(rows, grads, w_up, w_down, bias)


def team_body(
    inputs,
    segment_ids,
    cotangent,
    qkv_weight,
    out_weight,
    up_weight,
    down_weight,
    first_gain,
    first_bias,
    second_gain,
    second_bias,
    out_bias,
    up_bias,
    down_bias,
):
    batch_at, blk_at = lax.axis_index("batch"), lax.axis_index("blk")
    y, c = batch_at >> 1, batch_at & 1
    zh, z0, x = blk_at >> 2, (blk_at >> 1) & 1, blk_at & 1
    quarter = 2 * c + z0
    tokens, features = inputs.shape[2:]

    def send_rows(values):
        return [regroup(pick(values[:, 0], zh ^ flip), flip) for flip in (0, 1)]

    rows_near, rows_far = send_rows(inputs)
    grad_near, grad_far = send_rows(cotangent)
    singles = (first_gain, first_bias, second_gain, second_bias, out_bias, down_bias)
    own, *others = split(quarter, qkv_weight, up_weight, segment_ids, up_bias, singles)
    got = [swap(other, mask) for other, mask in zip(others, TEAM[1:])]
    w_out = grow(out_weight, 0, zh, ZH)
    own, *got, w_out, down_weight, grad_near, grad_far = tie(
        own, *got, w_out, down_weight, grad_near, grad_far
    )

    parts = ordered(ordered(own, got[0], z0, 0), ordered(got[1], got[2], z0, 0), c, 0)
    w_qkv = grow(parts[..., :896], 1, zh, ZH)
    w_up = parts[..., 896:]
    rows = wide(jnp.concatenate((rows_near, rows_far), 0))
    average = jnp.mean(rows, axis=-1, keepdims=True)
    centred = rows - average
    inverse_one = lax.rsqrt(jnp.mean(centred * centred, axis=-1, keepdims=True) + epsilon)
    scaled_one = centred * inverse_one
    sent = low(scaled_one)
    side = jnp.concatenate((sent, swap(sent, Z0)), 0)
    across = swap(side, C)
    w_qkv, down_weight = tie(w_qkv, down_weight)
    w_near = grow(w_qkv[0], 2, x, X)
    w_far = grow(w_qkv[1], 0, y, Y)
    w_near = grow(w_near, 0, y, Y)
    w_far = grow(w_far, 3, x, X)
    w_down = grow(down_weight, 0, zh, ZH)
    w_out = grow(grow(w_out, 1, z0, Z0), 0, y, Y)
    side, across, w_near, w_far, w_out, w_up, w_down, grad_near, grad_far = tie(
        side, across, w_near, w_far, w_out, w_up, w_down, grad_near, grad_far
    )

    w_qkv = jnp.stack((w_near, w_far), 1).reshape(features, -1)
    extra = wide(w_qkv[:, 768:]).T
    w_qkv = w_qkv[:, :768]
    gain_one, shift_one, gain_two, shift_two, bias_out, bias_down = (
        extra[i : i + 1] for i in range(6)
    )
    bias_up = extra[6:10].reshape(4, 2, 2, 2, 2, 2, 32)
    bias_up = pick(pick(bias_up, z0, 4), c, 2).transpose(1, 2, 3, 0, 4).reshape(1, -1)
    place = jnp.arange(features)
    ours = ((place >> 9) == y) & (((place >> 8) & 1) == x)
    ends = jnp.where(ours[None], lax.dynamic_slice_in_dim(extra, 10 + 3 * zh, 3, 0), 0.0)
    ends = jnp.sum(ends, 1) * (1.0 / 32.0)
    flips = jnp.stack((zh, z0, c))
    normed = low(wide(jnp.concatenate((side, across), 0)) * gain_one + shift_one)
    grad_own = jnp.concatenate((grad_near, grad_far), 0)
    grad_side = jnp.concatenate((grad_own, swap(grad_own, Z0)), 0)
    out_got = swap(w_out, X)
    down_near, down_far = w_down[:, :64], w_down[:, 64:]
    near_got = swap(down_near, Y)
    far_got = swap(down_far, X)
    up_got = swap(w_up, ZH)
    mixed = low(dense(normed, w_qkv))
    attended, away, logs = attend(ends, flips, mixed)
    came = swap(away, Z0)
    attended, out_got, up_got, near_got, far_got, grad_side = tie(
        attended, out_got, up_got, near_got, far_got, grad_side
    )
    w_out = ordered(w_out, out_got, x, 3)
    down_near = ordered(down_near, near_got, y, 0)
    down_far = ordered(down_far, far_got, x, 1)
    w_up = ordered(w_up, up_got, zh, 1)

    tokens_two = 2 * tokens
    out_both = jnp.concatenate(
        [pick(w_out, place, 1).reshape(-1, features) for place in (z0, 1 - z0)], 0
    )
    grad_across = swap(grad_side, C)
    w_near = grow(w_up[0], 2, x, X)
    w_far = grow(w_up[1], 0, y, Y)
    came, out_both, grad_across, down_near, down_far = tie(
        came, out_both, grad_across, down_near, down_far
    )
    down_near = grow(down_near, 2, x, X)
    down_far = grow(down_far, 0, y, Y)

    both = jnp.concatenate((attended, came), 1)
    far = dense(both[tokens_two:], out_both)
    near = dense(both[:tokens_two], out_both)
    middle = rows + near + wide(swap(low(far), C)) + bias_out
    normed_two, scaled_two, inverse_two = norm_rows(middle, gain_two, shift_two)
    normed_two = low(normed_two)
    near = jnp.concatenate((normed_two, swap(normed_two, Z0)), 0)
    far = swap(near, C)
    w_near = grow(w_near, 0, y, Y)
    w_far = grow(w_far, 3, x, X)
    w_up = jnp.stack((w_near, w_far), 1).reshape(features, -1)
    w_down = jnp.stack((down_near, down_far), 3).reshape(-1, features)
    near, far, w_down, w_up, grad_side, grad_across = tie(
        near, far, w_down, w_up, grad_side, grad_across
    )

    activ_far, upper_far, back_far, forth_far, sums_far = feed(
        far, grad_across, w_up, w_down, bias_up
    )
    activ, upper, back, forth, sums_near = feed(near, grad_side, w_up, w_down, bias_up)
    back, forth, back_far, forth_far, activ, upper = tie(
        back, forth, swap(back_far, C), swap(forth_far, C), activ, upper
    )

    count = back.shape[0] // 2
    back_own = wide(back[:count]) + wide(back_far[:count])
    back_other = low(wide(back[count:]) + wide(back_far[count:]))
    grad_two = back_own + wide(swap(back_other, Z0))
    grad_down = outer(activ, activ_far, grad_side, grad_across).reshape(2, 2, 2, 128, features)
    grad_up = outer(near, far, upper, upper_far).reshape(2, 2, 2, 2, 2, 32, -1)
    down_got = swap(pick(grad_down, 1 - y), Y)
    up_got = swap(pick(grad_up, 1 - x, 4), X)
    grad_two, grad_down, grad_up, forth, forth_far = tie(
        grad_two, grad_down, grad_up, forth, forth_far
    )

    grad_middle = wide(grad_own) + norm_back(grad_two, scaled_two, inverse_two, gain_two)
    branch_own = low(grad_middle)
    branch_own, branch, forth, forth_far = tie(
        branch_own, swap(branch_own, C), forth, forth_far
    )
    branch = jnp.concatenate((branch_own, branch), 0)
    grad_both = low(dot_t(branch, out_both))
    width = attended.shape[1]
    grad_attended = grad_both[:, :width]
    grad_came = swap(grad_both[:, width:], Z0)
    grad_w_out = low(dot_rows(both, branch)).reshape(2, 2, 2, 2, 32, features)
    grad_w_out = ordered(grad_w_out[0], grad_w_out[1], z0, 1)
    forth_own = wide(forth[:count]) + wide(forth_far[:count])
    forth_other = low(wide(forth[count:]) + wide(forth_far[count:]))
    final = low(middle + forth_own + wide(swap(forth_other, Z0)) + bias_down)
    grad_came, down_got, up_got, grad_w_out, final = tie(
        grad_came, down_got, up_got, grad_w_out, final
    )
    grad_down = low(wide(pick(grad_down, y)) + wide(down_got))
    grad_up = low(wide(pick(grad_up, x, 4)) + wide(up_got))

    def give_rows(values):
        got = (regroup(values[:tokens], 0), regroup(values[tokens:], 1))
        return wide(ordered(*got, zh, 0))[:, None]

    grad_down = low(shrink(grad_down, 1, x, X))
    grad_up = low(shrink(grad_up, 0, y, Y))
    grad_mixed = attend_back(ends, flips, mixed, grad_attended, grad_came, logs)
    final = give_rows(final)
    grad_w_out = low(shrink(grad_w_out, 0, y, Y))
    grad_mixed, grad_up, grad_down, final = tie(grad_mixed, grad_up, grad_down, final)

    half = 2 * tokens_two
    far = swap(low(dot_t(grad_mixed[half:], w_qkv)), C)
    back = dot_t(grad_mixed[:half], w_qkv)
    grad_qkv = low(dot_rows(normed, grad_mixed)).reshape(2, 2, 2, 2, 2, 32, -1)
    far, back, grad_qkv, grad_w_out, grad_up, grad_down = tie(
        far, back, grad_qkv, grad_w_out, grad_up, grad_down
    )
    back = back + wide(far)
    grad_one = back[:count] + wide(swap(low(back[count:]), Z0))
    qkv_near = low(shrink(low(shrink(grad_qkv[:, 0], 3, x, X)), 0, y, Y))
    qkv_far = low(shrink(low(shrink(grad_qkv[:, 1], 0, y, Y)), 2, x, X))
    grads = jnp.stack((grad_down, grad_up.transpose(1, 0, 2, 3, 4).reshape(2, 128, -1)), 1)
    grads = shrink(grads, 0, zh, ZH)
    grad_down = grads[0]
    grad_up = low(grads[1]).reshape(4, 32, -1)
    grad_w_out = low(shrink(grad_w_out, 2, x, X))
    grad_qkv = jnp.stack((qkv_near, qkv_far), 0)
    given = low(grad_middle + norm_back(grad_one, scaled_one, inverse_one, gain_one))
    given, grad_qkv, grad_w_out, grad_up, grad_down, grad_one = tie(
        given, grad_qkv, grad_w_out, grad_up, grad_down, grad_one
    )

    input_grad = give_rows(given)
    qkv_got = swap(pick(grad_qkv, 1 - zh, 1), ZH)
    out_got = swap(pick(grad_w_out, 1 - zh), ZH)
    qkv_got, out_got, grad_one = tie(qkv_got, out_got, grad_one)
    grad_qkv = low(wide(pick(grad_qkv, zh, 1)) + wide(qkv_got)).reshape(4, 32, -1)
    grad_w_out = wide(pick(grad_w_out, zh)) + wide(out_got)
    parts = jnp.concatenate((grad_qkv, grad_up), 2)
    parts = [pick(parts, quarter ^ r) for r in range(4)]
    parts[1] = jnp.concatenate((parts[1], low(pick(grad_w_out, 1 - z0))), 1)
    parts = parts[:1] + [swap(part, mask) for part, mask in zip(parts[1:], TEAM[1:])]
    grad_w_out = pick(grad_w_out, z0) + wide(parts[1][:, 1792:])
    grad_qkv, grad_up = join(quarter, parts)
    sums = jnp.stack(
        (
            jnp.sum(grad_one * scaled_one, 0),
            jnp.sum(grad_one, 0),
            jnp.sum(grad_two * scaled_two, 0),
            jnp.sum(grad_two, 0),
            jnp.sum(wide(branch_own), 0),
            jnp.sum(wide(grad_own), 0),
        )
    )
    sums = sums.reshape(6, 32, 32).transpose(1, 0, 2).reshape(32, 192)
    up_sums = (sums_near + sums_far).reshape(8, 1, 128)
    up_sums = jnp.where(jnp.arange(4)[None, :, None] == quarter, up_sums, 0.0)
    up_sums = up_sums.reshape(2, 2, 2, 2, 2, 128).transpose(0, 3, 1, 4, 2, 5).reshape(32, 128)
    sums = jnp.concatenate((up_sums, sums), 1)
    sums = jnp.sum(lax.all_to_all(sums, AXES, 0, 0, tiled=True), 0)
    grad_up_bias = sums[:128]
    small = [sums[128 + 32 * i : 160 + 32 * i] for i in range(6)]
    return (
        final,
        input_grad,
        grad_qkv,
        grad_w_out,
        grad_up,
        grad_down,
        small[0],
        small[1],
        small[2],
        small[3],
        small[4],
        grad_up_bias,
        small[5],
    )


def chosen_body(mesh, *arrays):
    shape = arrays[0].shape
    sizes = (mesh.shape["batch"], mesh.shape["blk"])
    if sizes == (4, 8) and shape == (2, 1, 128, 1024) and arrays[5].shape == (32, 4096):
        return team_body(*arrays)
    return body(*arrays)


def solution(mesh):
    return jax.shard_map(
        partial(chosen_body, mesh),
        mesh=mesh,
        in_specs=(
            P(None, "batch", "blk", None),
            P(None, "batch", "blk"),
            P(None, "batch", "blk", None),
            P(("batch", "blk"), None),
            P(("batch", "blk"), None),
            P(("batch", "blk"), None),
            P(("batch", "blk"), None),
            P(("batch", "blk")),
            P(("batch", "blk")),
            P(("batch", "blk")),
            P(("batch", "blk")),
            P(("batch", "blk")),
            P(("batch", "blk")),
            P(("batch", "blk")),
        ),
        out_specs=(
            P(None, "batch", "blk", None),
            P(None, "batch", "blk", None),
            P(("batch", "blk"), None),
            P(("batch", "blk"), None),
            P(("batch", "blk"), None),
            P(("batch", "blk"), None),
            P(("batch", "blk")),
            P(("batch", "blk")),
            P(("batch", "blk")),
            P(("batch", "blk")),
            P(("batch", "blk")),
            P(("batch", "blk")),
            P(("batch", "blk")),
        ),
        check_vma=False,
    )
```

```python
from functools import partial

import jax
import jax.numpy as jnp
from jax import lax
from jax.experimental import pallas as pl
from jax.experimental.pallas import tpu as pltpu
from jax.sharding import PartitionSpec as P

H = 8


epsilon = 1e-05
masked_score = -1e30


def dense(former, latter):
    return jnp.dot(former, latter, preferred_element_type=jnp.float32)


def norm_rows(values, gains, shifts):
    average = jnp.mean(values, axis=-1, keepdims=True)
    centred = values - average
    inverse = lax.rsqrt(jnp.mean(centred * centred, axis=-1, keepdims=True) + epsilon)
    scaled = centred * inverse
    return (scaled * gains + shifts, scaled, inverse)


def norm_back(gradient, scaled, inverse, gains):
    upstream = gradient * gains
    return inverse * (
        upstream
        - jnp.mean(upstream, axis=-1, keepdims=True)
        - scaled * jnp.mean(upstream * scaled, axis=-1, keepdims=True)
    )


def block_scan(update, carried, pieces):
    amount = pieces[0].shape[1]
    stride = min(512, amount)

    def block_step(state_now, number):
        sliced = tuple(
            (lax.dynamic_slice_in_dim(member, number * stride, stride, 1) for member in pieces)
        )
        return (update(state_now, sliced), None)

    carried, unused = lax.scan(block_step, carried, jnp.arange(amount // stride))
    return carried


def split_heads(rows, head_count):
    return rows.reshape(rows.shape[0], rows.shape[1], head_count, rows.shape[2] // head_count)


def attend_piece(running, sliced, queries, query_segs):
    maximum, totals, accumulated = running
    key_part, value_part, seg_part = sliced
    head_count, head_size = (queries.shape[2], queries.shape[3])
    key_heads = split_heads(key_part, head_count)
    value_heads = split_heads(value_part, head_count)
    scores = jnp.einsum(
        "sqhd,skhd->shqk", queries, key_heads, preferred_element_type=jnp.float32
    ) * head_size ** (-0.5)
    allowed = query_segs[:, None, :, None] == seg_part[:, None, None, :]
    scores = jnp.where(allowed, scores, masked_score)
    highest = jnp.maximum(maximum, jnp.max(scores, axis=-1, keepdims=True))
    factor = jnp.exp(maximum - highest)
    shares = jnp.exp(scores - highest)
    totals = totals * factor + jnp.sum(shares, axis=-1, keepdims=True)
    accumulated = accumulated * factor + jnp.einsum(
        "shqk,skhd->shqd",
        shares.astype(jnp.bfloat16),
        value_heads,
        preferred_element_type=jnp.float32,
    )
    return (highest, totals, accumulated)


def fold_keys(running, pieces, queries, query_segs):
    return block_scan(
        partial(attend_piece, queries=queries, query_segs=query_segs), running, pieces
    )


def grad_block(queries, grad_heads, query_segs, log_total, delta, key_heads, value_heads, key_segs):
    head_size = queries.shape[3]
    scores = jnp.einsum(
        "sqhd,skhd->shqk", queries, key_heads, preferred_element_type=jnp.float32
    ) * head_size ** (-0.5)
    allowed = query_segs[:, None, :, None] == key_segs[:, None, None, :]
    shares = jnp.where(allowed, jnp.exp(scores - log_total), 0.0)
    grad_shares = jnp.einsum(
        "sqhd,skhd->shqk", grad_heads, value_heads, preferred_element_type=jnp.float32
    )
    grad_scores = (shares * (grad_shares - delta)).astype(jnp.bfloat16)
    return (shares.astype(jnp.bfloat16), grad_scores)


def micro_step(set_inputs, set_segs, set_cotangent, gathered):
    (
        weight_qkv,
        weight_out,
        weight_up,
        weight_down,
        gain_one,
        shift_one,
        gain_two,
        shift_two,
        bias_out,
        bias_up,
        bias_down,
    ) = gathered
    set_count, tok_count, features = set_inputs.shape
    head_count = H
    head_size = features // head_count
    scale = head_size ** (-0.5)
    rows = set_inputs.astype(jnp.float32).reshape(-1, features)
    normed, scaled_one, inverse_one = norm_rows(
        rows, gain_one.astype(jnp.float32), shift_one.astype(jnp.float32)
    )
    normed_low = normed.astype(jnp.bfloat16)
    mixed = dense(normed_low, weight_qkv).astype(jnp.bfloat16)
    queries = mixed[:, :features].reshape(set_count, tok_count, head_count, head_size)
    key_rows = mixed[:, features : 2 * features].reshape(set_count, tok_count, features)
    value_rows = mixed[:, 2 * features :].reshape(set_count, tok_count, features)
    running = (
        jnp.full((set_count, head_count, tok_count, 1), masked_score, jnp.float32),
        jnp.zeros((set_count, head_count, tok_count, 1), jnp.float32),
        jnp.zeros((set_count, head_count, tok_count, head_size), jnp.float32),
    )
    running = fold_keys(
        running,
        (
            lax.all_gather(key_rows, "blk", axis=1, tiled=True),
            lax.all_gather(value_rows, "blk", axis=1, tiled=True),
            lax.all_gather(set_segs, "blk", axis=1, tiled=True),
        ),
        queries=queries,
        query_segs=set_segs,
    )
    maximum, totals, accumulated = running
    attended = accumulated / totals
    log_total = maximum + jnp.log(totals)
    attended_low = jnp.transpose(attended, (0, 2, 1, 3)).reshape(-1, features).astype(jnp.bfloat16)
    middle = rows + dense(attended_low, weight_out) + bias_out.astype(jnp.float32)
    normed_two, scaled_two, inverse_two = norm_rows(
        middle, gain_two.astype(jnp.float32), shift_two.astype(jnp.float32)
    )
    normed_two_low = normed_two.astype(jnp.bfloat16)
    upper = dense(normed_two_low, weight_up) + bias_up.astype(jnp.float32)
    activ_value, gelu_back = jax.vjp(lambda v: jax.nn.gelu(v, approximate=False), upper)
    activ_low = activ_value.astype(jnp.bfloat16)
    final = middle + dense(activ_low, weight_down) + bias_down.astype(jnp.float32)
    grad_out = set_cotangent.astype(jnp.float32).reshape(-1, features)
    grad_low = grad_out.astype(jnp.bfloat16)
    grad_down_bias = jnp.sum(grad_low.astype(jnp.float32), axis=0)
    grad_down = jnp.einsum("rf,rd->fd", activ_low, grad_low, preferred_element_type=jnp.float32)
    grad_activ = jnp.einsum("rd,fd->rf", grad_low, weight_down, preferred_element_type=jnp.float32)
    grad_upper = gelu_back(grad_activ)[0].astype(jnp.bfloat16)
    grad_up_bias = jnp.sum(grad_upper.astype(jnp.float32), axis=0)
    grad_up = jnp.einsum(
        "rd,rf->df", normed_two_low, grad_upper, preferred_element_type=jnp.float32
    )
    grad_normed_two = jnp.einsum(
        "rf,df->rd", grad_upper, weight_up, preferred_element_type=jnp.float32
    )
    grad_gain_two = jnp.sum(grad_normed_two * scaled_two, axis=0)
    grad_shift_two = jnp.sum(grad_normed_two, axis=0)
    grad_middle = grad_out + norm_back(
        grad_normed_two, scaled_two, inverse_two, gain_two.astype(jnp.float32)
    )
    branch_low = grad_middle.astype(jnp.bfloat16)
    grad_out_bias = jnp.sum(branch_low.astype(jnp.float32), axis=0)
    grad_out_weight = jnp.einsum(
        "rd,re->de", attended_low, branch_low, preferred_element_type=jnp.float32
    )
    grad_attended = jnp.einsum(
        "re,de->rd", branch_low, weight_out, preferred_element_type=jnp.float32
    )
    grad_heads = grad_attended.astype(jnp.bfloat16).reshape(
        set_count, tok_count, head_count, head_size
    )
    delta = jnp.einsum("sqhd,shqd->shq", grad_heads.astype(jnp.float32), attended)[..., None]
    everything = (
        lax.all_gather(key_rows, "blk", axis=1, tiled=True),
        lax.all_gather(value_rows, "blk", axis=1, tiled=True),
        lax.all_gather(set_segs, "blk", axis=1, tiled=True),
    )
    length = everything[0].shape[1]
    stride = min(512, length)

    def key_block(grad_query, number):
        key_part = lax.dynamic_slice_in_dim(everything[0], number * stride, stride, 1)
        value_part = lax.dynamic_slice_in_dim(everything[1], number * stride, stride, 1)
        seg_part = lax.dynamic_slice_in_dim(everything[2], number * stride, stride, 1)
        key_heads = split_heads(key_part, head_count)
        share_low, score_low = grad_block(
            queries,
            grad_heads,
            set_segs,
            log_total,
            delta,
            key_heads,
            split_heads(value_part, head_count),
            seg_part,
        )
        grad_query = (
            grad_query
            + jnp.einsum(
                "shqk,skhd->sqhd", score_low, key_heads, preferred_element_type=jnp.float32
            )
            * scale
        )
        key_term = (
            jnp.einsum("shqk,sqhd->kshd", score_low, queries, preferred_element_type=jnp.float32)
            * scale
        )
        value_term = jnp.einsum(
            "shqk,sqhd->kshd", share_low, grad_heads, preferred_element_type=jnp.float32
        )
        return (
            grad_query,
            jnp.concatenate(
                (
                    key_term.reshape(stride, set_count, features),
                    value_term.reshape(stride, set_count, features),
                ),
                axis=-1,
            ),
        )

    grad_query, terms = lax.scan(
        key_block, jnp.zeros(queries.shape, jnp.float32), jnp.arange(length // stride)
    )
    summed = lax.psum_scatter(
        terms.reshape(length, set_count, 2 * features).astype(jnp.bfloat16),
        "blk",
        scatter_dimension=0,
        tiled=True,
    ).astype(jnp.float32)
    summed = jnp.transpose(summed, (1, 0, 2)).reshape(-1, 2 * features)
    grad_keys = summed[:, :features]
    grad_values = summed[:, features:]
    grad_mixed = jnp.concatenate(
        (grad_query.reshape(-1, features), grad_keys, grad_values), axis=-1
    ).astype(jnp.bfloat16)
    grad_qkv = jnp.einsum("rd,re->de", normed_low, grad_mixed, preferred_element_type=jnp.float32)
    grad_normed = jnp.einsum(
        "re,de->rd", grad_mixed, weight_qkv, preferred_element_type=jnp.float32
    )
    grad_gain_one = jnp.sum(grad_normed * scaled_one, axis=0)
    grad_shift_one = jnp.sum(grad_normed, axis=0)
    grad_input = grad_middle + norm_back(
        grad_normed, scaled_one, inverse_one, gain_one.astype(jnp.float32)
    )
    local_grads = (
        grad_qkv,
        grad_out_weight,
        grad_up,
        grad_down,
        grad_gain_one,
        grad_shift_one,
        grad_gain_two,
        grad_shift_two,
        grad_out_bias,
        grad_up_bias,
        grad_down_bias,
    )
    return (
        final.reshape(set_count, tok_count, features),
        grad_input.reshape(set_count, tok_count, features),
        local_grads,
    )


def body(
    inputs,
    segment_ids,
    cotangent,
    qkv_weight,
    out_weight,
    up_weight,
    down_weight,
    first_gain,
    first_bias,
    second_gain,
    second_bias,
    out_bias,
    up_bias,
    down_bias,
):
    shards = (
        qkv_weight,
        out_weight,
        up_weight,
        down_weight,
        first_gain,
        first_bias,
        second_gain,
        second_bias,
        out_bias,
        up_bias,
        down_bias,
    )
    shard_sums = tuple((jnp.zeros(member.shape, jnp.float32) for member in shards))
    outcomes = []
    input_grads = []
    for micro_index in range(inputs.shape[0]):
        gathered = (
            lax.all_gather(qkv_weight, ("batch", "blk"), axis=0, tiled=True),
            lax.all_gather(out_weight, ("batch", "blk"), axis=0, tiled=True),
            lax.all_gather(up_weight, ("batch", "blk"), axis=0, tiled=True),
            lax.all_gather(down_weight, ("batch", "blk"), axis=0, tiled=True),
            lax.all_gather(first_gain, ("batch", "blk"), axis=0, tiled=True),
            lax.all_gather(first_bias, ("batch", "blk"), axis=0, tiled=True),
            lax.all_gather(second_gain, ("batch", "blk"), axis=0, tiled=True),
            lax.all_gather(second_bias, ("batch", "blk"), axis=0, tiled=True),
            lax.all_gather(out_bias, ("batch", "blk"), axis=0, tiled=True),
            lax.all_gather(up_bias, ("batch", "blk"), axis=0, tiled=True),
            lax.all_gather(down_bias, ("batch", "blk"), axis=0, tiled=True),
        )
        final, grad_input, local_grads = micro_step(
            inputs[micro_index], segment_ids[micro_index], cotangent[micro_index], gathered
        )
        outcomes.append(final)
        input_grads.append(grad_input)
        summed = (
            lax.psum_scatter(local_grads[0], ("batch", "blk"), scatter_dimension=0, tiled=True),
            lax.psum_scatter(local_grads[1], ("batch", "blk"), scatter_dimension=0, tiled=True),
            lax.psum_scatter(local_grads[2], ("batch", "blk"), scatter_dimension=0, tiled=True),
            lax.psum_scatter(local_grads[3], ("batch", "blk"), scatter_dimension=0, tiled=True),
            lax.psum_scatter(local_grads[4], ("batch", "blk"), scatter_dimension=0, tiled=True),
            lax.psum_scatter(local_grads[5], ("batch", "blk"), scatter_dimension=0, tiled=True),
            lax.psum_scatter(local_grads[6], ("batch", "blk"), scatter_dimension=0, tiled=True),
            lax.psum_scatter(local_grads[7], ("batch", "blk"), scatter_dimension=0, tiled=True),
            lax.psum_scatter(local_grads[8], ("batch", "blk"), scatter_dimension=0, tiled=True),
            lax.psum_scatter(local_grads[9], ("batch", "blk"), scatter_dimension=0, tiled=True),
            lax.psum_scatter(local_grads[10], ("batch", "blk"), scatter_dimension=0, tiled=True),
        )
        shard_sums = tuple((former + latter for former, latter in zip(shard_sums, summed)))
    return (jnp.stack(outcomes), jnp.stack(input_grads)) + tuple(shard_sums)


AXES = ("batch", "blk")
Y, C, ZH, Z0, X = 16, 8, 4, 2, 1
TEAM = (0, Z0, C, C | Z0)


def swap(values, mask):
    return lax.ppermute(values, AXES, [(i, i ^ mask) for i in range(32)])


def regroup(values, flip):
    pairs = []
    for i in range(32):
        core, right = (i >> 3) & 1, i & 1
        pairs.append((i, (i & (Y | Z0)) | (right << 3) | ((i & ZH) ^ (flip << 2)) | core))
    return lax.ppermute(values, AXES, pairs)


def ordered(near, far, bit, axis):
    return jnp.stack((jnp.where(bit == 0, near, far), jnp.where(bit == 0, far, near)), axis)


def grow(values, axis, bit, mask):
    return ordered(values, swap(values, mask), bit, axis)


def pick(values, place, axis=0):
    return lax.dynamic_index_in_dim(values, place, axis, keepdims=False)


def shrink(values, axis, bit, mask):
    got = swap(pick(values, 1 - bit, axis), mask)
    return pick(values, bit, axis).astype(jnp.float32) + got.astype(jnp.float32)


def tie(*values):
    return lax.optimization_barrier(values)


def low(values):
    return values.astype(jnp.bfloat16)


def wide(values):
    return values.astype(jnp.float32)


def team_trade(parts, quarter, bit_c, bit_z):
    own = pick(parts, quarter)
    got = [swap(pick(parts, quarter ^ r), TEAM[r]) for r in (1, 2, 3)]
    return ordered(
        ordered(own, got[0], bit_z, 0), ordered(got[1], got[2], bit_z, 0), bit_c, 0
    )


def team_gather(rows):
    near = jnp.concatenate((rows, swap(rows, Z0)), 0)
    return jnp.concatenate((near, swap(near, C)), 0)


def team_scatter(near, far):
    half = near.shape[0] // 2
    near = wide(near) + wide(swap(low(far), C))
    return near[:half] + wide(swap(low(near[half:]), Z0))


def dot_t(former, latter):
    return lax.dot_general(
        former, latter, (((1,), (1,)), ((), ())), preferred_element_type=jnp.float32
    )


def dot_rows(former, latter):
    return lax.dot_general(
        former, latter, (((0,), (0,)), ((), ())), preferred_element_type=jnp.float32
    )


STEP = 256
HEAD = 128


def image_of(ends, flips, shape, axis, base=0):
    row = lax.broadcasted_iota(jnp.int32, shape, axis) + base
    block = row >> 7
    chunk = 4 * ((block & 1) ^ flips[0]) + 2 * (((block >> 1) & 1) ^ flips[1])
    chunk = chunk + ((block >> 2) ^ flips[2])
    spot = (chunk * 128 + (row & 127)).astype(jnp.float32)
    return sum(jnp.where(spot >= ends[i], 1.0, 0.0) for i in range(3))


LOG2E = 1.4426950408889634


def attend_kernel(ends, flips, mixed, near, far, logs, images):
    rows = mixed.shape[0]
    heads = near.shape[1] // HEAD
    scale = HEAD ** (-0.5) * LOG2E
    images[...] = image_of(ends, flips, images.shape, 0)

    def block(number, unused):
        start = pl.multiple_of(number * STEP, STEP)
        spot = pl.ds(start, STEP)
        target = pl.ds(pl.multiple_of((number >> 1) * STEP, STEP), STEP)
        image = image_of(ends, flips, (1, STEP), 1, start)
        column = images[...]
        same = jnp.concatenate([column] * (STEP // HEAD), 1) == image

        def one_head(head, unused):
            at_q, at_k, at_v = (
                pl.ds(pl.multiple_of((part * heads + head) * HEAD, HEAD), HEAD) for part in range(3)
            )
            scores = dot_t(mixed[:, at_k], mixed[spot, at_q])
            scores = jnp.where(same, scores * scale, masked_score)
            highest = jnp.max(scores, axis=0, keepdims=True)
            shares = jnp.exp2(scores - highest)
            total = jnp.sum(shares, axis=0, keepdims=True)
            mixture = dot_rows(mixed[:, at_v], low(shares)) / total
            mixture = low(mixture.T)
            logs[pl.ds(head, 1), spot] = highest + jnp.log2(total)

            @pl.when(number % 2 == 0)
            def _():
                near[target, at_q] = mixture

            @pl.when(number % 2 == 1)
            def _():
                far[target, at_q] = mixture

            return unused

        return lax.fori_loop(0, heads, one_head, unused)

    lax.fori_loop(0, rows // STEP, block, 0)


def attend_back_kernel(
    ends, flips, mixed, near, far, logs, out, key_sum, value_sum, images, both
):
    rows = mixed.shape[0]
    heads = near.shape[1] // HEAD
    scale = HEAD ** (-0.5)
    images[...] = image_of(ends, flips, images.shape, 0)
    key_sum[...] = jnp.zeros_like(key_sum)
    value_sum[...] = jnp.zeros_like(value_sum)
    for number in range(rows // STEP):
        source = (near, far)[number % 2]
        spot = (number // 2) * STEP
        both[number * STEP : (number + 1) * STEP] = source[spot : spot + STEP]

    def block(number, unused):
        start = pl.multiple_of(number * STEP, STEP)
        spot = pl.ds(start, STEP)
        image = image_of(ends, flips, (1, STEP), 1, start)
        column = images[...]
        same = jnp.concatenate([column] * (STEP // HEAD), 1) == image

        def one_head(head, unused):
            at_q, at_k, at_v = (
                pl.ds(pl.multiple_of((part * heads + head) * HEAD, HEAD), HEAD) for part in range(3)
            )
            queries = mixed[spot, at_q]
            grad = both[spot, at_q]
            keys = mixed[:, at_k]
            scores = dot_t(keys, queries) * (scale * LOG2E) - logs[pl.ds(head, 1), spot]
            shares = jnp.exp2(jnp.where(same, scores, masked_score))
            grad_shares = dot_t(mixed[:, at_v], grad)
            delta = jnp.sum(shares * grad_shares, axis=0, keepdims=True)
            grad_scores = low(shares * (grad_shares - delta))
            value_sum[:, at_q] += jnp.dot(low(shares), grad, preferred_element_type=jnp.float32)
            key_sum[:, at_q] += jnp.dot(grad_scores, queries, preferred_element_type=jnp.float32)
            out[spot, at_q] = low((dot_rows(keys, grad_scores) * scale).T)
            return unused

        return lax.fori_loop(0, heads, one_head, unused)

    lax.fori_loop(0, rows // STEP, block, 0)
    width = heads * HEAD
    out[:, width : 2 * width] = low(key_sum[...] * scale)
    out[:, 2 * width :] = low(value_sum[...])


def in_smem():
    return pl.BlockSpec(memory_space=pltpu.SMEM)


def in_vmem():
    return pl.BlockSpec(memory_space=pltpu.VMEM)


def attend(ends, flips, mixed):
    rows, columns = mixed.shape
    heads = columns // (3 * HEAD)
    work = 2 * rows * rows * HEAD * heads
    half = jax.ShapeDtypeStruct((rows // 2, heads * HEAD), jnp.bfloat16)
    return pl.pallas_call(
        attend_kernel,
        in_specs=[in_smem(), in_smem(), in_vmem()],
        out_shape=(half, half, jax.ShapeDtypeStruct((heads, rows), jnp.float32)),
        scratch_shapes=[pltpu.VMEM((rows, HEAD), jnp.float32)],
        compiler_params=pltpu.CompilerParams(vmem_limit_bytes=16 << 20),
        cost_estimate=pl.CostEstimate(
            flops=18 * work, transcendentals=rows * rows * heads, bytes_accessed=4 << 20
        ),
        name="attend",
    )(ends, flips, mixed)


def attend_back(ends, flips, mixed, near, far, logs):
    rows, columns = mixed.shape
    heads = columns // (3 * HEAD)
    work = 2 * rows * rows * HEAD * heads
    return pl.pallas_call(
        attend_back_kernel,
        in_specs=[in_smem(), in_smem()] + [in_vmem()] * 4,
        out_shape=jax.ShapeDtypeStruct((rows, columns), jnp.bfloat16),
        scratch_shapes=[
            pltpu.VMEM((rows, heads * HEAD), jnp.float32),
            pltpu.VMEM((rows, heads * HEAD), jnp.float32),
            pltpu.VMEM((rows, HEAD), jnp.float32),
            pltpu.VMEM((rows, heads * HEAD), jnp.bfloat16),
        ],
        compiler_params=pltpu.CompilerParams(vmem_limit_bytes=20 << 20),
        cost_estimate=pl.CostEstimate(
            flops=22 * work, transcendentals=rows * rows * heads, bytes_accessed=6 << 20
        ),
        name="attend_back",
    )(ends, flips, mixed, near, far, logs)


def split_kernel(quarter, qkv, up, ids, up_vector, *refs):
    singles, outs, board = refs[:6], refs[6:10], refs[10]
    board[...] = jnp.zeros_like(board)
    for i, single in enumerate(singles):
        board[i : i + 1, :32] = wide(single[...])
    for i in range(4):
        board[6 + i : 7 + i, :32] = wide(up_vector[:, 32 * i : 32 * i + 32])
    for m in range(2):
        for i in range(3):
            below = jnp.where(ids[m : m + 1] <= i, 1.0, 0.0)
            below = jnp.sum(below, axis=1, keepdims=True)
            board[10 + 3 * m + i : 11 + 3 * m + i, :] = jnp.broadcast_to(below, (1, 128))
    extra = low(board[...].T[:32])
    for r, out in enumerate(outs):
        member = quarter[0] ^ r
        for part in range(6):
            spot = pl.ds(pl.multiple_of((4 * part + member) * HEAD, HEAD), HEAD)
            out[:, part * HEAD : (part + 1) * HEAD] = qkv[:, spot]
        out[:, 6 * HEAD : 7 * HEAD] = extra
        for part in range(8):
            block = 16 * (part >> 2) + 8 * (member >> 1) + 4 * ((part >> 1) & 1)
            block = block + 2 * (member & 1) + (part & 1)
            spot = pl.ds(pl.multiple_of(block * HEAD, HEAD), HEAD)
            out[:, (7 + part) * HEAD : (8 + part) * HEAD] = up[:, spot]


def split(quarter, qkv, up, ids, up_vector, singles):
    rows = qkv.shape[0]
    return pl.pallas_call(
        split_kernel,
        in_specs=[in_smem()] + [in_vmem()] * 10,
        out_shape=[jax.ShapeDtypeStruct((rows, 15 * HEAD), jnp.bfloat16)] * 4,
        out_specs=[in_vmem()] * 4,
        scratch_shapes=[pltpu.VMEM((128, 128), jnp.float32)],
        cost_estimate=pl.CostEstimate(flops=0, transcendentals=0, bytes_accessed=1 << 20),
        name="split",
    )(
        quarter.reshape(1),
        qkv,
        up,
        ids.reshape(2, -1),
        up_vector.reshape(1, -1),
        *(single.reshape(1, -1) for single in singles),
    )


def join_kernel(quarter, own, got_z, got_c, got_both, qkv, up):
    for r, part_of in enumerate((own, got_z, got_c, got_both)):
        member = quarter[0] ^ r
        for part in range(6):
            spot = pl.ds(pl.multiple_of((4 * part + member) * HEAD, HEAD), HEAD)
            qkv[:, spot] = wide(part_of[:, part * HEAD : (part + 1) * HEAD])
        for part in range(8):
            block = 16 * (part >> 2) + 8 * (member >> 1) + 4 * ((part >> 1) & 1)
            block = block + 2 * (member & 1) + (part & 1)
            spot = pl.ds(pl.multiple_of(block * HEAD, HEAD), HEAD)
            up[:, spot] = wide(part_of[:, (6 + part) * HEAD : (7 + part) * HEAD])


def join(quarter, parts):
    rows = parts[0].shape[0]
    return pl.pallas_call(
        join_kernel,
        in_specs=[in_smem()] + [in_vmem()] * 4,
        out_shape=[jax.ShapeDtypeStruct((rows, n * HEAD), jnp.float32) for n in (24, 32)],
        out_specs=[in_vmem()] * 2,
        cost_estimate=pl.CostEstimate(flops=0, transcendentals=0, bytes_accessed=8 << 20),
        name="join",
    )(quarter.reshape(1), *parts)


def outer_kernel(former_near, former_far, latter_near, latter_far, out):
    def block(number, unused):
        spot = pl.ds(pl.multiple_of(number * STEP, STEP), STEP)
        total = dot_rows(former_near[:, spot], latter_near[...])
        out[spot] = low(total + dot_rows(former_far[:, spot], latter_far[...]))
        return unused

    lax.fori_loop(0, out.shape[0] // STEP, block, 0)


def outer(former_near, former_far, latter_near, latter_far):
    count, rows = former_near.shape
    columns = latter_near.shape[1]
    return pl.pallas_call(
        outer_kernel,
        out_shape=jax.ShapeDtypeStruct((rows, columns), jnp.bfloat16),
        compiler_params=pltpu.CompilerParams(vmem_limit_bytes=20 << 20),
        cost_estimate=pl.CostEstimate(
            flops=6 * count * rows * columns, transcendentals=0, bytes_accessed=6 << 20
        ),
        name="outer",
    )(former_near, former_far, latter_near, latter_far)


def feed_kernel(rows, grads, w_up, w_down, bias, activ, grad_up, back, forth, sums):
    sums[...] = jnp.zeros_like(sums)

    def inner(number, unused):
        spot = pl.ds(pl.multiple_of(number * STEP, STEP), STEP)
        upper = dense(rows[spot], w_up[...]) + bias[...]
        share = 0.5 + 0.5 * lax.erf(upper * (0.5**0.5))
        activ[spot] = low(upper * share)
        slope = share + upper * jnp.exp(-0.5 * upper * upper) * 0.3989422804014327
        grad = low(dot_t(grads[spot], w_down[...]) * slope)
        grad_up[spot] = grad
        sums[...] += jnp.sum(wide(grad), axis=0, keepdims=True)
        return unused

    def outwards(number, unused):
        unit = pl.ds(pl.multiple_of(number * STEP, STEP), STEP)
        back[:, unit] = low(dot_t(grad_up[...], w_up[unit]))
        forth[:, unit] = low(dense(activ[...], w_down[:, unit]))
        return unused

    lax.fori_loop(0, rows.shape[0] // STEP, inner, 0)
    lax.fori_loop(0, w_up.shape[0] // STEP, outwards, 0)


def feed(rows, grads, w_up, w_down, bias):
    count, features = rows.shape
    hidden = w_up.shape[1]
    kind = jnp.bfloat16
    return pl.pallas_call(
        feed_kernel,
        out_shape=(
            jax.ShapeDtypeStruct((count, hidden), kind),
            jax.ShapeDtypeStruct((count, hidden), kind),
            jax.ShapeDtypeStruct((count, features), kind),
            jax.ShapeDtypeStruct((count, features), kind),
            jax.ShapeDtypeStruct((1, hidden), jnp.float32),
        ),
        compiler_params=pltpu.CompilerParams(vmem_limit_bytes=28 << 20),
        cost_estimate=pl.CostEstimate(
            flops=11 * count * features * hidden,
            transcendentals=2 * count * hidden,
            bytes_accessed=8 << 20,
        ),
        name="feed",
    )(rows, grads, w_up, w_down, bias)


def team_body(
    inputs,
    segment_ids,
    cotangent,
    qkv_weight,
    out_weight,
    up_weight,
    down_weight,
    first_gain,
    first_bias,
    second_gain,
    second_bias,
    out_bias,
    up_bias,
    down_bias,
):
    batch_at, blk_at = lax.axis_index("batch"), lax.axis_index("blk")
    y, c = batch_at >> 1, batch_at & 1
    zh, z0, x = blk_at >> 2, (blk_at >> 1) & 1, blk_at & 1
    quarter = 2 * c + z0
    tokens, features = inputs.shape[2:]

    def send_rows(values):
        return [regroup(pick(values[:, 0], zh ^ flip), flip) for flip in (0, 1)]

    rows_near, rows_far = send_rows(inputs)
    grad_near, grad_far = send_rows(cotangent)
    singles = (first_gain, first_bias, second_gain, second_bias, out_bias, down_bias)
    own, *others = split(quarter, qkv_weight, up_weight, segment_ids, up_bias, singles)
    got = [swap(other, mask) for other, mask in zip(others, TEAM[1:])]
    w_out = grow(out_weight, 0, zh, ZH)
    own, *got, w_out, down_weight, grad_near, grad_far = tie(
        own, *got, w_out, down_weight, grad_near, grad_far
    )

    parts = ordered(ordered(own, got[0], z0, 0), ordered(got[1], got[2], z0, 0), c, 0)
    w_qkv = grow(parts[..., :896], 1, zh, ZH)
    w_up = parts[..., 896:]
    rows = wide(jnp.concatenate((rows_near, rows_far), 0))
    average = jnp.mean(rows, axis=-1, keepdims=True)
    centred = rows - average
    inverse_one = lax.rsqrt(jnp.mean(centred * centred, axis=-1, keepdims=True) + epsilon)
    scaled_one = centred * inverse_one
    sent = low(scaled_one)
    side = jnp.concatenate((sent, swap(sent, Z0)), 0)
    across = swap(side, C)
    w_qkv, down_weight = tie(w_qkv, down_weight)
    w_near = grow(w_qkv[0], 2, x, X)
    w_far = grow(w_qkv[1], 0, y, Y)
    w_near = grow(w_near, 0, y, Y)
    w_far = grow(w_far, 3, x, X)
    w_down = grow(down_weight, 0, zh, ZH)
    w_out = grow(grow(w_out, 1, z0, Z0), 0, y, Y)
    side, across, w_near, w_far, w_out, w_up, w_down, grad_near, grad_far = tie(
        side, across, w_near, w_far, w_out, w_up, w_down, grad_near, grad_far
    )

    w_qkv = jnp.stack((w_near, w_far), 1).reshape(features, -1)
    extra = wide(w_qkv[:, 768:]).T
    w_qkv = w_qkv[:, :768]
    gain_one, shift_one, gain_two, shift_two, bias_out, bias_down = (
        extra[i : i + 1] for i in range(6)
    )
    bias_up = extra[6:10].reshape(4, 2, 2, 2, 2, 2, 32)
    bias_up = pick(pick(bias_up, z0, 4), c, 2).transpose(1, 2, 3, 0, 4).reshape(1, -1)
    place = jnp.arange(features)
    ours = ((place >> 9) == y) & (((place >> 8) & 1) == x)
    ends = jnp.where(ours[None], lax.dynamic_slice_in_dim(extra, 10 + 3 * zh, 3, 0), 0.0)
    ends = jnp.sum(ends, 1) * (1.0 / 32.0)
    flips = jnp.stack((zh, z0, c))
    normed = low(wide(jnp.concatenate((side, across), 0)) * gain_one + shift_one)
    grad_own = jnp.concatenate((grad_near, grad_far), 0)
    grad_side = jnp.concatenate((grad_own, swap(grad_own, Z0)), 0)
    out_got = swap(w_out, X)
    down_near, down_far = w_down[:, :64], w_down[:, 64:]
    near_got = swap(down_near, Y)
    far_got = swap(down_far, X)
    up_got = swap(w_up, ZH)
    mixed = low(dense(normed, w_qkv))
    attended, away, logs = attend(ends, flips, mixed)
    came = swap(away, Z0)
    attended, out_got, up_got, near_got, far_got, grad_side = tie(
        attended, out_got, up_got, near_got, far_got, grad_side
    )
    w_out = ordered(w_out, out_got, x, 3)
    down_near = ordered(down_near, near_got, y, 0)
    down_far = ordered(down_far, far_got, x, 1)
    w_up = ordered(w_up, up_got, zh, 1)

    tokens_two = 2 * tokens
    out_both = jnp.concatenate(
        [pick(w_out, place, 1).reshape(-1, features) for place in (z0, 1 - z0)], 0
    )
    grad_across = swap(grad_side, C)
    w_near = grow(w_up[0], 2, x, X)
    w_far = grow(w_up[1], 0, y, Y)
    came, out_both, grad_across, down_near, down_far = tie(
        came, out_both, grad_across, down_near, down_far
    )
    down_near = grow(down_near, 2, x, X)
    down_far = grow(down_far, 0, y, Y)

    both = jnp.concatenate((attended, came), 1)
    far = dense(both[tokens_two:], out_both)
    near = dense(both[:tokens_two], out_both)
    middle = rows + near + wide(swap(low(far), C)) + bias_out
    normed_two, scaled_two, inverse_two = norm_rows(middle, gain_two, shift_two)
    normed_two = low(normed_two)
    near = jnp.concatenate((normed_two, swap(normed_two, Z0)), 0)
    far = swap(near, C)
    w_near = grow(w_near, 0, y, Y)
    w_far = grow(w_far, 3, x, X)
    w_up = jnp.stack((w_near, w_far), 1).reshape(features, -1)
    w_down = jnp.stack((down_near, down_far), 3).reshape(-1, features)
    near, far, w_down, w_up, grad_side, grad_across = tie(
        near, far, w_down, w_up, grad_side, grad_across
    )

    activ_far, upper_far, back_far, forth_far, sums_far = feed(
        far, grad_across, w_up, w_down, bias_up
    )
    activ, upper, back, forth, sums_near = feed(near, grad_side, w_up, w_down, bias_up)
    back, forth, back_far, forth_far, activ, upper = tie(
        back, forth, swap(back_far, C), swap(forth_far, C), activ, upper
    )

    count = back.shape[0] // 2
    back_own = wide(back[:count]) + wide(back_far[:count])
    back_other = low(wide(back[count:]) + wide(back_far[count:]))
    grad_two = back_own + wide(swap(back_other, Z0))
    grad_down = outer(activ, activ_far, grad_side, grad_across).reshape(2, 2, 2, 128, features)
    grad_up = outer(near, far, upper, upper_far).reshape(2, 2, 2, 2, 2, 32, -1)
    down_got = swap(pick(grad_down, 1 - y), Y)
    up_got = swap(pick(grad_up, 1 - x, 4), X)
    grad_two, grad_down, grad_up, forth, forth_far = tie(
        grad_two, grad_down, grad_up, forth, forth_far
    )

    grad_middle = wide(grad_own) + norm_back(grad_two, scaled_two, inverse_two, gain_two)
    branch_own = low(grad_middle)
    branch_own, branch, forth, forth_far = tie(
        branch_own, swap(branch_own, C), forth, forth_far
    )
    branch = jnp.concatenate((branch_own, branch), 0)
    grad_both = low(dot_t(branch, out_both))
    width = attended.shape[1]
    grad_attended = grad_both[:, :width]
    grad_came = swap(grad_both[:, width:], Z0)
    grad_w_out = low(dot_rows(both, branch)).reshape(2, 2, 2, 2, 32, features)
    grad_w_out = ordered(grad_w_out[0], grad_w_out[1], z0, 1)
    forth_own = wide(forth[:count]) + wide(forth_far[:count])
    forth_other = low(wide(forth[count:]) + wide(forth_far[count:]))
    final = low(middle + forth_own + wide(swap(forth_other, Z0)) + bias_down)
    grad_came, down_got, up_got, grad_w_out, final = tie(
        grad_came, down_got, up_got, grad_w_out, final
    )
    grad_down = low(wide(pick(grad_down, y)) + wide(down_got))
    grad_up = low(wide(pick(grad_up, x, 4)) + wide(up_got))

    def give_rows(values):
        got = (regroup(values[:tokens], 0), regroup(values[tokens:], 1))
        return wide(ordered(*got, zh, 0))[:, None]

    grad_down = low(shrink(grad_down, 1, x, X))
    grad_up = low(shrink(grad_up, 0, y, Y))
    grad_mixed = attend_back(ends, flips, mixed, grad_attended, grad_came, logs)
    final = give_rows(final)
    grad_w_out = low(shrink(grad_w_out, 0, y, Y))
    grad_mixed, grad_up, grad_down, final = tie(grad_mixed, grad_up, grad_down, final)

    half = 2 * tokens_two
    far = swap(low(dot_t(grad_mixed[half:], w_qkv)), C)
    back = dot_t(grad_mixed[:half], w_qkv)
    grad_qkv = low(dot_rows(normed, grad_mixed)).reshape(2, 2, 2, 2, 2, 32, -1)
    far, back, grad_qkv, grad_w_out, grad_up, grad_down = tie(
        far, back, grad_qkv, grad_w_out, grad_up, grad_down
    )
    back_own = back[:count] + wide(far[:count])
    back_other = low(back[count:] + wide(far[count:]))
    grad_one = back_own + wide(swap(back_other, Z0))
    qkv_near = low(shrink(low(shrink(grad_qkv[:, 0], 3, x, X)), 0, y, Y))
    qkv_far = low(shrink(low(shrink(grad_qkv[:, 1], 0, y, Y)), 2, x, X))
    grads = jnp.stack((grad_down, grad_up.transpose(1, 0, 2, 3, 4).reshape(2, 128, -1)), 1)
    grads = shrink(grads, 0, zh, ZH)
    grad_down = grads[0]
    grad_up = low(grads[1]).reshape(4, 32, -1)
    grad_w_out = low(shrink(grad_w_out, 2, x, X))
    grad_qkv = jnp.stack((qkv_near, qkv_far), 0)
    given = low(grad_middle + norm_back(grad_one, scaled_one, inverse_one, gain_one))
    given, grad_qkv, grad_w_out, grad_up, grad_down, grad_one = tie(
        given, grad_qkv, grad_w_out, grad_up, grad_down, grad_one
    )

    input_grad = give_rows(given)
    qkv_got = swap(pick(grad_qkv, 1 - zh, 1), ZH)
    out_got = swap(pick(grad_w_out, 1 - zh), ZH)
    qkv_got, out_got, grad_one = tie(qkv_got, out_got, grad_one)
    grad_qkv = low(wide(pick(grad_qkv, zh, 1)) + wide(qkv_got)).reshape(4, 32, -1)
    grad_w_out = wide(pick(grad_w_out, zh)) + wide(out_got)
    parts = jnp.concatenate((grad_qkv, grad_up), 2)
    parts = [pick(parts, quarter ^ r) for r in range(4)]
    parts[1] = jnp.concatenate((parts[1], low(pick(grad_w_out, 1 - z0))), 1)
    parts = parts[:1] + [swap(part, mask) for part, mask in zip(parts[1:], TEAM[1:])]
    grad_w_out = pick(grad_w_out, z0) + wide(parts[1][:, 1792:])
    grad_qkv, grad_up = join(quarter, parts)
    sums = jnp.stack(
        (
            jnp.sum(grad_one * scaled_one, 0),
            jnp.sum(grad_one, 0),
            jnp.sum(grad_two * scaled_two, 0),
            jnp.sum(grad_two, 0),
            jnp.sum(wide(branch_own), 0),
            jnp.sum(wide(grad_own), 0),
        )
    )
    sums = sums.reshape(6, 32, 32).transpose(1, 0, 2).reshape(32, 192)
    up_sums = (sums_near + sums_far).reshape(8, 1, 128)
    up_sums = jnp.where(jnp.arange(4)[None, :, None] == quarter, up_sums, 0.0)
    up_sums = up_sums.reshape(2, 2, 2, 2, 2, 128).transpose(0, 3, 1, 4, 2, 5).reshape(32, 128)
    sums = jnp.concatenate((up_sums, sums), 1)
    sums = jnp.sum(lax.all_to_all(sums, AXES, 0, 0, tiled=True), 0)
    grad_up_bias = sums[:128]
    small = [sums[128 + 32 * i : 160 + 32 * i] for i in range(6)]
    return (
        final,
        input_grad,
        grad_qkv,
        grad_w_out,
        grad_up,
        grad_down,
        small[0],
        small[1],
        small[2],
        small[3],
        small[4],
        grad_up_bias,
        small[5],
    )


def chosen_body(mesh, *arrays):
    shape = arrays[0].shape
    sizes = (mesh.shape["batch"], mesh.shape["blk"])
    if sizes == (4, 8) and shape == (2, 1, 128, 1024) and arrays[5].shape == (32, 4096):
        return team_body(*arrays)
    return body(*arrays)


def solution(mesh):
    return jax.shard_map(
        partial(chosen_body, mesh),
        mesh=mesh,
        in_specs=(
            P(None, "batch", "blk", None),
            P(None, "batch", "blk"),
            P(None, "batch", "blk", None),
            P(("batch", "blk"), None),
            P(("batch", "blk"), None),
            P(("batch", "blk"), None),
            P(("batch", "blk"), None),
            P(("batch", "blk")),
            P(("batch", "blk")),
            P(("batch", "blk")),
            P(("batch", "blk")),
            P(("batch", "blk")),
            P(("batch", "blk")),
            P(("batch", "blk")),
        ),
        out_specs=(
            P(None, "batch", "blk", None),
            P(None, "batch", "blk", None),
            P(("batch", "blk"), None),
            P(("batch", "blk"), None),
            P(("batch", "blk"), None),
            P(("batch", "blk"), None),
            P(("batch", "blk")),
            P(("batch", "blk")),
            P(("batch", "blk")),
            P(("batch", "blk")),
            P(("batch", "blk")),
            P(("batch", "blk")),
            P(("batch", "blk")),
        ),
        check_vma=False,
    )
```

```python
from functools import partial

import jax
import jax.numpy as jnp
from jax import lax
from jax.experimental import pallas as pl
from jax.experimental.pallas import tpu as pltpu
from jax.sharding import PartitionSpec as P

H = 8


epsilon = 1e-05
masked_score = -1e30


def dense(former, latter):
    return jnp.dot(former, latter, preferred_element_type=jnp.float32)


def norm_rows(values, gains, shifts):
    average = jnp.mean(values, axis=-1, keepdims=True)
    centred = values - average
    inverse = lax.rsqrt(jnp.mean(centred * centred, axis=-1, keepdims=True) + epsilon)
    scaled = centred * inverse
    return (scaled * gains + shifts, scaled, inverse)


def norm_back(gradient, scaled, inverse, gains):
    upstream = gradient * gains
    return inverse * (
        upstream
        - jnp.mean(upstream, axis=-1, keepdims=True)
        - scaled * jnp.mean(upstream * scaled, axis=-1, keepdims=True)
    )


def block_scan(update, carried, pieces):
    amount = pieces[0].shape[1]
    stride = min(512, amount)

    def block_step(state_now, number):
        sliced = tuple(
            (lax.dynamic_slice_in_dim(member, number * stride, stride, 1) for member in pieces)
        )
        return (update(state_now, sliced), None)

    carried, unused = lax.scan(block_step, carried, jnp.arange(amount // stride))
    return carried


def split_heads(rows, head_count):
    return rows.reshape(rows.shape[0], rows.shape[1], head_count, rows.shape[2] // head_count)


def attend_piece(running, sliced, queries, query_segs):
    maximum, totals, accumulated = running
    key_part, value_part, seg_part = sliced
    head_count, head_size = (queries.shape[2], queries.shape[3])
    key_heads = split_heads(key_part, head_count)
    value_heads = split_heads(value_part, head_count)
    scores = jnp.einsum(
        "sqhd,skhd->shqk", queries, key_heads, preferred_element_type=jnp.float32
    ) * head_size ** (-0.5)
    allowed = query_segs[:, None, :, None] == seg_part[:, None, None, :]
    scores = jnp.where(allowed, scores, masked_score)
    highest = jnp.maximum(maximum, jnp.max(scores, axis=-1, keepdims=True))
    factor = jnp.exp(maximum - highest)
    shares = jnp.exp(scores - highest)
    totals = totals * factor + jnp.sum(shares, axis=-1, keepdims=True)
    accumulated = accumulated * factor + jnp.einsum(
        "shqk,skhd->shqd",
        shares.astype(jnp.bfloat16),
        value_heads,
        preferred_element_type=jnp.float32,
    )
    return (highest, totals, accumulated)


def fold_keys(running, pieces, queries, query_segs):
    return block_scan(
        partial(attend_piece, queries=queries, query_segs=query_segs), running, pieces
    )


def grad_block(queries, grad_heads, query_segs, log_total, delta, key_heads, value_heads, key_segs):
    head_size = queries.shape[3]
    scores = jnp.einsum(
        "sqhd,skhd->shqk", queries, key_heads, preferred_element_type=jnp.float32
    ) * head_size ** (-0.5)
    allowed = query_segs[:, None, :, None] == key_segs[:, None, None, :]
    shares = jnp.where(allowed, jnp.exp(scores - log_total), 0.0)
    grad_shares = jnp.einsum(
        "sqhd,skhd->shqk", grad_heads, value_heads, preferred_element_type=jnp.float32
    )
    grad_scores = (shares * (grad_shares - delta)).astype(jnp.bfloat16)
    return (shares.astype(jnp.bfloat16), grad_scores)


def micro_step(set_inputs, set_segs, set_cotangent, gathered):
    (
        weight_qkv,
        weight_out,
        weight_up,
        weight_down,
        gain_one,
        shift_one,
        gain_two,
        shift_two,
        bias_out,
        bias_up,
        bias_down,
    ) = gathered
    set_count, tok_count, features = set_inputs.shape
    head_count = H
    head_size = features // head_count
    scale = head_size ** (-0.5)
    rows = set_inputs.astype(jnp.float32).reshape(-1, features)
    normed, scaled_one, inverse_one = norm_rows(
        rows, gain_one.astype(jnp.float32), shift_one.astype(jnp.float32)
    )
    normed_low = normed.astype(jnp.bfloat16)
    mixed = dense(normed_low, weight_qkv).astype(jnp.bfloat16)
    queries = mixed[:, :features].reshape(set_count, tok_count, head_count, head_size)
    key_rows = mixed[:, features : 2 * features].reshape(set_count, tok_count, features)
    value_rows = mixed[:, 2 * features :].reshape(set_count, tok_count, features)
    running = (
        jnp.full((set_count, head_count, tok_count, 1), masked_score, jnp.float32),
        jnp.zeros((set_count, head_count, tok_count, 1), jnp.float32),
        jnp.zeros((set_count, head_count, tok_count, head_size), jnp.float32),
    )
    running = fold_keys(
        running,
        (
            lax.all_gather(key_rows, "blk", axis=1, tiled=True),
            lax.all_gather(value_rows, "blk", axis=1, tiled=True),
            lax.all_gather(set_segs, "blk", axis=1, tiled=True),
        ),
        queries=queries,
        query_segs=set_segs,
    )
    maximum, totals, accumulated = running
    attended = accumulated / totals
    log_total = maximum + jnp.log(totals)
    attended_low = jnp.transpose(attended, (0, 2, 1, 3)).reshape(-1, features).astype(jnp.bfloat16)
    middle = rows + dense(attended_low, weight_out) + bias_out.astype(jnp.float32)
    normed_two, scaled_two, inverse_two = norm_rows(
        middle, gain_two.astype(jnp.float32), shift_two.astype(jnp.float32)
    )
    normed_two_low = normed_two.astype(jnp.bfloat16)
    upper = dense(normed_two_low, weight_up) + bias_up.astype(jnp.float32)
    activ_value, gelu_back = jax.vjp(lambda v: jax.nn.gelu(v, approximate=False), upper)
    activ_low = activ_value.astype(jnp.bfloat16)
    final = middle + dense(activ_low, weight_down) + bias_down.astype(jnp.float32)
    grad_out = set_cotangent.astype(jnp.float32).reshape(-1, features)
    grad_low = grad_out.astype(jnp.bfloat16)
    grad_down_bias = jnp.sum(grad_low.astype(jnp.float32), axis=0)
    grad_down = jnp.einsum("rf,rd->fd", activ_low, grad_low, preferred_element_type=jnp.float32)
    grad_activ = jnp.einsum("rd,fd->rf", grad_low, weight_down, preferred_element_type=jnp.float32)
    grad_upper = gelu_back(grad_activ)[0].astype(jnp.bfloat16)
    grad_up_bias = jnp.sum(grad_upper.astype(jnp.float32), axis=0)
    grad_up = jnp.einsum(
        "rd,rf->df", normed_two_low, grad_upper, preferred_element_type=jnp.float32
    )
    grad_normed_two = jnp.einsum(
        "rf,df->rd", grad_upper, weight_up, preferred_element_type=jnp.float32
    )
    grad_gain_two = jnp.sum(grad_normed_two * scaled_two, axis=0)
    grad_shift_two = jnp.sum(grad_normed_two, axis=0)
    grad_middle = grad_out + norm_back(
        grad_normed_two, scaled_two, inverse_two, gain_two.astype(jnp.float32)
    )
    branch_low = grad_middle.astype(jnp.bfloat16)
    grad_out_bias = jnp.sum(branch_low.astype(jnp.float32), axis=0)
    grad_out_weight = jnp.einsum(
        "rd,re->de", attended_low, branch_low, preferred_element_type=jnp.float32
    )
    grad_attended = jnp.einsum(
        "re,de->rd", branch_low, weight_out, preferred_element_type=jnp.float32
    )
    grad_heads = grad_attended.astype(jnp.bfloat16).reshape(
        set_count, tok_count, head_count, head_size
    )
    delta = jnp.einsum("sqhd,shqd->shq", grad_heads.astype(jnp.float32), attended)[..., None]
    everything = (
        lax.all_gather(key_rows, "blk", axis=1, tiled=True),
        lax.all_gather(value_rows, "blk", axis=1, tiled=True),
        lax.all_gather(set_segs, "blk", axis=1, tiled=True),
    )
    length = everything[0].shape[1]
    stride = min(512, length)

    def key_block(grad_query, number):
        key_part = lax.dynamic_slice_in_dim(everything[0], number * stride, stride, 1)
        value_part = lax.dynamic_slice_in_dim(everything[1], number * stride, stride, 1)
        seg_part = lax.dynamic_slice_in_dim(everything[2], number * stride, stride, 1)
        key_heads = split_heads(key_part, head_count)
        share_low, score_low = grad_block(
            queries,
            grad_heads,
            set_segs,
            log_total,
            delta,
            key_heads,
            split_heads(value_part, head_count),
            seg_part,
        )
        grad_query = (
            grad_query
            + jnp.einsum(
                "shqk,skhd->sqhd", score_low, key_heads, preferred_element_type=jnp.float32
            )
            * scale
        )
        key_term = (
            jnp.einsum("shqk,sqhd->kshd", score_low, queries, preferred_element_type=jnp.float32)
            * scale
        )
        value_term = jnp.einsum(
            "shqk,sqhd->kshd", share_low, grad_heads, preferred_element_type=jnp.float32
        )
        return (
            grad_query,
            jnp.concatenate(
                (
                    key_term.reshape(stride, set_count, features),
                    value_term.reshape(stride, set_count, features),
                ),
                axis=-1,
            ),
        )

    grad_query, terms = lax.scan(
        key_block, jnp.zeros(queries.shape, jnp.float32), jnp.arange(length // stride)
    )
    summed = lax.psum_scatter(
        terms.reshape(length, set_count, 2 * features).astype(jnp.bfloat16),
        "blk",
        scatter_dimension=0,
        tiled=True,
    ).astype(jnp.float32)
    summed = jnp.transpose(summed, (1, 0, 2)).reshape(-1, 2 * features)
    grad_keys = summed[:, :features]
    grad_values = summed[:, features:]
    grad_mixed = jnp.concatenate(
        (grad_query.reshape(-1, features), grad_keys, grad_values), axis=-1
    ).astype(jnp.bfloat16)
    grad_qkv = jnp.einsum("rd,re->de", normed_low, grad_mixed, preferred_element_type=jnp.float32)
    grad_normed = jnp.einsum(
        "re,de->rd", grad_mixed, weight_qkv, preferred_element_type=jnp.float32
    )
    grad_gain_one = jnp.sum(grad_normed * scaled_one, axis=0)
    grad_shift_one = jnp.sum(grad_normed, axis=0)
    grad_input = grad_middle + norm_back(
        grad_normed, scaled_one, inverse_one, gain_one.astype(jnp.float32)
    )
    local_grads = (
        grad_qkv,
        grad_out_weight,
        grad_up,
        grad_down,
        grad_gain_one,
        grad_shift_one,
        grad_gain_two,
        grad_shift_two,
        grad_out_bias,
        grad_up_bias,
        grad_down_bias,
    )
    return (
        final.reshape(set_count, tok_count, features),
        grad_input.reshape(set_count, tok_count, features),
        local_grads,
    )


def body(
    inputs,
    segment_ids,
    cotangent,
    qkv_weight,
    out_weight,
    up_weight,
    down_weight,
    first_gain,
    first_bias,
    second_gain,
    second_bias,
    out_bias,
    up_bias,
    down_bias,
):
    shards = (
        qkv_weight,
        out_weight,
        up_weight,
        down_weight,
        first_gain,
        first_bias,
        second_gain,
        second_bias,
        out_bias,
        up_bias,
        down_bias,
    )
    shard_sums = tuple((jnp.zeros(member.shape, jnp.float32) for member in shards))
    outcomes = []
    input_grads = []
    for micro_index in range(inputs.shape[0]):
        gathered = (
            lax.all_gather(qkv_weight, ("batch", "blk"), axis=0, tiled=True),
            lax.all_gather(out_weight, ("batch", "blk"), axis=0, tiled=True),
            lax.all_gather(up_weight, ("batch", "blk"), axis=0, tiled=True),
            lax.all_gather(down_weight, ("batch", "blk"), axis=0, tiled=True),
            lax.all_gather(first_gain, ("batch", "blk"), axis=0, tiled=True),
            lax.all_gather(first_bias, ("batch", "blk"), axis=0, tiled=True),
            lax.all_gather(second_gain, ("batch", "blk"), axis=0, tiled=True),
            lax.all_gather(second_bias, ("batch", "blk"), axis=0, tiled=True),
            lax.all_gather(out_bias, ("batch", "blk"), axis=0, tiled=True),
            lax.all_gather(up_bias, ("batch", "blk"), axis=0, tiled=True),
            lax.all_gather(down_bias, ("batch", "blk"), axis=0, tiled=True),
        )
        final, grad_input, local_grads = micro_step(
            inputs[micro_index], segment_ids[micro_index], cotangent[micro_index], gathered
        )
        outcomes.append(final)
        input_grads.append(grad_input)
        summed = (
            lax.psum_scatter(local_grads[0], ("batch", "blk"), scatter_dimension=0, tiled=True),
            lax.psum_scatter(local_grads[1], ("batch", "blk"), scatter_dimension=0, tiled=True),
            lax.psum_scatter(local_grads[2], ("batch", "blk"), scatter_dimension=0, tiled=True),
            lax.psum_scatter(local_grads[3], ("batch", "blk"), scatter_dimension=0, tiled=True),
            lax.psum_scatter(local_grads[4], ("batch", "blk"), scatter_dimension=0, tiled=True),
            lax.psum_scatter(local_grads[5], ("batch", "blk"), scatter_dimension=0, tiled=True),
            lax.psum_scatter(local_grads[6], ("batch", "blk"), scatter_dimension=0, tiled=True),
            lax.psum_scatter(local_grads[7], ("batch", "blk"), scatter_dimension=0, tiled=True),
            lax.psum_scatter(local_grads[8], ("batch", "blk"), scatter_dimension=0, tiled=True),
            lax.psum_scatter(local_grads[9], ("batch", "blk"), scatter_dimension=0, tiled=True),
            lax.psum_scatter(local_grads[10], ("batch", "blk"), scatter_dimension=0, tiled=True),
        )
        shard_sums = tuple((former + latter for former, latter in zip(shard_sums, summed)))
    return (jnp.stack(outcomes), jnp.stack(input_grads)) + tuple(shard_sums)


AXES = ("batch", "blk")
Y, C, ZH, Z0, X = 16, 8, 4, 2, 1
TEAM = (0, Z0, C, C | Z0)


def swap(values, mask):
    return lax.ppermute(values, AXES, [(i, i ^ mask) for i in range(32)])


def regroup(values, flip):
    pairs = []
    for i in range(32):
        core, right = (i >> 3) & 1, i & 1
        pairs.append((i, (i & (Y | Z0)) | (right << 3) | ((i & ZH) ^ (flip << 2)) | core))
    return lax.ppermute(values, AXES, pairs)


def ordered(near, far, bit, axis):
    return jnp.stack((jnp.where(bit == 0, near, far), jnp.where(bit == 0, far, near)), axis)


def grow(values, axis, bit, mask):
    return ordered(values, swap(values, mask), bit, axis)


def pick(values, place, axis=0):
    return lax.dynamic_index_in_dim(values, place, axis, keepdims=False)


def shrink(values, axis, bit, mask):
    got = swap(pick(values, 1 - bit, axis), mask)
    return pick(values, bit, axis).astype(jnp.float32) + got.astype(jnp.float32)


def tie(*values):
    return lax.optimization_barrier(values)


def low(values):
    return values.astype(jnp.bfloat16)


def wide(values):
    return values.astype(jnp.float32)


def team_trade(parts, quarter, bit_c, bit_z):
    own = pick(parts, quarter)
    got = [swap(pick(parts, quarter ^ r), TEAM[r]) for r in (1, 2, 3)]
    return ordered(
        ordered(own, got[0], bit_z, 0), ordered(got[1], got[2], bit_z, 0), bit_c, 0
    )


def team_gather(rows):
    near = jnp.concatenate((rows, swap(rows, Z0)), 0)
    return jnp.concatenate((near, swap(near, C)), 0)


def team_scatter(near, far):
    half = near.shape[0] // 2
    near = wide(near) + wide(swap(low(far), C))
    return near[:half] + wide(swap(low(near[half:]), Z0))


def dot_t(former, latter):
    return lax.dot_general(
        former, latter, (((1,), (1,)), ((), ())), preferred_element_type=jnp.float32
    )


def dot_rows(former, latter):
    return lax.dot_general(
        former, latter, (((0,), (0,)), ((), ())), preferred_element_type=jnp.float32
    )


STEP = 256
HEAD = 128


def image_of(ends, flips, shape, axis, base=0):
    row = lax.broadcasted_iota(jnp.int32, shape, axis) + base
    block = row >> 7
    chunk = 4 * ((block & 1) ^ flips[0]) + 2 * (((block >> 1) & 1) ^ flips[1])
    chunk = chunk + ((block >> 2) ^ flips[2])
    spot = (chunk * 128 + (row & 127)).astype(jnp.float32)
    return sum(jnp.where(spot >= ends[i], 1.0, 0.0) for i in range(3))


LOG2E = 1.4426950408889634


def attend_kernel(ends, flips, mixed, near, far, logs, images):
    rows = mixed.shape[0]
    heads = near.shape[1] // HEAD
    scale = HEAD ** (-0.5) * LOG2E
    images[...] = image_of(ends, flips, images.shape, 0)

    def block(number, unused):
        start = pl.multiple_of(number * STEP, STEP)
        spot = pl.ds(start, STEP)
        target = pl.ds(pl.multiple_of((number >> 1) * STEP, STEP), STEP)
        image = image_of(ends, flips, (1, STEP), 1, start)
        column = images[...]
        same = jnp.concatenate([column] * (STEP // HEAD), 1) == image

        def one_head(head, unused):
            at_q, at_k, at_v = (
                pl.ds(pl.multiple_of((part * heads + head) * HEAD, HEAD), HEAD) for part in range(3)
            )
            scores = dot_t(mixed[:, at_k], mixed[spot, at_q])
            scores = jnp.where(same, scores * scale, masked_score)
            highest = jnp.max(scores, axis=0, keepdims=True)
            shares = jnp.exp2(scores - highest)
            total = jnp.sum(shares, axis=0, keepdims=True)
            mixture = dot_rows(mixed[:, at_v], low(shares)) / total
            mixture = low(mixture.T)
            logs[pl.ds(head, 1), spot] = highest + jnp.log2(total)

            @pl.when(number % 2 == 0)
            def _():
                near[target, at_q] = mixture

            @pl.when(number % 2 == 1)
            def _():
                far[target, at_q] = mixture

            return unused

        return lax.fori_loop(0, heads, one_head, unused)

    lax.fori_loop(0, rows // STEP, block, 0)


def attend_back_kernel(
    ends, flips, mixed, near, far, logs, out, key_sum, value_sum, images, both
):
    rows = mixed.shape[0]
    heads = near.shape[1] // HEAD
    scale = HEAD ** (-0.5)
    images[...] = image_of(ends, flips, images.shape, 0)
    key_sum[...] = jnp.zeros_like(key_sum)
    value_sum[...] = jnp.zeros_like(value_sum)
    for number in range(rows // STEP):
        source = (near, far)[number % 2]
        spot = (number // 2) * STEP
        both[number * STEP : (number + 1) * STEP] = source[spot : spot + STEP]

    def block(number, unused):
        start = pl.multiple_of(number * STEP, STEP)
        spot = pl.ds(start, STEP)
        image = image_of(ends, flips, (1, STEP), 1, start)
        column = images[...]
        same = jnp.concatenate([column] * (STEP // HEAD), 1) == image

        def one_head(head, unused):
            at_q, at_k, at_v = (
                pl.ds(pl.multiple_of((part * heads + head) * HEAD, HEAD), HEAD) for part in range(3)
            )
            queries = mixed[spot, at_q]
            grad = both[spot, at_q]
            keys = mixed[:, at_k]
            scores = dot_t(keys, queries) * (scale * LOG2E) - logs[pl.ds(head, 1), spot]
            shares = jnp.exp2(jnp.where(same, scores, masked_score))
            grad_shares = dot_t(mixed[:, at_v], grad)
            delta = jnp.sum(shares * grad_shares, axis=0, keepdims=True)
            grad_scores = low(shares * (grad_shares - delta))
            value_sum[:, at_q] += jnp.dot(low(shares), grad, preferred_element_type=jnp.float32)
            key_sum[:, at_q] += jnp.dot(grad_scores, queries, preferred_element_type=jnp.float32)
            out[spot, at_q] = low((dot_rows(keys, grad_scores) * scale).T)
            return unused

        return lax.fori_loop(0, heads, one_head, unused)

    lax.fori_loop(0, rows // STEP, block, 0)
    width = heads * HEAD
    out[:, width : 2 * width] = low(key_sum[...] * scale)
    out[:, 2 * width :] = low(value_sum[...])


def in_smem():
    return pl.BlockSpec(memory_space=pltpu.SMEM)


def in_vmem():
    return pl.BlockSpec(memory_space=pltpu.VMEM)


def attend(ends, flips, mixed):
    rows, columns = mixed.shape
    heads = columns // (3 * HEAD)
    work = 2 * rows * rows * HEAD * heads
    half = jax.ShapeDtypeStruct((rows // 2, heads * HEAD), jnp.bfloat16)
    return pl.pallas_call(
        attend_kernel,
        in_specs=[in_smem(), in_smem(), in_vmem()],
        out_shape=(half, half, jax.ShapeDtypeStruct((heads, rows), jnp.float32)),
        scratch_shapes=[pltpu.VMEM((rows, HEAD), jnp.float32)],
        compiler_params=pltpu.CompilerParams(vmem_limit_bytes=16 << 20),
        cost_estimate=pl.CostEstimate(
            flops=18 * work, transcendentals=rows * rows * heads, bytes_accessed=4 << 20
        ),
        name="attend",
    )(ends, flips, mixed)


def attend_back(ends, flips, mixed, near, far, logs):
    rows, columns = mixed.shape
    heads = columns // (3 * HEAD)
    work = 2 * rows * rows * HEAD * heads
    return pl.pallas_call(
        attend_back_kernel,
        in_specs=[in_smem(), in_smem()] + [in_vmem()] * 4,
        out_shape=jax.ShapeDtypeStruct((rows, columns), jnp.bfloat16),
        scratch_shapes=[
            pltpu.VMEM((rows, heads * HEAD), jnp.float32),
            pltpu.VMEM((rows, heads * HEAD), jnp.float32),
            pltpu.VMEM((rows, HEAD), jnp.float32),
            pltpu.VMEM((rows, heads * HEAD), jnp.bfloat16),
        ],
        compiler_params=pltpu.CompilerParams(vmem_limit_bytes=20 << 20),
        cost_estimate=pl.CostEstimate(
            flops=22 * work, transcendentals=rows * rows * heads, bytes_accessed=6 << 20
        ),
        name="attend_back",
    )(ends, flips, mixed, near, far, logs)


def split_kernel(quarter, qkv, up, ids, up_vector, *refs):
    singles, outs, board = refs[:6], refs[6:10], refs[10]
    board[...] = jnp.zeros_like(board)
    for i, single in enumerate(singles):
        board[i : i + 1, :32] = wide(single[...])
    for i in range(4):
        board[6 + i : 7 + i, :32] = wide(up_vector[:, 32 * i : 32 * i + 32])
    for m in range(2):
        for i in range(3):
            below = jnp.where(ids[m : m + 1] <= i, 1.0, 0.0)
            below = jnp.sum(below, axis=1, keepdims=True)
            board[10 + 3 * m + i : 11 + 3 * m + i, :] = jnp.broadcast_to(below, (1, 128))
    extra = low(board[...].T[:32])
    for r, out in enumerate(outs):
        member = quarter[0] ^ r
        for part in range(6):
            spot = pl.ds(pl.multiple_of((4 * part + member) * HEAD, HEAD), HEAD)
            out[:, part * HEAD : (part + 1) * HEAD] = qkv[:, spot]
        out[:, 6 * HEAD : 7 * HEAD] = extra
        for part in range(8):
            block = 16 * (part >> 2) + 8 * (member >> 1) + 4 * ((part >> 1) & 1)
            block = block + 2 * (member & 1) + (part & 1)
            spot = pl.ds(pl.multiple_of(block * HEAD, HEAD), HEAD)
            out[:, (7 + part) * HEAD : (8 + part) * HEAD] = up[:, spot]


def split(quarter, qkv, up, ids, up_vector, singles):
    rows = qkv.shape[0]
    return pl.pallas_call(
        split_kernel,
        in_specs=[in_smem()] + [in_vmem()] * 10,
        out_shape=[jax.ShapeDtypeStruct((rows, 15 * HEAD), jnp.bfloat16)] * 4,
        out_specs=[in_vmem()] * 4,
        scratch_shapes=[pltpu.VMEM((128, 128), jnp.float32)],
        cost_estimate=pl.CostEstimate(flops=0, transcendentals=0, bytes_accessed=1 << 20),
        name="split",
    )(
        quarter.reshape(1),
        qkv,
        up,
        ids.reshape(2, -1),
        up_vector.reshape(1, -1),
        *(single.reshape(1, -1) for single in singles),
    )


def join_kernel(quarter, own, got_z, got_c, got_both, qkv, up):
    for r, part_of in enumerate((own, got_z, got_c, got_both)):
        member = quarter[0] ^ r
        for part in range(6):
            spot = pl.ds(pl.multiple_of((4 * part + member) * HEAD, HEAD), HEAD)
            qkv[:, spot] = wide(part_of[:, part * HEAD : (part + 1) * HEAD])
        for part in range(8):
            block = 16 * (part >> 2) + 8 * (member >> 1) + 4 * ((part >> 1) & 1)
            block = block + 2 * (member & 1) + (part & 1)
            spot = pl.ds(pl.multiple_of(block * HEAD, HEAD), HEAD)
            up[:, spot] = wide(part_of[:, (6 + part) * HEAD : (7 + part) * HEAD])


def join(quarter, parts):
    rows = parts[0].shape[0]
    return pl.pallas_call(
        join_kernel,
        in_specs=[in_smem()] + [in_vmem()] * 4,
        out_shape=[jax.ShapeDtypeStruct((rows, n * HEAD), jnp.float32) for n in (24, 32)],
        out_specs=[in_vmem()] * 2,
        cost_estimate=pl.CostEstimate(flops=0, transcendentals=0, bytes_accessed=8 << 20),
        name="join",
    )(quarter.reshape(1), *parts)


def outer_kernel(former_near, former_far, latter_near, latter_far, out):
    def block(number, unused):
        spot = pl.ds(pl.multiple_of(number * STEP, STEP), STEP)
        total = dot_rows(former_near[:, spot], latter_near[...])
        out[spot] = low(total + dot_rows(former_far[:, spot], latter_far[...]))
        return unused

    lax.fori_loop(0, out.shape[0] // STEP, block, 0)


def outer(former_near, former_far, latter_near, latter_far):
    count, rows = former_near.shape
    columns = latter_near.shape[1]
    return pl.pallas_call(
        outer_kernel,
        out_shape=jax.ShapeDtypeStruct((rows, columns), jnp.bfloat16),
        compiler_params=pltpu.CompilerParams(vmem_limit_bytes=20 << 20),
        cost_estimate=pl.CostEstimate(
            flops=6 * count * rows * columns, transcendentals=0, bytes_accessed=6 << 20
        ),
        name="outer",
    )(former_near, former_far, latter_near, latter_far)


def feed_kernel(rows, grads, w_up, w_down, bias, activ, grad_up, back, forth, sums):
    sums[...] = jnp.zeros_like(sums)

    def block(number, unused):
        spot = pl.ds(pl.multiple_of(number * STEP, STEP), STEP)
        upper = dense(rows[spot], w_up[...]) + bias[...]
        share = 0.5 + 0.5 * lax.erf(upper * (0.5**0.5))
        act = low(upper * share)
        slope = share + upper * jnp.exp(-0.5 * upper * upper) * 0.3989422804014327
        grad = low(dot_t(grads[spot], w_down[...]) * slope)
        activ[spot] = act
        grad_up[spot] = grad
        sums[...] += jnp.sum(wide(grad), axis=0, keepdims=True)
        back[spot] = low(dot_t(grad, w_up[...]))
        forth[spot] = low(dense(act, w_down[...]))
        return unused

    lax.fori_loop(0, rows.shape[0] // STEP, block, 0)


def feed(rows, grads, w_up, w_down, bias):
    count, features = rows.shape
    hidden = w_up.shape[1]
    kind = jnp.bfloat16
    return pl.pallas_call(
        feed_kernel,
        out_shape=(
            jax.ShapeDtypeStruct((count, hidden), kind),
            jax.ShapeDtypeStruct((count, hidden), kind),
            jax.ShapeDtypeStruct((count, features), kind),
            jax.ShapeDtypeStruct((count, features), kind),
            jax.ShapeDtypeStruct((1, hidden), jnp.float32),
        ),
        compiler_params=pltpu.CompilerParams(vmem_limit_bytes=28 << 20),
        cost_estimate=pl.CostEstimate(
            flops=11 * count * features * hidden,
            transcendentals=2 * count * hidden,
            bytes_accessed=8 << 20,
        ),
        name="feed",
    )(rows, grads, w_up, w_down, bias)


def team_body(
    inputs,
    segment_ids,
    cotangent,
    qkv_weight,
    out_weight,
    up_weight,
    down_weight,
    first_gain,
    first_bias,
    second_gain,
    second_bias,
    out_bias,
    up_bias,
    down_bias,
):
    batch_at, blk_at = lax.axis_index("batch"), lax.axis_index("blk")
    y, c = batch_at >> 1, batch_at & 1
    zh, z0, x = blk_at >> 2, (blk_at >> 1) & 1, blk_at & 1
    quarter = 2 * c + z0
    tokens, features = inputs.shape[2:]

    def send_rows(values):
        return [regroup(pick(values[:, 0], zh ^ flip), flip) for flip in (0, 1)]

    rows_near, rows_far = send_rows(inputs)
    grad_near, grad_far = send_rows(cotangent)
    singles = (first_gain, first_bias, second_gain, second_bias, out_bias, down_bias)
    own, *others = split(quarter, qkv_weight, up_weight, segment_ids, up_bias, singles)
    got = [swap(other, mask) for other, mask in zip(others, TEAM[1:])]
    w_out = grow(out_weight, 0, zh, ZH)
    own, *got, w_out, down_weight, grad_near, grad_far = tie(
        own, *got, w_out, down_weight, grad_near, grad_far
    )

    parts = ordered(ordered(own, got[0], z0, 0), ordered(got[1], got[2], z0, 0), c, 0)
    w_qkv = grow(parts[..., :896], 1, zh, ZH)
    w_up = parts[..., 896:]
    rows = wide(jnp.concatenate((rows_near, rows_far), 0))
    average = jnp.mean(rows, axis=-1, keepdims=True)
    centred = rows - average
    inverse_one = lax.rsqrt(jnp.mean(centred * centred, axis=-1, keepdims=True) + epsilon)
    scaled_one = centred * inverse_one
    sent = low(scaled_one)
    side = jnp.concatenate((sent, swap(sent, Z0)), 0)
    across = swap(side, C)
    w_qkv, down_weight = tie(w_qkv, down_weight)
    w_near = grow(w_qkv[0], 2, x, X)
    w_far = grow(w_qkv[1], 0, y, Y)
    w_near = grow(w_near, 0, y, Y)
    w_far = grow(w_far, 3, x, X)
    w_down = grow(down_weight, 0, zh, ZH)
    w_out = grow(grow(w_out, 1, z0, Z0), 0, y, Y)
    side, across, w_near, w_far, w_out, w_up, w_down, grad_near, grad_far = tie(
        side, across, w_near, w_far, w_out, w_up, w_down, grad_near, grad_far
    )

    w_qkv = jnp.stack((w_near, w_far), 1).reshape(features, -1)
    extra = wide(w_qkv[:, 768:]).T
    w_qkv = w_qkv[:, :768]
    gain_one, shift_one, gain_two, shift_two, bias_out, bias_down = (
        extra[i : i + 1] for i in range(6)
    )
    bias_up = extra[6:10].reshape(4, 2, 2, 2, 2, 2, 32)
    bias_up = pick(pick(bias_up, z0, 4), c, 2).transpose(1, 2, 3, 0, 4).reshape(1, -1)
    place = jnp.arange(features)
    ours = ((place >> 9) == y) & (((place >> 8) & 1) == x)
    ends = jnp.where(ours[None], lax.dynamic_slice_in_dim(extra, 10 + 3 * zh, 3, 0), 0.0)
    ends = jnp.sum(ends, 1) * (1.0 / 32.0)
    flips = jnp.stack((zh, z0, c))
    normed = low(wide(jnp.concatenate((side, across), 0)) * gain_one + shift_one)
    grad_own = jnp.concatenate((grad_near, grad_far), 0)
    grad_side = jnp.concatenate((grad_own, swap(grad_own, Z0)), 0)
    out_got = swap(w_out, X)
    down_near, down_far = w_down[:, :64], w_down[:, 64:]
    near_got = swap(down_near, Y)
    far_got = swap(down_far, X)
    up_got = swap(w_up, ZH)
    mixed = low(dense(normed, w_qkv))
    attended, away, logs = attend(ends, flips, mixed)
    came = swap(away, Z0)
    attended, out_got, up_got, near_got, far_got, grad_side = tie(
        attended, out_got, up_got, near_got, far_got, grad_side
    )
    w_out = ordered(w_out, out_got, x, 3)
    down_near = ordered(down_near, near_got, y, 0)
    down_far = ordered(down_far, far_got, x, 1)
    w_up = ordered(w_up, up_got, zh, 1)

    tokens_two = 2 * tokens
    out_both = jnp.concatenate(
        [pick(w_out, place, 1).reshape(-1, features) for place in (z0, 1 - z0)], 0
    )
    grad_across = swap(grad_side, C)
    w_near = grow(w_up[0], 2, x, X)
    w_far = grow(w_up[1], 0, y, Y)
    came, out_both, grad_across, down_near, down_far = tie(
        came, out_both, grad_across, down_near, down_far
    )
    down_near = grow(down_near, 2, x, X)
    down_far = grow(down_far, 0, y, Y)

    both = jnp.concatenate((attended, came), 1)
    far = dense(both[tokens_two:], out_both)
    near = dense(both[:tokens_two], out_both)
    middle = rows + near + wide(swap(low(far), C)) + bias_out
    normed_two, scaled_two, inverse_two = norm_rows(middle, gain_two, shift_two)
    normed_two = low(normed_two)
    near = jnp.concatenate((normed_two, swap(normed_two, Z0)), 0)
    far = swap(near, C)
    w_near = grow(w_near, 0, y, Y)
    w_far = grow(w_far, 3, x, X)
    w_up = jnp.stack((w_near, w_far), 1).reshape(features, -1)
    w_down = jnp.stack((down_near, down_far), 3).reshape(-1, features)
    near, far, w_down, w_up, grad_side, grad_across = tie(
        near, far, w_down, w_up, grad_side, grad_across
    )

    activ_far, upper_far, back_far, forth_far, sums_far = feed(
        far, grad_across, w_up, w_down, bias_up
    )
    activ, upper, back, forth, sums_near = feed(near, grad_side, w_up, w_down, bias_up)
    back, forth, back_far, forth_far, activ, upper = tie(
        back, forth, swap(back_far, C), swap(forth_far, C), activ, upper
    )

    count = back.shape[0] // 2
    back_own = wide(back[:count]) + wide(back_far[:count])
    back_other = low(wide(back[count:]) + wide(back_far[count:]))
    grad_two = back_own + wide(swap(back_other, Z0))
    grad_down = outer(activ, activ_far, grad_side, grad_across).reshape(2, 2, 2, 128, features)
    grad_up = outer(near, far, upper, upper_far).reshape(2, 2, 2, 2, 2, 32, -1)
    down_got = swap(pick(grad_down, 1 - y), Y)
    up_got = swap(pick(grad_up, 1 - x, 4), X)
    grad_two, grad_down, grad_up, forth, forth_far = tie(
        grad_two, grad_down, grad_up, forth, forth_far
    )

    grad_middle = wide(grad_own) + norm_back(grad_two, scaled_two, inverse_two, gain_two)
    branch_own = low(grad_middle)
    branch_own, branch, forth, forth_far = tie(
        branch_own, swap(branch_own, C), forth, forth_far
    )
    branch = jnp.concatenate((branch_own, branch), 0)
    grad_both = low(dot_t(branch, out_both))
    width = attended.shape[1]
    grad_attended = grad_both[:, :width]
    grad_came = swap(grad_both[:, width:], Z0)
    grad_w_out = low(dot_rows(both, branch)).reshape(2, 2, 2, 2, 32, features)
    grad_w_out = ordered(grad_w_out[0], grad_w_out[1], z0, 1)
    forth_own = wide(forth[:count]) + wide(forth_far[:count])
    forth_other = low(wide(forth[count:]) + wide(forth_far[count:]))
    final = low(middle + forth_own + wide(swap(forth_other, Z0)) + bias_down)
    grad_came, down_got, up_got, grad_w_out, final = tie(
        grad_came, down_got, up_got, grad_w_out, final
    )
    grad_down = low(wide(pick(grad_down, y)) + wide(down_got))
    grad_up = low(wide(pick(grad_up, x, 4)) + wide(up_got))

    def give_rows(values):
        got = (regroup(values[:tokens], 0), regroup(values[tokens:], 1))
        return wide(ordered(*got, zh, 0))[:, None]

    grad_down = low(shrink(grad_down, 1, x, X))
    grad_up = low(shrink(grad_up, 0, y, Y))
    grad_mixed = attend_back(ends, flips, mixed, grad_attended, grad_came, logs)
    final = give_rows(final)
    grad_w_out = low(shrink(grad_w_out, 0, y, Y))
    grad_mixed, grad_up, grad_down, final = tie(grad_mixed, grad_up, grad_down, final)

    half = 2 * tokens_two
    far = swap(low(dot_t(grad_mixed[half:], w_qkv)), C)
    back = dot_t(grad_mixed[:half], w_qkv)
    grad_qkv = low(dot_rows(normed, grad_mixed)).reshape(2, 2, 2, 2, 2, 32, -1)
    far, back, grad_qkv, grad_w_out, grad_up, grad_down = tie(
        far, back, grad_qkv, grad_w_out, grad_up, grad_down
    )
    back_own = back[:count] + wide(far[:count])
    back_other = low(back[count:] + wide(far[count:]))
    grad_one = back_own + wide(swap(back_other, Z0))
    qkv_near = low(shrink(low(shrink(grad_qkv[:, 0], 3, x, X)), 0, y, Y))
    qkv_far = low(shrink(low(shrink(grad_qkv[:, 1], 0, y, Y)), 2, x, X))
    grads = jnp.stack((grad_down, grad_up.transpose(1, 0, 2, 3, 4).reshape(2, 128, -1)), 1)
    grads = shrink(grads, 0, zh, ZH)
    grad_down = grads[0]
    grad_up = low(grads[1]).reshape(4, 32, -1)
    grad_w_out = low(shrink(grad_w_out, 2, x, X))
    grad_qkv = jnp.stack((qkv_near, qkv_far), 0)
    given = low(grad_middle + norm_back(grad_one, scaled_one, inverse_one, gain_one))
    given, grad_qkv, grad_w_out, grad_up, grad_down, grad_one = tie(
        given, grad_qkv, grad_w_out, grad_up, grad_down, grad_one
    )

    input_grad = give_rows(given)
    qkv_got = swap(pick(grad_qkv, 1 - zh, 1), ZH)
    out_got = swap(pick(grad_w_out, 1 - zh), ZH)
    qkv_got, out_got, grad_one = tie(qkv_got, out_got, grad_one)
    grad_qkv = low(wide(pick(grad_qkv, zh, 1)) + wide(qkv_got)).reshape(4, 32, -1)
    grad_w_out = wide(pick(grad_w_out, zh)) + wide(out_got)
    parts = jnp.concatenate((grad_qkv, grad_up), 2)
    parts = [pick(parts, quarter ^ r) for r in range(4)]
    parts[1] = jnp.concatenate((parts[1], low(pick(grad_w_out, 1 - z0))), 1)
    parts = parts[:1] + [swap(part, mask) for part, mask in zip(parts[1:], TEAM[1:])]
    grad_w_out = pick(grad_w_out, z0) + wide(parts[1][:, 1792:])
    grad_qkv, grad_up = join(quarter, parts)
    sums = jnp.stack(
        (
            jnp.sum(grad_one * scaled_one, 0),
            jnp.sum(grad_one, 0),
            jnp.sum(grad_two * scaled_two, 0),
            jnp.sum(grad_two, 0),
            jnp.sum(wide(branch_own), 0),
            jnp.sum(wide(grad_own), 0),
        )
    )
    sums = sums.reshape(6, 32, 32).transpose(1, 0, 2).reshape(32, 192)
    up_sums = (sums_near + sums_far).reshape(8, 1, 128)
    up_sums = jnp.where(jnp.arange(4)[None, :, None] == quarter, up_sums, 0.0)
    up_sums = up_sums.reshape(2, 2, 2, 2, 2, 128).transpose(0, 3, 1, 4, 2, 5).reshape(32, 128)
    sums = jnp.concatenate((up_sums, sums), 1)
    sums = jnp.sum(lax.all_to_all(sums, AXES, 0, 0, tiled=True), 0)
    grad_up_bias = sums[:128]
    small = [sums[128 + 32 * i : 160 + 32 * i] for i in range(6)]
    return (
        final,
        input_grad,
        grad_qkv,
        grad_w_out,
        grad_up,
        grad_down,
        small[0],
        small[1],
        small[2],
        small[3],
        small[4],
        grad_up_bias,
        small[5],
    )


def chosen_body(mesh, *arrays):
    shape = arrays[0].shape
    sizes = (mesh.shape["batch"], mesh.shape["blk"])
    if sizes == (4, 8) and shape == (2, 1, 128, 1024) and arrays[5].shape == (32, 4096):
        return team_body(*arrays)
    return body(*arrays)


def solution(mesh):
    return jax.shard_map(
        partial(chosen_body, mesh),
        mesh=mesh,
        in_specs=(
            P(None, "batch", "blk", None),
            P(None, "batch", "blk"),
            P(None, "batch", "blk", None),
            P(("batch", "blk"), None),
            P(("batch", "blk"), None),
            P(("batch", "blk"), None),
            P(("batch", "blk"), None),
            P(("batch", "blk")),
            P(("batch", "blk")),
            P(("batch", "blk")),
            P(("batch", "blk")),
            P(("batch", "blk")),
            P(("batch", "blk")),
            P(("batch", "blk")),
        ),
        out_specs=(
            P(None, "batch", "blk", None),
            P(None, "batch", "blk", None),
            P(("batch", "blk"), None),
            P(("batch", "blk"), None),
            P(("batch", "blk"), None),
            P(("batch", "blk"), None),
            P(("batch", "blk")),
            P(("batch", "blk")),
            P(("batch", "blk")),
            P(("batch", "blk")),
            P(("batch", "blk")),
            P(("batch", "blk")),
            P(("batch", "blk")),
        ),
        check_vma=False,
    )
```
